32 devices in a mesh: rep: 2 (over x), shard: 16 (over z, y, core).
Axes of the slice: x: 2, y: 2, z: 4, core: 2. Of those that a mesh axis runs over, the one named last changes fastest.
Arguments:
- tokens: bfloat16 [2, 32, 64, 1024], P(None, ('rep', 'shard')), may hold values from -6 to 6
- prefix: int32 [2, 32], P(None, ('rep', 'shard')), may hold values from 6 to 32
- qkv_weight: bfloat16 [1024, 3072], P('shard'), may hold values from -0.1875 to 0.1875
- out_weight: bfloat16 [1024, 1024], P('shard'), may hold values from -1 to 1
- in_weight: bfloat16 [1024, 5632], P('shard'), may hold values from -0.1875 to 0.1875
- down_weight: bfloat16 [2816, 1024], P('shard'), may hold values from -0.109375 to 0.109375
- cotangent: bfloat16 [2, 32, 64, 1024], P(None, ('rep', 'shard')), may hold values from -6 to 6
Outputs:
- result: bfloat16 [2, 32, 64, 1024], P(None, ('rep', 'shard'))
- grad_tokens: float32 [2, 32, 64, 1024], P(None, ('rep', 'shard'))
- grad_qkv: float32 [1024, 3072], P('shard')
- grad_out: float32 [1024, 1024], P('shard')
- grad_in: float32 [1024, 5632], P('shard')
- grad_down: float32 [2816, 1024], P('shard')
The draws below stay inside these ranges and needn't reach their ends.
Inputs may be any that keep to these rules, and one draw needn't show every extreme that they name: Each sequence's prefix length, a tenth to a half of 64.
All inputs are finite; a program needn't handle non-finite values.
Results may differ from the reference program's by a relative error of at most 0.014.
Values may be sent and summed in bfloat16 or wider, within the bound.
No kernel may reach another device: no remote copies, remote signals or barrier semaphores. Data moves between devices by JAX's collectives and lax.ppermute only.
A program may use at most 256 MiB of HBM per device.

```python
import math
import jax
import jax.numpy as jnp
from jax import lax

D = 1024
H = 16
HD = 64
FF = 2816
LEN = 64
MB = 2
GROUPS = 32
N_REP = 2
N_SHARD = 16


def plant(drawn, own_key, smallest, high):
    extent = drawn.shape
    place = [jax.random.randint(jax.random.fold_in(own_key, axis), (), 0, extent[axis]) for axis in range(len(extent))]
    drawn = drawn.at[tuple(place)].set(smallest)
    longest = extent.index(max(extent))
    place[longest] = (place[longest] + 1) % extent[longest]
    return drawn.at[tuple(place)].set(high)


def raised(entries, own_key, source, target, blocks, factor):
    def block_of(dim):
        return (jnp.arange(entries.shape[dim]) // (entries.shape[dim] // blocks)).reshape((-1,) + (1,) * (entries.ndim - 1 - dim))

    one_side = jax.random.permutation(own_key, blocks)[block_of(target)]
    far = (block_of(target) + blocks // 2) % blocks
    return jnp.where((block_of(source) == one_side) | (block_of(source) == far), factor * entries, entries)


def levels(own_key, dims, split, smallest, top_value):
    level, own = 1.0, jax.random.fold_in(own_key, 6)
    for dim, shards_of in split:
        heights = jnp.exp(jax.random.uniform(jax.random.fold_in(own, dim), (shards_of,), jnp.float32, smallest / len(split), top_value / len(split)))
        level = level * jnp.repeat(heights, dims[dim] // shards_of).reshape([-1 if axis == dim else 1 for axis in range(len(dims))])
    return level


def noise(key, shape, width, reach, cuts=(), kind=jnp.bfloat16):
    array = width * jax.random.normal(key, shape, jnp.float32)
    if cuts:
        array = array * levels(key, shape, cuts, -0.22, 0.18)
    return jnp.clip(array, -reach, reach).astype(kind)


def bell_draw_with(own_key, shape, scale, reach, split, heavy, kind=jnp.bfloat16):
    result = scale * jax.random.normal(own_key, shape, jnp.float32)
    if split:
        result = result * levels(own_key, shape, split, -0.22, 0.18)
    return jnp.clip(raised(result, jax.random.fold_in(own_key, 3), *heavy), -reach, reach).astype(kind)


def setup_inputs(seed: int = 0) -> dict:
    arg_keys = jax.random.split(jax.random.key(seed), 8)
    tokens = bell_draw_with(arg_keys[0], (MB, GROUPS, LEN, D), 1.0, 6.0, ((1, 32),), (1, 3, 32, 2.75))
    prefix = plant(jax.random.randint(arg_keys[1], (MB, GROUPS), LEN // 10, LEN // 2 + 1), jax.random.fold_in(arg_keys[1], 1), LEN // 10, (LEN // 2 + 1) - 1).astype(jnp.int32)
    qkv_weight = noise(arg_keys[2], (D, 3 * D), D ** -0.5, 0.1875, ((0, 16),))
    out_weight = noise(arg_keys[3], (D, D), (max(1, 2 * D // LEN)) ** -0.5, 1.0, ((0, 16),))
    in_weight = noise(arg_keys[4], (D, 2 * FF), D ** -0.5, 0.1875, ((0, 16),))
    down_weight = noise(arg_keys[5], (FF, D), FF ** -0.5, 0.109375, ((0, 16),))
    cotangent = noise(arg_keys[6], (MB, GROUPS, LEN, D), 1.0, 6.0, ((1, 32),))
    return {"tokens": tokens, "prefix": prefix, "qkv_weight": qkv_weight, "out_weight": out_weight, "in_weight": in_weight, "down_weight": down_weight, "cotangent": cotangent}


@jax.custom_vjp
def low(v):
    return lax.optimization_barrier(v.astype(jnp.bfloat16)).astype(jnp.float32)

@jax.custom_vjp
def low_back(v):
    return v

def low_keep(v):
    return (low(v), None)

def low_pass(kept, grad):
    return (grad,)

def back_keep(v):
    return (v, None)

def back_low(kept, grad):
    return (low(grad),)
low.defvjp(low_keep, low_pass)
low_back.defvjp(back_keep, back_low)

def layer_norm(values):
    centre = values - lax.optimization_barrier(jnp.mean(values, axis=-1, keepdims=True))
    spread = lax.optimization_barrier(jnp.mean(centre * centre, axis=-1, keepdims=True))
    return centre * lax.rsqrt(spread + 1e-05)

def matmul(left, right):
    return jnp.einsum('bld,de->ble', left, right, precision=lax.Precision.HIGHEST)

def rope_tables():
    position = jnp.arange(LEN, dtype=jnp.float32)[:, None]
    frequency = 10000.0 ** (-jnp.arange(0, HD, 2, dtype=jnp.float32) / HD)
    angles = position * frequency[None, :]
    angles = jnp.concatenate([angles, angles], axis=-1)
    return (jnp.cos(angles)[None, :, None, :], jnp.sin(angles)[None, :, None, :])

def rotate(values, cosine, sine):
    half_size = values.shape[-1] // 2
    turned = jnp.concatenate([-values[..., half_size:], values[..., :half_size]], axis=-1)
    return values * cosine + turned * sine

def layer(block_x, w_qkv, w_out, w_in, w_down, block_prefix, cosine, sine):
    batch = block_x.shape[0]
    normed = low(layer_norm(block_x))
    mixed = low_back(matmul(normed, w_qkv))
    query = low(rotate(mixed[..., :D].reshape(batch, LEN, H, HD), cosine, sine))
    keys = low(rotate(mixed[..., D:2 * D].reshape(batch, LEN, H, HD), cosine, sine))
    values = low(mixed[..., 2 * D:].reshape(batch, LEN, H, HD))
    scores = low_back(jnp.einsum('blhe,bmhe->bhlm', query, keys, precision=lax.Precision.HIGHEST) * HD ** (-0.5))
    row_pos = jnp.arange(LEN, dtype=jnp.int32)[:, None]
    col_pos = jnp.arange(LEN, dtype=jnp.int32)[None, :]
    allowed = (col_pos <= row_pos)[None] | (col_pos[None] < block_prefix[:, None, None])
    scores = jnp.where(allowed[:, None], scores, -1e+30)
    probs = low(jax.nn.softmax(scores, axis=-1))
    attended = jnp.einsum('bhlm,bmhe->blhe', probs, values, precision=lax.Precision.HIGHEST).reshape(batch, LEN, D)
    attended = low(low_back(attended))
    middle = block_x + low_back(matmul(attended, w_out))
    normed_two = low(layer_norm(middle))
    gate_up = low_back(matmul(normed_two, w_in))
    hidden = low(jax.nn.silu(gate_up[..., FF:]) * gate_up[..., :FF])
    return middle + low_back(matmul(hidden, w_down))

def reference(tokens, prefix, qkv_weight, out_weight, in_weight, down_weight, cotangent):
    total = MB * N_REP * N_SHARD
    per_block = math.gcd(total, max(1, 4096 // LEN))
    block_count = total // per_block
    block_tokens = tokens.reshape(block_count, per_block, LEN, D)
    block_prefix = prefix.reshape(block_count, per_block).astype(jnp.int32)
    block_cot = cotangent.reshape(block_count, per_block, LEN, D)
    w_qkv = qkv_weight.astype(jnp.float32)
    w_out = out_weight.astype(jnp.float32)
    w_in = in_weight.astype(jnp.float32)
    w_down = down_weight.astype(jnp.float32)
    cosine, sine = rope_tables()

    def one_block(totals, inputs):
        these_tokens, these_prefix, these_cot = inputs

        def forward(x_in, first, second, third, fourth):
            return layer(x_in, first, second, third, fourth, these_prefix, cosine, sine)
        output, pullback = jax.vjp(forward, these_tokens.astype(jnp.float32), w_qkv, w_out, w_in, w_down)
        gradients = pullback(these_cot.astype(jnp.float32))
        totals = (totals[0] + gradients[1], totals[1] + gradients[2], totals[2] + gradients[3], totals[3] + gradients[4])
        return (totals, (output.astype(jnp.bfloat16), gradients[0]))
    initial = (jnp.zeros_like(w_qkv), jnp.zeros_like(w_out), jnp.zeros_like(w_in), jnp.zeros_like(w_down))
    totals, (outputs, grad_x) = lax.scan(one_block, initial, (block_tokens, block_prefix, block_cot))
    shape_out = (MB, N_REP * N_SHARD, LEN, D)
    return (outputs.reshape(shape_out), grad_x.reshape(shape_out), totals[0], totals[1], totals[2], totals[3])
```

```python
import jax
import jax.numpy as jnp
import numpy as np
from jax import lax
from jax.sharding import Mesh, PartitionSpec as P

H = 16
HD = 64
LANES = 128
BF = jnp.bfloat16
F32 = jnp.float32
SWAP = ((0, 1), (1, 0))


def norm_rows(values):
    centre = values - jnp.mean(values, axis=-1, keepdims=True)
    inverse = lax.rsqrt(jnp.mean(centre * centre, axis=-1, keepdims=True) + 1e-05)
    return (centre * inverse, inverse)


def norm_back(normed, inverse, upstream):
    return inverse * (
        upstream
        - jnp.mean(upstream, axis=-1, keepdims=True)
        - normed * jnp.mean(upstream * normed, axis=-1, keepdims=True)
    )


def rope_tables(length):
    position = jnp.arange(length, dtype=F32)[:, None]
    frequency = 10000.0 ** (-jnp.arange(0, HD, 2, dtype=F32) / HD)
    angles = position * frequency[None, :]
    angles = jnp.concatenate([angles, angles], axis=-1)
    return (jnp.cos(angles)[:, None, :], jnp.sin(angles)[:, None, :])


def rotate(values, cosine, sine):
    half = HD // 2
    turned = jnp.concatenate([-values[..., half:], values[..., :half]], axis=-1)
    return values * cosine + turned * sine


def rotate_back(grads, cosine, sine):
    half = HD // 2
    scaled = grads * sine
    return grads * cosine + jnp.concatenate([scaled[..., half:], -scaled[..., :half]], axis=-1)


def dot(left, right):
    return jnp.dot(left, right, preferred_element_type=F32)


def dot_rt(left, right):
    return lax.dot_general(left, right, (((1,), (1,)), ((), ())), preferred_element_type=F32)


def dot_lt(left, right):
    return lax.dot_general(left, right, (((0,), (0,)), ((), ())), preferred_element_type=F32)


def across(value):
    return lax.ppermute(value, "rep", SWAP)


def sibling(value):
    return lax.ppermute(value, "core", SWAP)


class Ring:
    def __init__(self, size):
        self.size = size
        self.half = size // 2
        order = list(range(0, size, 2)) + list(range(size - 1, 0, -2))
        place = np.argsort(order)
        self.right = [(order[i], order[(i + 1) % size]) for i in range(size)]
        self.left = [(b, a) for a, b in self.right]
        me = lax.axis_index("ring")
        self.at = jnp.asarray([[order[(place[g] + k) % size] for k in range(size)] for g in range(size)], jnp.int32)[me]
        self.of = jnp.asarray([[(place[o] - place[g]) % size for o in range(size)] for g in range(size)], jnp.int32)[me]

    def go_right(self, value):
        return lax.ppermute(value, "ring", self.right)

    def go_left(self, value):
        return lax.ppermute(value, "ring", self.left)

    def gather(self, chunk):
        got = {0: chunk}
        right = left = chunk
        for step in range(1, self.half):
            right = self.go_right(right)
            left = self.go_left(left)
            got[self.size - step] = right
            got[step] = left
        cut = chunk.shape[0] // 2
        got[self.half] = jnp.concatenate([self.go_right(right[:cut]), self.go_left(left[cut:])], axis=0)
        stacked = jnp.stack([got[k] for k in range(self.size)])
        return jnp.stack([lax.dynamic_index_in_dim(stacked, self.of[g], 0, keepdims=False) for g in range(self.size)])

    def scatter(self, parts):
        def part(place):
            return lax.dynamic_index_in_dim(parts, self.at[place % self.size], 0, keepdims=False)

        cut = parts.shape[1] // 2
        far = part(self.half).astype(BF)
        right = self.go_right(far[:cut]).astype(F32)
        left = self.go_left(far[cut:]).astype(F32)
        rest = parts.shape[1] - cut
        right = jnp.pad(right, ((0, rest), (0, 0)))
        left = jnp.pad(left, ((cut, 0), (0, 0)))
        for step in range(self.half - 1, 0, -1):
            right = self.go_right((part(step) + right).astype(BF)).astype(F32)
            left = self.go_left((part(-step) + left).astype(BF)).astype(F32)
        return part(0) + right + left


def local(tokens, prefix, qkv_weight, out_weight, in_weight, down_weight, cotangent):
    micro, _, length, width = tokens.shape
    rows = micro * length
    ring_size = lax.axis_size("ring")
    ring = Ring(ring_size)
    rep = lax.axis_index("rep")
    core = lax.axis_index("core")
    shard_rows = qkv_weight.shape[0]
    units = in_weight.shape[1] // 2
    quarter = width // 4
    heads = H // 4
    piece = units // (4 * ring_size)
    member_units = -(-(units // 4) // LANES) * LANES
    padded = member_units // ring_size
    scale = HD ** (-0.5)
    cosine, sine = rope_tables(length)
    mine = 2 * core + rep
    theirs = 2 * (1 - core) + rep

    own = jnp.concatenate(
        [tokens.reshape(rows, width), jnp.broadcast_to(prefix.astype(BF), (micro, width))], axis=0
    )
    cot_own = cotangent.reshape(rows, width)
    far = across(own)
    near = sibling(own)
    blocks = [own, near, far, sibling(far)]
    cot_far = across(cot_own)
    cot_blocks = [cot_own, sibling(cot_own), cot_far, sibling(cot_far)]

    def first_columns(member):
        def cut(weight, start):
            return lax.dynamic_slice(weight, (0, start + member * quarter), (shard_rows, quarter))

        return jnp.concatenate([cut(qkv_weight, 0), cut(qkv_weight, width), cut(qkv_weight, 2 * width), cut(out_weight, 0)], axis=1)

    in_pieces = in_weight.reshape(shard_rows, 2, ring_size, 4, piece)

    def in_columns(member):
        taken = lax.dynamic_index_in_dim(in_pieces, member, 3, keepdims=False)
        return jnp.pad(taken, ((0, 0), (0, 0), (0, 0), (0, padded - piece))).reshape(shard_rows, 2 * member_units)

    def both_rows(columns):
        return jnp.concatenate([columns(mine), sibling(columns(theirs))], axis=0)

    def in_order(gathered):
        chips, double, columns = gathered.shape
        pair = gathered.reshape(chips, 2, double // 2, columns)
        swapped = jnp.stack([pair[:, 1], pair[:, 0]], axis=1)
        return jnp.where(core == 0, pair, swapped).reshape(chips * double, columns)

    first_full = in_order(ring.gather(both_rows(first_columns)))
    qkv_mine = first_full[:, : 3 * quarter]
    out_mine = first_full[:, 3 * quarter :]
    in_mine = in_order(ring.gather(both_rows(in_columns)))
    down_chunk = lax.dynamic_slice(down_weight, (rep * piece, 0), (piece, width))
    down_mine = jnp.pad(ring.gather(down_chunk), ((0, 0), (0, padded - piece), (0, 0))).reshape(member_units, width)
    out_pair = jnp.stack([out_mine, sibling(out_mine)])
    out_far = across(out_pair)

    def by_member(a, b, c, d):
        even = jnp.where(rep == 0, jnp.stack([a, c]), jnp.stack([c, a]))
        odd = jnp.where(rep == 0, jnp.stack([b, d]), jnp.stack([d, b]))
        return jnp.where(core == 0, jnp.concatenate([even, odd]), jnp.concatenate([odd, even]))

    out_full = by_member(out_pair[0], out_pair[1], out_far[0], out_far[1]).transpose(1, 0, 2).reshape(width, width)

    x_all = jnp.concatenate([b[:rows] for b in blocks], axis=0).astype(F32)
    prefixes = jnp.concatenate([b[rows:, 0] for b in blocks], axis=0).astype(jnp.int32)
    gm_all = jnp.concatenate(cot_blocks, axis=0)
    sequences = 4 * micro

    normed_one, inverse_one = norm_rows(x_all)
    h1 = normed_one.astype(BF)
    qkv = dot(h1, qkv_mine).reshape(sequences, length, 3, heads, HD)
    query = rotate(qkv[:, :, 0], cosine, sine).astype(BF)
    keys = rotate(qkv[:, :, 1], cosine, sine).astype(BF)
    values = qkv[:, :, 2].astype(BF)
    row_pos = lax.broadcasted_iota(jnp.int32, (length, length), 0)
    col_pos = lax.broadcasted_iota(jnp.int32, (length, length), 1)
    allowed = (col_pos <= row_pos)[None] | (col_pos[None] < prefixes[:, None, None])
    scores = jnp.einsum("slhe,smhe->shlm", query, keys, preferred_element_type=F32) * scale
    scores = jnp.where(allowed[:, None], scores, -1e30)
    expo = jnp.exp(scores - jnp.max(scores, axis=-1, keepdims=True))
    probs = expo / jnp.sum(expo, axis=-1, keepdims=True)
    probs_low = probs.astype(BF)
    o_mine = jnp.einsum("shlm,smhe->slhe", probs_low, values, preferred_element_type=F32)
    o_mine = o_mine.reshape(4, rows, quarter).astype(BF)
    o_far = across(o_mine)
    o_far = jnp.concatenate([o_far[2:], o_far[:2]], axis=0)
    o_near = sibling(jnp.stack([o_mine, o_far]))
    o_near = jnp.stack([o_near[:, 1], o_near[:, 0], o_near[:, 3], o_near[:, 2]], axis=1)
    o_all = by_member(o_mine, o_near[0], o_far, o_near[1]).transpose(1, 2, 0, 3).reshape(4 * rows, width)
    x2 = x_all + dot(o_all, out_full)
    normed_two, inverse_two = norm_rows(x2)
    h2 = normed_two.astype(BF)
    gate_up = dot(h2, in_mine)
    up = gate_up[:, :member_units]
    gate = gate_up[:, member_units:]
    sig = jax.nn.sigmoid(gate)
    hidden = (gate * sig * up).astype(BF)

    def to_owner_core(partial):
        split = partial.reshape(4, rows, width)
        got = sibling(jnp.stack([split[1], split[3]]).astype(BF)).astype(F32)
        return split[0] + got[0], split[2] + got[1]

    y_own, y_other = to_owner_core(dot(hidden, down_mine))
    y = y_own + across(y_other.astype(BF)).astype(F32) + x2[:rows]
    result = y.astype(BF)

    grad_hidden = dot_rt(gm_all, down_mine)
    grad_up = grad_hidden * (gate * sig)
    grad_gate = grad_hidden * up * (sig * (1.0 + gate * (1.0 - sig)))
    ggu = jnp.concatenate([grad_up, grad_gate], axis=-1).astype(BF)
    grad_down_part = dot_lt(hidden, gm_all).reshape(ring_size, padded, width)[:, :piece]
    down_sum = ring.scatter(grad_down_part)
    u_own, u_other = to_owner_core(dot_rt(ggu, in_mine))
    u_far = across(jnp.stack([u_own, u_other]).astype(BF)).astype(F32)
    u2 = jnp.concatenate([u_own + u_far[1], u_other + u_far[0]], axis=0)

    def own_rows(values):
        split = values.reshape(4, rows, values.shape[-1])
        return jnp.concatenate([split[0], split[2]], axis=0)

    gx2 = own_rows(gm_all).astype(F32) + norm_back(own_rows(normed_two), own_rows(inverse_two), u2)
    ga = gx2.astype(BF).reshape(2, rows, width)
    ga_near = sibling(ga)
    ga_all = jnp.concatenate([ga[0], ga_near[0], ga[1], ga_near[1]], axis=0)
    in_sum = ring.scatter(dot_lt(h2, ggu).reshape(ring_size, 2 * shard_rows, 2 * member_units))
    out_rows = lax.dynamic_slice(out_full, (mine * quarter, 0), (quarter, width))
    go = dot_rt(ga_all, out_rows).astype(BF).reshape(sequences, length, heads, HD)
    dprob = jnp.einsum("slhe,smhe->shlm", go, values, preferred_element_type=F32)
    dscore = (probs * (dprob - jnp.sum(probs * dprob, axis=-1, keepdims=True))).astype(BF)
    dquery = jnp.einsum("shlm,smhe->slhe", dscore, keys, preferred_element_type=F32) * scale
    dkeys = jnp.einsum("shlm,slhe->smhe", dscore, query, preferred_element_type=F32) * scale
    dvalues = jnp.einsum("shlm,slhe->smhe", probs_low, go, preferred_element_type=F32)
    gqkv = jnp.stack([rotate_back(dquery, cosine, sine), rotate_back(dkeys, cosine, sine), dvalues], axis=2)
    gqkv = gqkv.astype(BF).reshape(4 * rows, 3 * quarter)
    v_own, v_other = to_owner_core(dot_rt(gqkv, qkv_mine))
    u1 = v_own + across(v_other.astype(BF)).astype(F32)
    grad_tokens = gx2[:rows] + norm_back(normed_one[:rows], inverse_one[:rows], u1)
    ga_mine = lax.dynamic_slice(ga_all, (0, mine * quarter), (4 * rows, quarter))
    first_part = jnp.concatenate([dot_lt(h1, gqkv), dot_lt(o_all, ga_mine)], axis=1)
    first_sum = ring.scatter(first_part.reshape(ring_size, 2 * shard_rows, 4 * quarter))

    def all_members(summed):
        low = summed.astype(BF)
        keep = lax.dynamic_slice(low, (core * shard_rows, 0), (shard_rows, low.shape[1]))
        give = lax.dynamic_slice(low, ((1 - core) * shard_rows, 0), (shard_rows, low.shape[1]))
        pair = jnp.stack([keep, sibling(give)])
        other = across(pair)
        return by_member(pair[0], pair[1], other[0], other[1]).astype(F32)

    first_members = all_members(first_sum)
    in_members = all_members(in_sum)
    grad_qkv = first_members[:, :, : 3 * quarter].reshape(4, shard_rows, 3, quarter).transpose(1, 2, 0, 3).reshape(shard_rows, 3 * width)
    grad_out = first_members[:, :, 3 * quarter :].transpose(1, 0, 2).reshape(shard_rows, width)
    grad_in = in_members.reshape(4, shard_rows, 2, ring_size, padded)[..., :piece].transpose(1, 2, 3, 0, 4).reshape(shard_rows, 2 * units)
    down_low = down_sum.astype(BF)
    down_other = across(down_low)
    grad_down = jnp.where(rep == 0, jnp.concatenate([down_low, down_other]), jnp.concatenate([down_other, down_low])).astype(F32)
    return (
        result.reshape(micro, 1, length, width),
        grad_tokens.reshape(micro, 1, length, width),
        grad_qkv,
        grad_out,
        grad_in,
        grad_down,
    )


def solution(mesh):
    inner = Mesh(
        mesh.devices.reshape(mesh.shape["rep"], mesh.shape["shard"] // 2, 2), ("rep", "ring", "core")
    )
    everyone = ("rep", "ring", "core")
    group = ("ring", "core")
    placed = (
        P(None, everyone, None, None),
        P(None, everyone),
        P(group, None),
        P(group, None),
        P(group, None),
        P(group, None),
        P(None, everyone, None, None),
    )
    return jax.shard_map(
        local,
        mesh=inner,
        in_specs=placed,
        out_specs=(
            P(None, everyone, None, None),
            P(None, everyone, None, None),
            P(group, None),
            P(group, None),
            P(group, None),
            P(group, None),
        ),
        check_vma=False,
    )
```

```python
import functools

import jax
import jax.numpy as jnp
import numpy as np
from jax import lax
from jax.experimental import pallas as pl
from jax.experimental.pallas import tpu as pltpu
from jax.sharding import Mesh, PartitionSpec as P

H = 16
HD = 64
HALF = HD // 2
LANES = 128
PACK = 16
BF = jnp.bfloat16
F32 = jnp.float32
SWAP = ((0, 1), (1, 0))
MIB = 1 << 20
BLOCKS = ((0, 1, 2, 3), (1, 0, 3, 2), (2, 3, 0, 1), (3, 2, 1, 0))


def dot(left, right):
    return jnp.dot(left, right, preferred_element_type=F32)


def dot_rt(left, right):
    return lax.dot_general(left, right, (((1,), (1,)), ((), ())), preferred_element_type=F32)


def dot_lt(left, right):
    return lax.dot_general(left, right, (((0,), (0,)), ((), ())), preferred_element_type=F32)


def norm_rows(values):
    centre = values - jnp.mean(values, axis=-1, keepdims=True)
    inverse = lax.rsqrt(jnp.mean(centre * centre, axis=-1, keepdims=True) + 1e-05)
    return (centre * inverse, inverse)


def norm_back(normed, inverse, upstream):
    return inverse * (
        upstream
        - jnp.mean(upstream, axis=-1, keepdims=True)
        - normed * jnp.mean(upstream * normed, axis=-1, keepdims=True)
    )


def across(value):
    return lax.ppermute(value, "rep", SWAP)


def sibling(value):
    return lax.ppermute(value, "core", SWAP)


def order_of(size):
    return list(range(0, size, 2)) + list(range(size - 1, 0, -2))


def scalar_table(size):
    order = order_of(size)
    place = np.argsort(order)
    table = np.zeros((2, size, 2, 2 * size + 5), np.int32)
    for rep in range(2):
        for g in range(size):
            for core in range(2):
                at = [order[(place[g] + k) % size] for k in range(size)]
                of = [(place[o] - place[g]) % size for o in range(size)]
                members = [2 * core + rep, 2 * (1 - core) + rep, 2 * core + 1 - rep, 2 * (1 - core) + 1 - rep]
                table[rep, g, core] = at + of + [core] + members
    return table


def upper_half(rows):
    return -(-(rows // 2) // PACK) * PACK


class Ring:
    def __init__(self, size):
        self.size = size
        self.half = size // 2
        order = order_of(size)
        self.right = [(order[i], order[(i + 1) % size]) for i in range(size)]
        self.left = [(b, a) for a, b in self.right]

    def go_right(self, value):
        return lax.ppermute(value, "ring", self.right)

    def go_left(self, value):
        return lax.ppermute(value, "ring", self.left)

    def gather(self, chunk):
        got = {0: chunk}
        right = left = chunk
        for step in range(1, self.half):
            right = self.go_right(right)
            left = self.go_left(left)
            got[self.size - step] = right
            got[step] = left
        cut = upper_half(chunk.shape[0])
        far = [self.go_right(right[:cut]), self.go_left(left[cut:])]
        return [got[k] for k in range(self.size) if k != self.half] + far

    def scatter(self, parts):
        cut = upper_half(parts.shape[1])
        rest = parts.shape[1] - cut
        far = parts[self.half]
        right = self.go_right(far[:cut].astype(BF)).astype(F32)
        left = self.go_left(far[cut:].astype(BF)).astype(F32)
        right = jnp.pad(right, ((0, rest), (0, 0)))
        left = jnp.pad(left, ((cut, 0), (0, 0)))
        for step in range(self.half - 1, 0, -1):
            right = self.go_right((parts[step] + right).astype(BF)).astype(F32)
            left = self.go_left((parts[self.size - step] + left).astype(BF)).astype(F32)
        return parts[0] + right + left


def call(body, outs, scratch, limit, flops, *args):
    nbytes = sum(a.size * a.dtype.itemsize for a in args) + sum(o.size * o.dtype.itemsize for o in outs)
    return pl.pallas_call(
        body,
        out_shape=outs,
        in_specs=[pl.BlockSpec(memory_space=pltpu.SMEM)] + [pl.BlockSpec(memory_space=pltpu.VMEM)] * (len(args) - 1),
        out_specs=[pl.BlockSpec(memory_space=pltpu.VMEM)] * len(outs),
        scratch_shapes=scratch,
        compiler_params=pltpu.CompilerParams(vmem_limit_bytes=limit * MIB),
        cost_estimate=pl.CostEstimate(flops=flops, bytes_accessed=nbytes, transcendentals=0),
    )(*args)


def shape(dims, dtype):
    return jax.ShapeDtypeStruct(dims, dtype)


def lanes(start, size):
    return pl.ds(pl.multiple_of(start, LANES), size)


def pack_first(size, width, scal, qkv_ref, out_ref, own_ref, sib_ref):
    quarter = width // 4
    for ref, member in ((own_ref, scal[2 * size + 1]), (sib_ref, scal[2 * size + 2])):
        for j in range(3):
            ref[:, j * quarter : (j + 1) * quarter] = qkv_ref[:, lanes(j * width + member * quarter, quarter)]
        ref[:, 3 * quarter :] = out_ref[:, lanes(member * quarter, quarter)]


def pack_in(size, units, piece, padded, scal, in_ref, own_ref, sib_ref):
    for ref, member in ((own_ref, scal[2 * size + 1]), (sib_ref, scal[2 * size + 2])):
        ref[...] = jnp.zeros_like(ref)
        for q in range(4):

            @pl.when(member == q)
            def _(ref=ref, q=q):
                for part in range(2):
                    for g in range(size):
                        start = part * units + (g * 4 + q) * piece
                        to = (part * size + g) * padded
                        ref[:, to : to + piece] = in_ref[:, start : start + piece]


def place_chunks(size, scal, chunk_refs, store):
    half = size // 2
    places = [k for k in range(size) if k != half]
    for k, ref in zip(places, chunk_refs, strict=False):
        store(scal[k], 0, ref[...])
    top, bottom = chunk_refs[-2:]
    store(scal[half], 0, top[...])
    store(scal[half], top.shape[0], bottom[...])


def place_rows(size, shard_rows, scal, chunk_refs, put):
    core = scal[2 * size]

    def store(chip, first, value):
        for lower in range(2):
            begin = lower * shard_rows - first
            if begin < 0 or begin >= value.shape[0]:
                continue
            row = chip * (2 * shard_rows) + (core if lower == 0 else 1 - core) * shard_rows
            put(pl.multiple_of(row, PACK), value[begin : begin + shard_rows])

    place_chunks(size, scal, chunk_refs, store)


def turned(values):
    lane = lax.broadcasted_iota(jnp.int32, values.shape, 1) % HD
    wide = values.shape[1]
    return jnp.where(lane < HALF, pltpu.roll(values, wide - HALF, 1), pltpu.roll(values, HALF, 1))


def visible(rows, length, limits):
    query = lax.broadcasted_iota(jnp.int32, (rows, rows), 0)
    key = lax.broadcasted_iota(jnp.int32, (rows, rows), 1)
    inside = (key % length).astype(F32)
    limit = jnp.zeros((rows, rows), F32)
    for s in range(rows // length):
        limit = jnp.where(key // length == s, limits[s : s + 1, :rows].astype(F32), limit)
    return (query // length == key // length) & ((key <= query) | (inside < limit))


def attention(size, shard_rows, rows, length, width, n_chunks, scal, *refs):
    blocks = refs[:4]
    chunks = refs[4 : 4 + n_chunks]
    cos_ref, sin_ref, o_ref, h1_ref, qkv_ref, p_ref, w_ref, out_ref = refs[4 + n_chunks :]
    quarter = width // 4

    def put(row, value):
        w_ref[pl.ds(row, shard_rows), :] = value[:, : 3 * quarter]
        out_ref[pl.ds(row, shard_rows), :] = value[:, 3 * quarter :]

    place_rows(size, shard_rows, scal, chunks, put)
    for b in range(4):
        normed, _ = norm_rows(blocks[b][:rows, :].astype(F32))
        h1_ref[b * rows : (b + 1) * rows, :] = normed.astype(BF)
    for j in range(3):
        mixed = dot(h1_ref[...], w_ref[:, j * quarter : (j + 1) * quarter])
        for b in range(4):
            piece = mixed[b * rows : (b + 1) * rows, :]
            if j < 2:
                piece = piece * cos_ref[...] + turned(piece) * sin_ref[...]
            qkv_ref[b * rows : (b + 1) * rows, j * quarter : (j + 1) * quarter] = piece.astype(BF)
    for b in range(4):
        allowed = visible(rows, length, blocks[b][rows:, :])
        block = slice(b * rows, (b + 1) * rows)
        for h in range(quarter // HD):
            query = qkv_ref[block, h * HD : (h + 1) * HD]
            keys = qkv_ref[block, quarter + h * HD : quarter + (h + 1) * HD]
            values = qkv_ref[block, 2 * quarter + h * HD : 2 * quarter + (h + 1) * HD]
            scores = jnp.where(allowed, dot_rt(query, keys) * HD ** (-0.5), -1e30)
            expo = jnp.exp(scores - jnp.max(scores, axis=-1, keepdims=True))
            probs = expo / jnp.sum(expo, axis=-1, keepdims=True)
            p_ref[b * (quarter // HD) + h] = probs
            o_ref[b, :, h * HD : (h + 1) * HD] = dot(probs.astype(BF), values).astype(BF)


def middle(size, rows, width, scal, *refs):
    blocks = refs[:4]
    o_own, o_far, o_near, w_own, w_near, w_far, x2_ref, h2_ref, o_ref, rows_ref, w_full = refs[4:]
    quarter = width // 4
    members = [scal[2 * size + 1 + m] for m in range(4)]
    weights = (w_own[...], w_near[...], w_far[0], w_far[1])
    for m in range(4):
        w_full[:, lanes(members[m] * quarter, quarter)] = weights[m]
        for b in range(4):
            kept = BLOCKS[m][b]
            value = (o_own, o_near.at[0], o_far, o_near.at[1])[m][kept]
            o_ref[b * rows : (b + 1) * rows, lanes(members[m] * quarter, quarter)] = value
    rows_ref[...] = w_full[pl.ds(pl.multiple_of(members[0] * quarter, quarter), quarter), :]
    for j in range(4):
        columns = slice(j * quarter, (j + 1) * quarter)
        added = dot(o_ref[...], w_full[:, columns])
        for b in range(4):
            x2_ref[b * rows : (b + 1) * rows, columns] = blocks[b][:rows, columns].astype(F32) + added[b * rows : (b + 1) * rows, :]
    for b in range(4):
        block = slice(b * rows, (b + 1) * rows)
        normed, _ = norm_rows(x2_ref[block, :])
        h2_ref[block, :] = normed.astype(BF)


def hidden_units(size, shard_rows, members_units, n_chunks, scal, h2_ref, *refs):
    chunks = refs[:n_chunks]
    up_ref, gate_ref, hid_ref, w_ref = refs[n_chunks:]

    def put(row, value):
        w_ref[pl.ds(row, shard_rows), :] = value

    place_rows(size, shard_rows, scal, chunks, put)
    tile = 256

    @pl.loop(0, members_units // tile)
    def _(i):
        at = pl.multiple_of(i * tile, tile)
        up = dot(h2_ref[...], w_ref[:, pl.ds(at, tile)])
        gate = dot(h2_ref[...], w_ref[:, pl.ds(members_units + at, tile)])
        up_ref[:, pl.ds(at, tile)] = up
        gate_ref[:, pl.ds(at, tile)] = gate
        hid_ref[:, pl.ds(at, tile)] = (gate * jax.nn.sigmoid(gate) * up).astype(BF)


def hidden_back(size, rows, padded, piece, n_chunks, scal, *refs):
    cots = refs[:4]
    chunks = refs[4 : 4 + n_chunks]
    up_ref, gate_ref, w_in, ggu_ref, keep_ref, give_ref, down_ref, gm_ref = refs[4 + n_chunks :]
    units = up_ref.shape[1]
    width = gm_ref.shape[1]
    down_ref[...] = jnp.zeros_like(down_ref)

    def store(chip, first, value):
        down_ref[pl.ds(pl.multiple_of(chip * padded + first, PACK), value.shape[0]), :] = value

    place_chunks(size, scal, chunks, store)
    for b in range(4):
        gm_ref[b * rows : (b + 1) * rows, :] = cots[b][...]
    tile = 256

    @pl.loop(0, units // tile)
    def _(i):
        at = pl.multiple_of(i * tile, tile)
        grad = dot_rt(gm_ref[...], down_ref[pl.ds(at, tile), :])
        up = up_ref[:, pl.ds(at, tile)]
        gate = gate_ref[:, pl.ds(at, tile)]
        sig = jax.nn.sigmoid(gate)
        ggu_ref[:, pl.ds(at, tile)] = (grad * (gate * sig)).astype(BF)
        ggu_ref[:, pl.ds(units + at, tile)] = (grad * up * (sig * (1.0 + gate * (1.0 - sig)))).astype(BF)

    @pl.loop(0, width // tile)
    def _(i):
        at = pl.multiple_of(i * tile, tile)
        back = dot_rt(ggu_ref[...], w_in[pl.ds(at, tile), :])
        share(back, rows, keep_ref, give_ref, pl.ds(at, tile))


def share(partial, rows, keep_ref, give_ref, columns):
    keep_ref[0, :, columns] = partial[:rows]
    give_ref[0, :, columns] = partial[rows : 2 * rows].astype(BF)
    keep_ref[1, :, columns] = partial[2 * rows : 3 * rows]
    give_ref[1, :, columns] = partial[3 * rows :].astype(BF)


def last_projection(rows, scal, hid_ref, down_ref, keep_ref, give_ref):
    tile = 256

    @pl.loop(0, down_ref.shape[1] // tile)
    def _(i):
        columns = pl.ds(pl.multiple_of(i * tile, tile), tile)
        share(dot(hid_ref[...], down_ref[:, columns]), rows, keep_ref, give_ref, columns)


def grad_down_parts(size, padded, piece, scal, hid_ref, gm_ref, part_ref):
    tile = 256

    @pl.loop(0, gm_ref.shape[1] // tile)
    def _(i):
        columns = pl.ds(pl.multiple_of(i * tile, tile), tile)
        grads = dot_lt(hid_ref[...], gm_ref[:, columns])
        for g in range(size):
            part_ref[scal[size + g], :, columns] = grads[g * padded : g * padded + piece]


def grad_in_parts(size, double, scal, h2_ref, ggu_ref, part_ref):
    tile = 256

    @pl.loop(0, ggu_ref.shape[1] // tile)
    def _(i):
        columns = pl.ds(pl.multiple_of(i * tile, tile), tile)
        grads = dot_lt(h2_ref[...], ggu_ref[:, columns])
        for g in range(size):
            part_ref[scal[size + g], :, columns] = grads[g * double : (g + 1) * double]


def middle_back(rows, scal, keep_ref, got_ref, far_ref, x2_ref, cot_own, cot_far, gx2_ref, ga_ref):
    for i, cot in ((0, cot_own), (1, cot_far)):
        upstream = keep_ref[i] + got_ref[i].astype(F32) + far_ref[1 - i].astype(F32)
        normed, inverse = norm_rows(x2_ref[2 * i * rows : (2 * i + 1) * rows, :])
        total = cot[...].astype(F32) + norm_back(normed, inverse, upstream)
        if i == 0:
            gx2_ref[...] = total
        ga_ref[i] = total.astype(BF)


def attention_back(rows, width, scal, ga_own, ga_near, out_rows, qkv_ref, p_ref, w_ref, cos_ref, sin_ref, gqkv_ref, ga_ref, keep_ref, give_ref, go_ref, grad_ref):
    quarter = width // 4
    for b, value in enumerate((ga_own[0], ga_near[0], ga_own[1], ga_near[1])):
        ga_ref[b * rows : (b + 1) * rows, :] = value
    go_ref[...] = dot_rt(ga_ref[...], out_rows[...]).astype(BF)
    for b in range(4):
        block = slice(b * rows, (b + 1) * rows)
        for h in range(quarter // HD):
            head = slice(h * HD, (h + 1) * HD)
            query = qkv_ref[block, h * HD : (h + 1) * HD]
            keys = qkv_ref[block, quarter + h * HD : quarter + (h + 1) * HD]
            values = qkv_ref[block, 2 * quarter + h * HD : 2 * quarter + (h + 1) * HD]
            probs = p_ref[b * (quarter // HD) + h]
            go = go_ref[block, head]
            dprob = dot_rt(go, values)
            centre = jnp.sum(probs * dprob, axis=-1, keepdims=True)
            dscore = (probs * (dprob - centre)).astype(BF)
            grad_ref[0, :, head] = dot(dscore, keys) * HD ** (-0.5)
            grad_ref[1, :, head] = dot_lt(dscore, query) * HD ** (-0.5)
            grad_ref[2, :, head] = dot_lt(probs.astype(BF), go)
        for j in range(3):
            grad = grad_ref[j]
            if j < 2:
                grad = grad * cos_ref[...] - turned(grad) * sin_ref[...]
            gqkv_ref[block, j * quarter : (j + 1) * quarter] = grad.astype(BF)
    for j in range(4):
        columns = slice(j * quarter, (j + 1) * quarter)
        share(dot_rt(gqkv_ref[...], w_ref[columns, :]), rows, keep_ref, give_ref, columns)


def grad_first_parts(size, double, width, scal, h1_ref, gqkv_ref, o_ref, ga_ref, part_ref):
    quarter = width // 4
    for j in range(4):
        if j < 3:
            grads = dot_lt(h1_ref[...], gqkv_ref[:, j * quarter : (j + 1) * quarter])
        else:
            grads = dot_lt(o_ref[...], ga_ref[:, lanes(scal[2 * size + 1] * quarter, quarter)])
        for g in range(size):
            part_ref[scal[size + g], :, j * quarter : (j + 1) * quarter] = grads[g * double : (g + 1) * double]


def finish_tokens(rows, scal, keep_ref, got_ref, far_ref, block_ref, gx2_ref, out_ref):
    upstream = keep_ref[0] + got_ref[0].astype(F32) + far_ref[...].astype(F32)
    normed, inverse = norm_rows(block_ref[:rows, :].astype(F32))
    out_ref[...] = gx2_ref[...] + norm_back(normed, inverse, upstream)


def unpack_first(size, width, scal, pair_ref, other_ref, qkv_ref, out_ref):
    quarter = width // 4
    for m, value in enumerate((pair_ref[0], pair_ref[1], other_ref[0], other_ref[1])):
        value = value.astype(F32)
        at = scal[2 * size + 1 + m] * quarter
        for j in range(3):
            qkv_ref[:, lanes(j * width + at, quarter)] = value[:, j * quarter : (j + 1) * quarter]
        out_ref[:, lanes(at, quarter)] = value[:, 3 * quarter :]


def unpack_in(size, units, piece, padded, scal, pair_ref, other_ref, in_ref, held):
    for m, value in enumerate((pair_ref[0], pair_ref[1], other_ref[0], other_ref[1])):
        held[scal[2 * size + 1 + m]] = value.astype(F32)
    for q in range(4):
        for part in range(2):
            for g in range(size):
                start = part * units + (g * 4 + q) * piece
                frm = (part * size + g) * padded
                in_ref[:, start : start + piece] = held[q, :, frm : frm + piece]


def local(tokens, prefix, qkv_weight, out_weight, in_weight, down_weight, cotangent):
    micro, _, length, width = tokens.shape
    rows = micro * length
    size = lax.axis_size("ring")
    ring = Ring(size)
    rep = lax.axis_index("rep")
    core = lax.axis_index("core")
    shard_rows = qkv_weight.shape[0]
    double = 2 * shard_rows
    units = in_weight.shape[1] // 2
    quarter = width // 4
    heads = quarter // HD
    piece = units // (4 * size)
    padded = -(-piece // PACK) * PACK
    while size * padded % 256:
        padded += PACK
    member_units = size * padded
    chunks = size + 1
    table = scalar_table(size)
    scal = lax.dynamic_slice(
        jnp.asarray(table.reshape(-1, table.shape[-1])), ((rep * size + lax.axis_index("ring")) * 2 + core, 0), (1, table.shape[-1])
    )[0]

    position = np.arange(length, dtype=np.float32)[:, None]
    frequency = np.float32(10000.0) ** (-np.arange(0, HD, 2, dtype=np.float32) / np.float32(HD))
    angles = (position * frequency[None, :]).astype(np.float32)
    angles = np.concatenate([angles, angles], axis=-1)
    sign = np.where(np.arange(HD) < HALF, -1.0, 1.0).astype(np.float32)
    cosine = jnp.asarray(np.tile(np.cos(angles), (micro, heads)).astype(np.float32))
    sine = jnp.asarray(np.tile(np.sin(angles) * sign, (micro, heads)).astype(np.float32))

    own = jnp.concatenate([tokens.reshape(rows, width), jnp.broadcast_to(prefix.astype(BF), (micro, width))], axis=0)
    cot_own = cotangent.reshape(rows, width)
    far = across(own)
    near = sibling(own)
    blocks = [own, near, far, sibling(far)]
    cot_far = across(cot_own)
    cots = [cot_own, sibling(cot_own), cot_far, sibling(cot_far)]

    a_own, a_sib = call(
        functools.partial(pack_first, size, width), [shape((shard_rows, width), BF)] * 2, [], 8, 0, scal, qkv_weight, out_weight
    )
    a_chunks = ring.gather(jnp.concatenate([a_own, sibling(a_sib)], axis=0))
    b_own, b_sib = call(
        functools.partial(pack_in, size, units, piece, padded), [shape((shard_rows, 2 * member_units), BF)] * 2, [], 8, 0, scal, in_weight
    )
    b_chunks = ring.gather(jnp.concatenate([b_own, sibling(b_sib)], axis=0))
    c_chunks = ring.gather(lax.dynamic_slice(down_weight, (rep * piece, 0), (piece, width)))

    o_own, h1, qkv, probs, qkv_mine, out_mine = call(
        functools.partial(attention, size, shard_rows, rows, length, width, chunks),
        [
            shape((4, rows, quarter), BF),
            shape((4 * rows, width), BF),
            shape((4 * rows, 3 * quarter), BF),
            shape((4 * heads, rows, rows), F32),
            shape((width, 3 * quarter), BF),
            shape((width, quarter), BF),
        ],
        [],
        24,
        2 * 4 * rows * width * 3 * quarter,
        scal,
        *blocks,
        *a_chunks,
        cosine,
        sine,
    )
    out_near = sibling(out_mine)
    out_far = across(jnp.stack([out_mine, out_near]))
    o_far = across(o_own)
    o_near = sibling(jnp.stack([o_own, o_far]))
    x2, h2, o_all, out_rows = call(
        functools.partial(middle, size, rows, width),
        [
            shape((4 * rows, width), F32),
            shape((4 * rows, width), BF),
            shape((4 * rows, width), BF),
            shape((quarter, width), BF),
        ],
        [pltpu.VMEM((width, width), BF)],
        24,
        2 * 4 * rows * width * width,
        scal,
        *blocks,
        o_own,
        o_far,
        o_near,
        out_mine,
        out_near,
        out_far,
    )
    up, gate, hid, in_mine = call(
        functools.partial(hidden_units, size, shard_rows, member_units, chunks),
        [
            shape((4 * rows, member_units), F32),
            shape((4 * rows, member_units), F32),
            shape((4 * rows, member_units), BF),
            shape((width, 2 * member_units), BF),
        ],
        [],
        28,
        4 * 4 * rows * width * member_units,
        scal,
        h2,
        *b_chunks,
    )
    pair_low = shape((2, rows, width), BF)
    pair_full = shape((2, rows, width), F32)
    ggu, u2_keep, u2_give, down_mine, gm = call(
        functools.partial(hidden_back, size, rows, padded, piece, chunks),
        [shape((4 * rows, 2 * member_units), BF), pair_full, pair_low, shape((member_units, width), BF), shape((4 * rows, width), BF)],
        [],
        32,
        6 * 4 * rows * width * member_units,
        scal,
        *cots,
        *c_chunks,
        up,
        gate,
        in_mine,
    )
    u2_got = sibling(u2_give)
    u2_far = across((u2_keep + u2_got.astype(F32)).astype(BF))

    y_keep, y_give = call(
        functools.partial(last_projection, rows), [pair_full, pair_low], [], 16, 2 * 4 * rows * width * member_units, scal, hid, down_mine
    )
    y_got = sibling(y_give)
    y_far = across((y_keep[1] + y_got[1].astype(F32)).astype(BF))
    result = (x2[:rows] + (y_keep[0] + y_got[0].astype(F32) + y_far.astype(F32))).astype(BF)

    (down_parts,) = call(
        functools.partial(grad_down_parts, size, padded, piece),
        [shape((size, piece, width), F32)],
        [],
        16,
        2 * 4 * rows * width * member_units,
        scal,
        hid,
        gm,
    )
    down_low = ring.scatter(down_parts).astype(BF)
    down_other = across(down_low)
    grad_down = jnp.where(rep == 0, jnp.concatenate([down_low, down_other]), jnp.concatenate([down_other, down_low])).astype(F32)
    (in_parts,) = call(
        functools.partial(grad_in_parts, size, double),
        [shape((size, double, 2 * member_units), F32)],
        [],
        24,
        4 * 4 * rows * width * member_units,
        scal,
        h2,
        ggu,
    )

    def all_members(summed):
        low = summed.astype(BF)
        keep = lax.dynamic_slice(low, (core * shard_rows, 0), (shard_rows, low.shape[1]))
        give = lax.dynamic_slice(low, ((1 - core) * shard_rows, 0), (shard_rows, low.shape[1]))
        pair = jnp.stack([keep, sibling(give)])
        return pair, across(pair)

    gx2, ga = call(
        functools.partial(middle_back, rows), [shape((rows, width), F32), pair_low], [], 16, 0, scal, u2_keep, u2_got, u2_far, x2, cots[0], cots[2]
    )
    ga_near = sibling(ga)
    gqkv, ga_all, u1_keep, u1_give = call(
        functools.partial(attention_back, rows, width),
        [shape((4 * rows, 3 * quarter), BF), shape((4 * rows, width), BF), pair_full, pair_low],
        [pltpu.VMEM((4 * rows, quarter), BF), pltpu.VMEM((3, rows, quarter), F32)],
        24,
        4 * 4 * rows * width * 3 * quarter,
        scal,
        ga,
        ga_near,
        out_rows,
        qkv,
        probs,
        qkv_mine,
        cosine,
        sine,
    )
    in_pair, in_other = all_members(ring.scatter(in_parts))
    (grad_in,) = call(
        functools.partial(unpack_in, size, units, piece, padded),
        [shape((shard_rows, 2 * units), F32)],
        [pltpu.VMEM((4, shard_rows, 2 * member_units), F32)],
        16,
        0,
        scal,
        in_pair,
        in_other,
    )
    u1_got = sibling(u1_give)
    u1_far = across((u1_keep[1] + u1_got[1].astype(F32)).astype(BF))
    (first_parts,) = call(
        functools.partial(grad_first_parts, size, double, width),
        [shape((size, double, width), F32)],
        [],
        24,
        2 * 4 * rows * width * width,
        scal,
        h1,
        gqkv,
        o_all,
        ga_all,
    )
    (grad_tokens,) = call(
        functools.partial(finish_tokens, rows), [shape((rows, width), F32)], [], 16, 0, scal, u1_keep, u1_got, u1_far, own, gx2
    )
    first_pair, first_other = all_members(ring.scatter(first_parts))
    grad_qkv, grad_out = call(
        functools.partial(unpack_first, size, width),
        [shape((shard_rows, 3 * width), F32), shape((shard_rows, width), F32)],
        [],
        16,
        0,
        scal,
        first_pair,
        first_other,
    )
    return (
        result.reshape(micro, 1, length, width),
        grad_tokens.reshape(micro, 1, length, width),
        grad_qkv,
        grad_out,
        grad_in,
        grad_down,
    )


def solution(mesh):
    inner = Mesh(mesh.devices.reshape(mesh.shape["rep"], mesh.shape["shard"] // 2, 2), ("rep", "ring", "core"))
    everyone = ("rep", "ring", "core")
    group = ("ring", "core")
    sequences = P(None, everyone, None, None)
    weights = P(group, None)
    return jax.shard_map(
        local,
        mesh=inner,
        in_specs=(sequences, P(None, everyone), weights, weights, weights, weights, sequences),
        out_specs=(sequences, sequences, weights, weights, weights, weights),
        check_vma=False,
    )
```

```python
import functools

import jax
import jax.numpy as jnp
import numpy as np
from jax import lax
from jax.experimental import pallas as pl
from jax.experimental.pallas import tpu as pltpu
from jax.sharding import Mesh, PartitionSpec as P

H = 16
HD = 64
HALF = HD // 2
LANES = 128
PACK = 16
BF = jnp.bfloat16
F32 = jnp.float32
SWAP = ((0, 1), (1, 0))
MIB = 1 << 20
BLOCKS = ((0, 1, 2, 3), (1, 0, 3, 2), (2, 3, 0, 1), (3, 2, 1, 0))


def dot(left, right):
    return jnp.dot(left, right, preferred_element_type=F32)


def dot_rt(left, right):
    return lax.dot_general(left, right, (((1,), (1,)), ((), ())), preferred_element_type=F32)


def dot_lt(left, right):
    return lax.dot_general(left, right, (((0,), (0,)), ((), ())), preferred_element_type=F32)


def norm_rows(values):
    centre = values - jnp.mean(values, axis=-1, keepdims=True)
    inverse = lax.rsqrt(jnp.mean(centre * centre, axis=-1, keepdims=True) + 1e-05)
    return (centre * inverse, inverse)


def norm_back(normed, inverse, upstream):
    return inverse * (
        upstream
        - jnp.mean(upstream, axis=-1, keepdims=True)
        - normed * jnp.mean(upstream * normed, axis=-1, keepdims=True)
    )


def across(value):
    return lax.ppermute(value, "rep", SWAP)


def sibling(value):
    return lax.ppermute(value, "core", SWAP)


def order_of(size):
    return list(range(0, size, 2)) + list(range(size - 1, 0, -2))


def scalar_table(size):
    order = order_of(size)
    place = np.argsort(order)
    table = np.zeros((2, size, 2, 2 * size + 5), np.int32)
    for rep in range(2):
        for g in range(size):
            for core in range(2):
                at = [order[(place[g] + k) % size] for k in range(size)]
                of = [(place[o] - place[g]) % size for o in range(size)]
                members = [2 * core + rep, 2 * (1 - core) + rep, 2 * core + 1 - rep, 2 * (1 - core) + 1 - rep]
                table[rep, g, core] = at + of + [core] + members
    return table


def upper_half(rows):
    return -(-(rows // 2) // PACK) * PACK


class Ring:
    def __init__(self, size):
        self.size = size
        self.half = size // 2
        order = order_of(size)
        self.right = [(order[i], order[(i + 1) % size]) for i in range(size)]
        self.left = [(b, a) for a, b in self.right]

    def exchange(self, pair):
        return lax.ppermute(pair[0], "ring", self.right), lax.ppermute(pair[1], "ring", self.left)


class Gather:
    def __init__(self, ring, chunk):
        self.ring = ring
        self.step = 0
        self.got = {0: chunk}
        self.cut = upper_half(chunk.shape[0])
        self.state = (chunk, chunk)

    def advance(self):
        if self.step == self.ring.half:
            return
        self.step += 1
        if self.step == self.ring.half:
            self.far = self.ring.exchange((self.state[0][: self.cut], self.state[1][self.cut :]))
            self.state = ()
            return
        self.state = self.ring.exchange(self.state)
        self.got[self.ring.size - self.step], self.got[self.step] = self.state

    def finish(self):
        while self.step < self.ring.half:
            self.advance()
        return [self.got[k] for k in range(self.ring.size) if k != self.ring.half] + list(self.far)


class Scatter:
    def __init__(self, ring, parts):
        self.ring = ring
        self.step = 0
        self.parts = parts
        self.cut = upper_half(parts.shape[1])
        far = parts[ring.half]
        self.state = (far[: self.cut].astype(BF), far[self.cut :].astype(BF))

    def advance(self):
        ring = self.ring
        if self.step == ring.half:
            return
        right, left = (v.astype(F32) for v in ring.exchange(self.state))
        if self.step == 0:
            right = jnp.pad(right, ((0, self.parts.shape[1] - self.cut), (0, 0)))
            left = jnp.pad(left, ((self.cut, 0), (0, 0)))
        self.step += 1
        if self.step == ring.half:
            self.total = self.parts[0] + right + left
            self.state = ()
            return
        place = ring.half - self.step
        self.state = ((self.parts[place] + right).astype(BF), (self.parts[ring.size - place] + left).astype(BF))

    def finish(self):
        while self.step < self.ring.half:
            self.advance()
        return self.total


def sync(*values):
    return lax.optimization_barrier(values)


def call(body, outs, scratch, limit, flops, *args):
    nbytes = sum(a.size * a.dtype.itemsize for a in args) + sum(o.size * o.dtype.itemsize for o in outs)
    return pl.pallas_call(
        body,
        name=body.func.__name__,
        out_shape=outs,
        in_specs=[pl.BlockSpec(memory_space=pltpu.SMEM)] + [pl.BlockSpec(memory_space=pltpu.VMEM)] * (len(args) - 1),
        out_specs=[pl.BlockSpec(memory_space=pltpu.VMEM)] * len(outs),
        scratch_shapes=scratch,
        compiler_params=pltpu.CompilerParams(vmem_limit_bytes=limit * MIB),
        cost_estimate=pl.CostEstimate(flops=flops, bytes_accessed=nbytes, transcendentals=0),
    )(*args)


def shape(dims, dtype):
    return jax.ShapeDtypeStruct(dims, dtype)


def lanes(start, size):
    return pl.ds(pl.multiple_of(start, LANES), size)


def pack_first(size, width, scal, qkv_ref, out_ref, own_ref, sib_ref):
    quarter = width // 4
    for ref, member in ((own_ref, scal[2 * size + 1]), (sib_ref, scal[2 * size + 2])):
        for j in range(3):
            ref[:, j * quarter : (j + 1) * quarter] = qkv_ref[:, lanes(j * width + member * quarter, quarter)]
        ref[:, 3 * quarter :] = out_ref[:, lanes(member * quarter, quarter)]


def pack_in(size, units, piece, padded, scal, in_ref, own_ref, sib_ref):
    for ref, member in ((own_ref, scal[2 * size + 1]), (sib_ref, scal[2 * size + 2])):
        ref[...] = jnp.zeros_like(ref)
        for q in range(4):

            @pl.when(member == q)
            def _(ref=ref, q=q):
                for part in range(2):
                    for g in range(size):
                        start = part * units + (g * 4 + q) * piece
                        to = (part * size + g) * padded
                        ref[:, to : to + piece] = in_ref[:, start : start + piece]


def place_chunks(size, scal, chunk_refs, store):
    half = size // 2
    places = [k for k in range(size) if k != half]
    for k, ref in zip(places, chunk_refs, strict=False):
        store(scal[k], 0, ref[...])
    top, bottom = chunk_refs[-2:]
    store(scal[half], 0, top[...])
    store(scal[half], top.shape[0], bottom[...])


def place_rows(size, shard_rows, scal, chunk_refs, put):
    core = scal[2 * size]

    def store(chip, first, value):
        for lower in range(2):
            begin = lower * shard_rows - first
            if begin < 0 or begin >= value.shape[0]:
                continue
            row = chip * (2 * shard_rows) + (core if lower == 0 else 1 - core) * shard_rows
            put(pl.multiple_of(row, PACK), value[begin : begin + shard_rows])

    place_chunks(size, scal, chunk_refs, store)


def turned(values):
    lane = lax.broadcasted_iota(jnp.int32, values.shape, 1) % HD
    wide = values.shape[1]
    return jnp.where(lane < HALF, pltpu.roll(values, wide - HALF, 1), pltpu.roll(values, HALF, 1))


def visible(rows, length, limits):
    query = lax.broadcasted_iota(jnp.int32, (rows, rows), 0)
    key = lax.broadcasted_iota(jnp.int32, (rows, rows), 1)
    inside = (key % length).astype(F32)
    limit = jnp.zeros((rows, rows), F32)
    for s in range(rows // length):
        limit = jnp.where(key // length == s, limits[s : s + 1, :rows].astype(F32), limit)
    return (query // length == key // length) & ((key <= query) | (inside < limit))


def gather_out(size, shard_rows, quarter, scal, *refs):
    out_ref = refs[-1]

    def put(row, value):
        out_ref[pl.ds(row, shard_rows), :] = value[:, 3 * quarter :]

    place_rows(size, shard_rows, scal, refs[:-1], put)


def attention(size, shard_rows, rows, length, width, n_chunks, scal, *refs):
    blocks = refs[:4]
    chunks = refs[4 : 4 + n_chunks]
    cos_ref, sin_ref, o_ref, h1_ref, qkv_ref, p_ref, w_ref = refs[4 + n_chunks :]
    quarter = width // 4

    def put(row, value):
        w_ref[pl.ds(row, shard_rows), :] = value[:, : 3 * quarter]

    place_rows(size, shard_rows, scal, chunks, put)
    for b in range(4):
        normed, _ = norm_rows(blocks[b][:rows, :].astype(F32))
        h1_ref[b * rows : (b + 1) * rows, :] = normed.astype(BF)
    for j in range(3):
        mixed = dot(h1_ref[...], w_ref[:, j * quarter : (j + 1) * quarter])
        for b in range(4):
            piece = mixed[b * rows : (b + 1) * rows, :]
            if j < 2:
                piece = piece * cos_ref[...] + turned(piece) * sin_ref[...]
            qkv_ref[b * rows : (b + 1) * rows, j * quarter : (j + 1) * quarter] = piece.astype(BF)
    for b in range(4):
        allowed = visible(rows, length, blocks[b][rows:, :])
        block = slice(b * rows, (b + 1) * rows)
        for h in range(quarter // HD):
            query = qkv_ref[block, h * HD : (h + 1) * HD]
            keys = qkv_ref[block, quarter + h * HD : quarter + (h + 1) * HD]
            values = qkv_ref[block, 2 * quarter + h * HD : 2 * quarter + (h + 1) * HD]
            scores = jnp.where(allowed, dot_rt(query, keys) * HD ** (-0.5), -1e30)
            expo = jnp.exp(scores - jnp.max(scores, axis=-1, keepdims=True))
            probs = expo / jnp.sum(expo, axis=-1, keepdims=True)
            p_ref[b * (quarter // HD) + h] = probs
            o_ref[b, :, h * HD : (h + 1) * HD] = dot(probs.astype(BF), values).astype(BF)


def middle(size, rows, width, scal, *refs):
    blocks, cots, outputs, weights = refs[:4], refs[4:8], refs[8:12], refs[12:16]
    x2_ref, h2_ref, o_ref, rows_ref, gm_ref, w_full = refs[16:]
    quarter = width // 4
    members = [scal[2 * size + 1 + m] for m in range(4)]
    for m in range(4):
        w_full[:, lanes(members[m] * quarter, quarter)] = weights[m][...]
        gm_ref[m * rows : (m + 1) * rows, :] = cots[m][...]
        for b in range(4):
            o_ref[b * rows : (b + 1) * rows, lanes(members[m] * quarter, quarter)] = outputs[m][BLOCKS[m][b]]
    rows_ref[...] = w_full[pl.ds(pl.multiple_of(members[0] * quarter, quarter), quarter), :]
    for j in range(4):
        columns = slice(j * quarter, (j + 1) * quarter)
        added = dot(o_ref[...], w_full[:, columns])
        for b in range(4):
            x2_ref[b * rows : (b + 1) * rows, columns] = blocks[b][:rows, columns].astype(F32) + added[b * rows : (b + 1) * rows, :]
    for b in range(4):
        block = slice(b * rows, (b + 1) * rows)
        normed, _ = norm_rows(x2_ref[block, :])
        h2_ref[block, :] = normed.astype(BF)


def hidden_units(size, shard_rows, members_units, n_chunks, scal, h2_ref, *refs):
    chunks = refs[:n_chunks]
    up_ref, gate_ref, hid_ref, w_ref = refs[n_chunks:]

    def put(row, value):
        w_ref[pl.ds(row, shard_rows), :] = value

    place_rows(size, shard_rows, scal, chunks, put)
    tile = 256

    @pl.loop(0, members_units // tile)
    def _(i):
        at = pl.multiple_of(i * tile, tile)
        up = dot(h2_ref[...], w_ref[:, pl.ds(at, tile)])
        gate = dot(h2_ref[...], w_ref[:, pl.ds(members_units + at, tile)])
        up_ref[:, pl.ds(at, tile)] = up
        gate_ref[:, pl.ds(at, tile)] = gate
        hid_ref[:, pl.ds(at, tile)] = (gate * jax.nn.sigmoid(gate) * up).astype(BF)


def hidden_back(size, rows, padded, piece, n_chunks, scal, *refs):
    gm_ref = refs[0]
    chunks = refs[1 : 1 + n_chunks]
    up_ref, gate_ref, w_in, ggu_ref, keep_ref, give_ref, down_ref = refs[1 + n_chunks :]
    units = up_ref.shape[1]
    width = gm_ref.shape[1]
    down_ref[...] = jnp.zeros_like(down_ref)

    def store(chip, first, value):
        down_ref[pl.ds(pl.multiple_of(chip * padded + first, PACK), value.shape[0]), :] = value

    place_chunks(size, scal, chunks, store)
    tile = 256

    @pl.loop(0, units // tile)
    def _(i):
        at = pl.multiple_of(i * tile, tile)
        grad = dot_rt(gm_ref[...], down_ref[pl.ds(at, tile), :])
        up = up_ref[:, pl.ds(at, tile)]
        gate = gate_ref[:, pl.ds(at, tile)]
        sig = jax.nn.sigmoid(gate)
        ggu_ref[:, pl.ds(at, tile)] = (grad * (gate * sig)).astype(BF)
        ggu_ref[:, pl.ds(units + at, tile)] = (grad * up * (sig * (1.0 + gate * (1.0 - sig)))).astype(BF)

    @pl.loop(0, width // tile)
    def _(i):
        at = pl.multiple_of(i * tile, tile)
        back = dot_rt(ggu_ref[...], w_in[pl.ds(at, tile), :])
        share(back, rows, keep_ref, give_ref, pl.ds(at, tile))


def share(partial, rows, keep_ref, give_ref, columns):
    keep_ref[0, :, columns] = partial[:rows]
    give_ref[0, :, columns] = partial[rows : 2 * rows].astype(BF)
    keep_ref[1, :, columns] = partial[2 * rows : 3 * rows]
    give_ref[1, :, columns] = partial[3 * rows :].astype(BF)


def last_projection(rows, scal, hid_ref, down_ref, keep_ref, give_ref):
    tile = 256

    @pl.loop(0, down_ref.shape[1] // tile)
    def _(i):
        columns = pl.ds(pl.multiple_of(i * tile, tile), tile)
        share(dot(hid_ref[...], down_ref[:, columns]), rows, keep_ref, give_ref, columns)


def grad_down_parts(size, padded, piece, scal, hid_ref, gm_ref, part_ref):
    tile = 256

    @pl.loop(0, gm_ref.shape[1] // tile)
    def _(i):
        columns = pl.ds(pl.multiple_of(i * tile, tile), tile)
        grads = dot_lt(hid_ref[...], gm_ref[:, columns])
        for g in range(size):
            part_ref[scal[size + g], :, columns] = grads[g * padded : g * padded + piece]


def grad_in_parts(size, double, scal, h2_ref, ggu_ref, part_ref):
    tile = 256

    @pl.loop(0, ggu_ref.shape[1] // tile)
    def _(i):
        columns = pl.ds(pl.multiple_of(i * tile, tile), tile)
        grads = dot_lt(h2_ref[...], ggu_ref[:, columns])
        for g in range(size):
            part_ref[scal[size + g], :, columns] = grads[g * double : (g + 1) * double]


def middle_back(rows, scal, keep_ref, got_ref, far_ref, x2_ref, cot_own, cot_far, gx2_ref, ga_ref):
    for i, cot in ((0, cot_own), (1, cot_far)):
        upstream = keep_ref[i] + got_ref[i].astype(F32) + far_ref[1 - i].astype(F32)
        normed, inverse = norm_rows(x2_ref[2 * i * rows : (2 * i + 1) * rows, :])
        total = cot[...].astype(F32) + norm_back(normed, inverse, upstream)
        if i == 0:
            gx2_ref[...] = total
        ga_ref[i] = total.astype(BF)


def attention_back(rows, width, scal, ga_own, ga_near, out_rows, qkv_ref, p_ref, w_ref, cos_ref, sin_ref, gqkv_ref, ga_ref, keep_ref, give_ref, go_ref, grad_ref):
    quarter = width // 4
    for b, value in enumerate((ga_own[0], ga_near[0], ga_own[1], ga_near[1])):
        ga_ref[b * rows : (b + 1) * rows, :] = value
    go_ref[...] = dot_rt(ga_ref[...], out_rows[...]).astype(BF)
    for b in range(4):
        block = slice(b * rows, (b + 1) * rows)
        for h in range(quarter // HD):
            head = slice(h * HD, (h + 1) * HD)
            query = qkv_ref[block, h * HD : (h + 1) * HD]
            keys = qkv_ref[block, quarter + h * HD : quarter + (h + 1) * HD]
            values = qkv_ref[block, 2 * quarter + h * HD : 2 * quarter + (h + 1) * HD]
            probs = p_ref[b * (quarter // HD) + h]
            go = go_ref[block, head]
            dprob = dot_rt(go, values)
            centre = jnp.sum(probs * dprob, axis=-1, keepdims=True)
            dscore = (probs * (dprob - centre)).astype(BF)
            grad_ref[0, :, head] = dot(dscore, keys) * HD ** (-0.5)
            grad_ref[1, :, head] = dot_lt(dscore, query) * HD ** (-0.5)
            grad_ref[2, :, head] = dot_lt(probs.astype(BF), go)
        for j in range(3):
            grad = grad_ref[j]
            if j < 2:
                grad = grad * cos_ref[...] - turned(grad) * sin_ref[...]
            gqkv_ref[block, j * quarter : (j + 1) * quarter] = grad.astype(BF)
    for j in range(4):
        columns = slice(j * quarter, (j + 1) * quarter)
        share(dot_rt(gqkv_ref[...], w_ref[columns, :]), rows, keep_ref, give_ref, columns)


def grad_first_parts(size, double, width, scal, h1_ref, gqkv_ref, o_ref, ga_ref, part_ref):
    quarter = width // 4
    for j in range(4):
        if j < 3:
            grads = dot_lt(h1_ref[...], gqkv_ref[:, j * quarter : (j + 1) * quarter])
        else:
            grads = dot_lt(o_ref[...], ga_ref[:, lanes(scal[2 * size + 1] * quarter, quarter)])
        for g in range(size):
            part_ref[scal[size + g], :, j * quarter : (j + 1) * quarter] = grads[g * double : (g + 1) * double]


def finish_tokens(rows, scal, keep_ref, got_ref, far_ref, block_ref, gx2_ref, out_ref):
    upstream = keep_ref[0] + got_ref[0].astype(F32) + far_ref[...].astype(F32)
    normed, inverse = norm_rows(block_ref[:rows, :].astype(F32))
    out_ref[...] = gx2_ref[...] + norm_back(normed, inverse, upstream)


def unpack_first(size, width, scal, pair_ref, other_ref, qkv_ref, out_ref):
    quarter = width // 4
    for m, value in enumerate((pair_ref[0], pair_ref[1], other_ref[0], other_ref[1])):
        value = value.astype(F32)
        at = scal[2 * size + 1 + m] * quarter
        for j in range(3):
            qkv_ref[:, lanes(j * width + at, quarter)] = value[:, j * quarter : (j + 1) * quarter]
        out_ref[:, lanes(at, quarter)] = value[:, 3 * quarter :]


def unpack_in(size, units, piece, padded, scal, pair_ref, other_ref, in_ref, held):
    for m, value in enumerate((pair_ref[0], pair_ref[1], other_ref[0], other_ref[1])):
        held[scal[2 * size + 1 + m]] = value.astype(F32)
    for q in range(4):
        for part in range(2):
            for g in range(size):
                start = part * units + (g * 4 + q) * piece
                frm = (part * size + g) * padded
                in_ref[:, start : start + piece] = held[q, :, frm : frm + piece]


def local(tokens, prefix, qkv_weight, out_weight, in_weight, down_weight, cotangent):
    micro, _, length, width = tokens.shape
    rows = micro * length
    size = lax.axis_size("ring")
    ring = Ring(size)
    rep = lax.axis_index("rep")
    core = lax.axis_index("core")
    shard_rows = qkv_weight.shape[0]
    double = 2 * shard_rows
    units = in_weight.shape[1] // 2
    quarter = width // 4
    heads = quarter // HD
    piece = units // (4 * size)
    padded = -(-piece // PACK) * PACK
    while size * padded % 256:
        padded += PACK
    member_units = size * padded
    chunks = size + 1
    table = scalar_table(size)
    scal = lax.dynamic_slice(
        jnp.asarray(table.reshape(-1, table.shape[-1])), ((rep * size + lax.axis_index("ring")) * 2 + core, 0), (1, table.shape[-1])
    )[0]

    position = np.arange(length, dtype=np.float32)[:, None]
    frequency = np.float32(10000.0) ** (-np.arange(0, HD, 2, dtype=np.float32) / np.float32(HD))
    angles = (position * frequency[None, :]).astype(np.float32)
    angles = np.concatenate([angles, angles], axis=-1)
    sign = np.where(np.arange(HD) < HALF, -1.0, 1.0).astype(np.float32)
    cosine = jnp.asarray(np.tile(np.cos(angles), (micro, heads)).astype(np.float32))
    sine = jnp.asarray(np.tile(np.sin(angles) * sign, (micro, heads)).astype(np.float32))

    full_rows = 4 * rows
    pair_low = shape((2, rows, width), BF)
    pair_full = shape((2, rows, width), F32)
    project = 2 * full_rows * width * quarter

    own = jnp.concatenate([tokens.reshape(rows, width), jnp.broadcast_to(prefix.astype(BF), (micro, width))], axis=0)
    cot_own = cotangent.reshape(rows, width)
    a_own, a_sib = call(
        functools.partial(pack_first, size, width), [shape((shard_rows, width), BF)] * 2, [], 8, 0, scal, qkv_weight, out_weight
    )
    a_got = sibling(a_sib)
    near = sibling(own)
    a = Gather(ring, jnp.concatenate([a_own, a_got], axis=0))

    a.state, own, cot_own, in_weight, near = sync(a.state, own, cot_own, in_weight, near)
    a.advance()
    far = across(own)
    cot_near = sibling(cot_own)
    b_own, b_sib = call(
        functools.partial(pack_in, size, units, piece, padded), [shape((shard_rows, 2 * member_units), BF)] * 2, [], 8, 0, scal, in_weight
    )

    a.state, far, cot_own, b_own, b_sib, cot_near = sync(a.state, far, cot_own, b_own, b_sib, cot_near)
    a.advance()
    diagonal = sibling(far)
    cot_far = across(cot_own)
    b_got = sibling(b_sib)

    a.state, cot_far, b_own, b_got, diagonal, down_weight = sync(a.state, cot_far, b_own, b_got, diagonal, down_weight)
    a.advance()
    cot_diagonal = sibling(cot_far)
    b = Gather(ring, jnp.concatenate([b_own, b_got], axis=0))
    c = Gather(ring, lax.dynamic_slice(down_weight, (rep * piece, 0), (piece, width)))
    blocks = [own, near, far, diagonal]

    a.state, b.state, c.state, cot_diagonal, blocks = sync(a.state, b.state, c.state, cot_diagonal, blocks)
    c.advance()
    a_chunks = a.finish()
    cots = [cot_own, cot_near, cot_far, cot_diagonal]

    a_chunks, b.state, c.state = sync(a_chunks, b.state, c.state)
    b.advance()
    c.advance()
    (out_mine,) = call(functools.partial(gather_out, size, shard_rows, quarter), [shape((width, quarter), BF)], [], 8, 0, scal, *a_chunks)
    out_far = across(out_mine)
    o_own, h1, qkv, probs, qkv_mine = call(
        functools.partial(attention, size, shard_rows, rows, length, width, chunks),
        [
            shape((4, rows, quarter), BF),
            shape((full_rows, width), BF),
            shape((full_rows, 3 * quarter), BF),
            shape((4 * heads, rows, rows), F32),
            shape((width, 3 * quarter), BF),
        ],
        [],
        24,
        3 * project,
        scal,
        *blocks,
        *a_chunks,
        cosine,
        sine,
    )

    o_own, out_mine, out_far, b.state, c.state = sync(o_own, out_mine, out_far, b.state, c.state)
    o_far = across(o_own)
    b.advance()
    c.advance()
    o_near = sibling(o_own)
    out_near = sibling(out_mine)
    out_diagonal = sibling(out_far)

    o_far, o_near, out_near, out_diagonal, b.state, c.state = sync(o_far, o_near, out_near, out_diagonal, b.state, c.state)
    o_diagonal = sibling(o_far)
    b.advance()
    c_chunks = c.finish()
    x2, h2, o_all, out_rows, gm = call(
        functools.partial(middle, size, rows, width),
        [
            shape((full_rows, width), F32),
            shape((full_rows, width), BF),
            shape((full_rows, width), BF),
            shape((quarter, width), BF),
            shape((full_rows, width), BF),
        ],
        [pltpu.VMEM((width, width), BF)],
        24,
        4 * project,
        scal,
        *blocks,
        *cots,
        o_own,
        o_near,
        o_far,
        o_diagonal,
        out_mine,
        out_near,
        out_far,
        out_diagonal,
    )

    h2, b.state, c_chunks = sync(h2, b.state, c_chunks)
    b_chunks = b.finish()
    up, gate, hid, in_mine = call(
        functools.partial(hidden_units, size, shard_rows, member_units, chunks),
        [
            shape((full_rows, member_units), F32),
            shape((full_rows, member_units), F32),
            shape((full_rows, member_units), BF),
            shape((width, 2 * member_units), BF),
        ],
        [],
        28,
        6 * project,
        scal,
        h2,
        *b_chunks,
    )
    (down_parts,) = call(
        functools.partial(grad_down_parts, size, padded, piece), [shape((size, piece, width), F32)], [], 16, 3 * project, scal, hid, gm
    )

    c = Scatter(ring, down_parts)
    c.state, gm, up = sync(c.state, gm, up)
    c.advance()
    ggu, u2_keep, u2_give, down_mine = call(
        functools.partial(hidden_back, size, rows, padded, piece, chunks),
        [shape((full_rows, 2 * member_units), BF), pair_full, pair_low, shape((member_units, width), BF)],
        [],
        32,
        9 * project,
        scal,
        gm,
        *c_chunks,
        up,
        gate,
        in_mine,
    )

    u2_give, c.state, ggu = sync(u2_give, c.state, ggu)
    u2_got = sibling(u2_give)
    c.advance()
    (in_parts,) = call(
        functools.partial(grad_in_parts, size, double), [shape((size, double, 2 * member_units), F32)], [], 24, 6 * project, scal, h2, ggu
    )
    b = Scatter(ring, in_parts)
    u2_low = (u2_keep + u2_got.astype(F32)).astype(BF)

    u2_low, b.state, c.state, hid = sync(u2_low, b.state, c.state, hid)
    u2_far = across(u2_low)
    b.advance()
    c.advance()
    y_keep, y_give = call(functools.partial(last_projection, rows), [pair_full, pair_low], [], 16, 3 * project, scal, hid, down_mine)

    u2_far, b.state, c.state, y_give = sync(u2_far, b.state, c.state, y_give)
    b.advance()
    c.advance()
    y_got = sibling(y_give)
    gx2, ga = call(
        functools.partial(middle_back, rows), [shape((rows, width), F32), pair_low], [], 16, 0, scal, u2_keep, u2_got, u2_far, x2, cots[0], cots[2]
    )
    ga_near = sibling(ga)
    gqkv, ga_all, u1_keep, u1_give = call(
        functools.partial(attention_back, rows, width),
        [shape((full_rows, 3 * quarter), BF), shape((full_rows, width), BF), pair_full, pair_low],
        [pltpu.VMEM((full_rows, quarter), BF), pltpu.VMEM((3, rows, quarter), F32)],
        24,
        7 * project,
        scal,
        ga,
        ga_near,
        out_rows,
        qkv,
        probs,
        qkv_mine,
        cosine,
        sine,
    )
    (first_parts,) = call(
        functools.partial(grad_first_parts, size, double, width),
        [shape((size, double, width), F32)],
        [],
        24,
        4 * project,
        scal,
        h1,
        gqkv,
        o_all,
        ga_all,
    )
    a = Scatter(ring, first_parts)
    down_low = c.finish().astype(BF)
    y_low = (y_keep[1] + y_got[1].astype(F32)).astype(BF)

    a.state, b.state, u1_give, y_low = sync(a.state, b.state, u1_give, y_low)
    a.advance()
    b.advance()
    u1_got = sibling(u1_give)
    y_far = across(y_low)
    u1_low = (u1_keep[1] + u1_got[1].astype(F32)).astype(BF)

    def halves(low):
        keep = lax.dynamic_slice(low, (core * shard_rows, 0), (shard_rows, low.shape[1]))
        give = lax.dynamic_slice(low, ((1 - core) * shard_rows, 0), (shard_rows, low.shape[1]))
        return keep, give

    a.state, b.state, u1_low, y_far = sync(a.state, b.state, u1_low, y_far)
    a.advance()
    in_low = b.finish().astype(BF)
    u1_far = across(u1_low)
    result = (x2[:rows] + (y_keep[0] + y_got[0].astype(F32) + y_far.astype(F32))).astype(BF)

    in_keep, in_give = halves(in_low)
    a.state, in_give, u1_far, down_low = sync(a.state, in_give, u1_far, down_low)
    a.advance()
    in_got = sibling(in_give)
    down_other = across(down_low)
    (grad_tokens,) = call(
        functools.partial(finish_tokens, rows), [shape((rows, width), F32)], [], 16, 0, scal, u1_keep, u1_got, u1_far, own, gx2
    )

    in_pair = jnp.stack([in_keep, in_got])
    a.state, in_pair, down_other = sync(a.state, in_pair, down_other)
    in_other = across(in_pair)
    first_keep, first_give = halves(a.finish().astype(BF))
    grad_down = jnp.where(rep == 0, jnp.concatenate([down_low, down_other]), jnp.concatenate([down_other, down_low])).astype(F32)

    first_pair = jnp.stack([first_keep, sibling(first_give)])
    first_pair, in_other = sync(first_pair, in_other)
    first_other = across(first_pair)
    (grad_in,) = call(
        functools.partial(unpack_in, size, units, piece, padded),
        [shape((shard_rows, 2 * units), F32)],
        [pltpu.VMEM((4, shard_rows, 2 * member_units), F32)],
        16,
        0,
        scal,
        in_pair,
        in_other,
    )
    grad_qkv, grad_out = call(
        functools.partial(unpack_first, size, width),
        [shape((shard_rows, 3 * width), F32), shape((shard_rows, width), F32)],
        [],
        16,
        0,
        scal,
        first_pair,
        first_other,
    )
    return (
        result.reshape(micro, 1, length, width),
        grad_tokens.reshape(micro, 1, length, width),
        grad_qkv,
        grad_out,
        grad_in,
        grad_down,
    )


def solution(mesh):
    inner = Mesh(mesh.devices.reshape(mesh.shape["rep"], mesh.shape["shard"] // 2, 2), ("rep", "ring", "core"))
    everyone = ("rep", "ring", "core")
    group = ("ring", "core")
    sequences = P(None, everyone, None, None)
    weights = P(group, None)
    return jax.shard_map(
        local,
        mesh=inner,
        in_specs=(sequences, P(None, everyone), weights, weights, weights, weights, sequences),
        out_specs=(sequences, sequences, weights, weights, weights, weights),
        check_vma=False,
    )
```

```python
import functools

import jax
import jax.numpy as jnp
import numpy as np
from jax import lax
from jax.experimental import pallas as pl
from jax.experimental.pallas import tpu as pltpu
from jax.sharding import Mesh, PartitionSpec as P

H = 16
HD = 64
HALF = HD // 2
LANES = 128
PACK = 16
BF = jnp.bfloat16
F32 = jnp.float32
SWAP = ((0, 1), (1, 0))
MIB = 1 << 20
BLOCKS = ((0, 1, 2, 3), (1, 0, 3, 2), (2, 3, 0, 1), (3, 2, 1, 0))


def dot(left, right):
    return jnp.dot(left, right, preferred_element_type=F32)


def dot_rt(left, right):
    return lax.dot_general(left, right, (((1,), (1,)), ((), ())), preferred_element_type=F32)


def dot_lt(left, right):
    return lax.dot_general(left, right, (((0,), (0,)), ((), ())), preferred_element_type=F32)


def norm_rows(values):
    centre = values - jnp.mean(values, axis=-1, keepdims=True)
    inverse = lax.rsqrt(jnp.mean(centre * centre, axis=-1, keepdims=True) + 1e-05)
    return (centre * inverse, inverse)


def norm_back(normed, inverse, upstream):
    return inverse * (
        upstream
        - jnp.mean(upstream, axis=-1, keepdims=True)
        - normed * jnp.mean(upstream * normed, axis=-1, keepdims=True)
    )


def across(value):
    return lax.ppermute(value, "rep", SWAP)


def sibling(value):
    return lax.ppermute(value, "core", SWAP)


def order_of(size):
    return list(range(0, size, 2)) + list(range(size - 1, 0, -2))


def scalar_table(size):
    order = order_of(size)
    place = np.argsort(order)
    table = np.zeros((2, size, 2, 2 * size + 5), np.int32)
    for rep in range(2):
        for g in range(size):
            for core in range(2):
                at = [order[(place[g] + k) % size] for k in range(size)]
                of = [(place[o] - place[g]) % size for o in range(size)]
                members = [2 * core + rep, 2 * (1 - core) + rep, 2 * core + 1 - rep, 2 * (1 - core) + 1 - rep]
                table[rep, g, core] = at + of + [core] + members
    return table


def upper_half(rows):
    return -(-(rows // 2) // PACK) * PACK


class Ring:
    def __init__(self, size):
        self.size = size
        self.half = size // 2
        order = order_of(size)
        self.right = [(order[i], order[(i + 1) % size]) for i in range(size)]
        self.left = [(b, a) for a, b in self.right]

    def exchange(self, pair):
        return lax.ppermute(pair[0], "ring", self.right), lax.ppermute(pair[1], "ring", self.left)


class Gather:
    def __init__(self, ring, chunk):
        self.ring = ring
        self.step = 0
        self.got = {0: chunk}
        self.cut = upper_half(chunk.shape[0])
        self.state = (chunk, chunk)

    def advance(self):
        if self.step == self.ring.half:
            return
        self.step += 1
        if self.step == self.ring.half:
            self.far = self.ring.exchange((self.state[0][: self.cut], self.state[1][self.cut :]))
            self.state = ()
            return
        self.state = self.ring.exchange(self.state)
        self.got[self.ring.size - self.step], self.got[self.step] = self.state

    def finish(self):
        while self.step < self.ring.half:
            self.advance()
        return [self.got[k] for k in range(self.ring.size) if k != self.ring.half] + list(self.far)


class Scatter:
    def __init__(self, ring, parts):
        self.ring = ring
        self.step = 0
        self.parts = parts
        self.cut = upper_half(parts[0].shape[0])
        far = parts[ring.half]
        self.state = (far[: self.cut], far[self.cut :])

    def send(self):
        self.got = self.ring.exchange(self.state)

    def add(self):
        ring = self.ring
        self.step += 1
        place = ring.half - self.step
        right, left = self.got
        if self.step == 1:
            right = jnp.pad(right, ((0, self.parts[0].shape[0] - self.cut), (0, 0)))
            left = jnp.pad(left, ((self.cut, 0), (0, 0)))
        terms = (self.parts[place], self.parts[ring.size - place])
        self.state = tuple((t.astype(F32) + v.astype(F32)).astype(BF) for t, v in zip(terms, (right, left), strict=True))

    def run(self):
        while self.step < self.ring.half - 1:
            self.add()
            self.send()
        return self.parts[0], *self.got


def sync(*values):
    return lax.optimization_barrier(values)


def call(body, outs, scratch, flops, *args):
    nbytes = sum(a.size * a.dtype.itemsize for a in args) + sum(o.size * o.dtype.itemsize for o in outs)
    return pl.pallas_call(
        body,
        name=body.func.__name__,
        out_shape=outs,
        in_specs=[pl.BlockSpec(memory_space=pltpu.SMEM)] + [pl.BlockSpec(memory_space=pltpu.VMEM)] * (len(args) - 1),
        out_specs=[pl.BlockSpec(memory_space=pltpu.VMEM)] * len(outs),
        scratch_shapes=scratch,
        compiler_params=pltpu.CompilerParams(vmem_limit_bytes=32 * MIB),
        cost_estimate=pl.CostEstimate(flops=flops, bytes_accessed=nbytes, transcendentals=0),
    )(*args)


def shape(dims, dtype):
    return jax.ShapeDtypeStruct(dims, dtype)


def lanes(start, size):
    return pl.ds(pl.multiple_of(start, LANES), size)


def pack_tokens(rows, prefix_ref, tokens_ref, own_ref):
    own_ref[:rows, :] = tokens_ref[...]
    for m in range(own_ref.shape[0] - rows):
        own_ref[rows + m : rows + m + 1, :] = jnp.full((1, own_ref.shape[1]), prefix_ref[m, 0].astype(F32)).astype(BF)


def pack_first(size, width, scal, qkv_ref, out_ref, own_ref, sib_ref):
    quarter = width // 4
    for ref, member in ((own_ref, scal[2 * size + 1]), (sib_ref, scal[2 * size + 2])):
        for j in range(3):
            ref[:, j * quarter : (j + 1) * quarter] = qkv_ref[:, lanes(j * width + member * quarter, quarter)]
        ref[:, 3 * quarter :] = out_ref[:, lanes(member * quarter, quarter)]


def pack_in(size, units, piece, padded, scal, in_ref, own_ref, sib_ref):
    for ref, member in ((own_ref, scal[2 * size + 1]), (sib_ref, scal[2 * size + 2])):
        ref[...] = jnp.zeros_like(ref)
        for q in range(4):

            @pl.when(member == q)
            def _(ref=ref, q=q):
                for part in range(2):
                    for g in range(size):
                        start = part * units + (g * 4 + q) * piece
                        to = (part * size + g) * padded
                        ref[:, to : to + piece] = in_ref[:, start : start + piece]


def place_chunks(size, scal, chunk_refs, store):
    half = size // 2
    places = [k for k in range(size) if k != half]
    for k, ref in zip(places, chunk_refs, strict=False):
        store(scal[k], 0, ref[...])
    top, bottom = chunk_refs[-2:]
    store(scal[half], 0, top[...])
    store(scal[half], top.shape[0], bottom[...])


def place_rows(size, shard_rows, scal, chunk_refs, put):
    core = scal[2 * size]

    def store(chip, first, value):
        for lower in range(2):
            begin = lower * shard_rows - first
            if begin < 0 or begin >= value.shape[0]:
                continue
            row = chip * (2 * shard_rows) + (core if lower == 0 else 1 - core) * shard_rows
            put(pl.multiple_of(row, PACK), value[begin : begin + shard_rows])

    place_chunks(size, scal, chunk_refs, store)


def turned(values):
    lane = lax.broadcasted_iota(jnp.int32, values.shape, 1) % HD
    wide = values.shape[1]
    return jnp.where(lane < HALF, pltpu.roll(values, wide - HALF, 1), pltpu.roll(values, HALF, 1))


def visible(rows, length, limits):
    query = lax.broadcasted_iota(jnp.int32, (rows, rows), 0)
    key = lax.broadcasted_iota(jnp.int32, (rows, rows), 1)
    inside = (key % length).astype(F32)
    limit = jnp.zeros((rows, rows), F32)
    for s in range(rows // length):
        limit = jnp.where(key // length == s, limits[s : s + 1, :rows].astype(F32), limit)
    return (query // length == key // length) & ((key <= query) | (inside < limit))


def gather_out(size, shard_rows, quarter, scal, *refs):
    out_ref = refs[-1]

    def put(row, value):
        out_ref[pl.ds(row, shard_rows), :] = value[:, 3 * quarter :]

    place_rows(size, shard_rows, scal, refs[:-1], put)


def attention(size, shard_rows, rows, length, width, n_chunks, scal, *refs):
    blocks = refs[:4]
    chunks = refs[4 : 4 + n_chunks]
    cos_ref, sin_ref, o_ref, h1_ref, qkv_ref, p_ref, w_ref = refs[4 + n_chunks :]
    quarter = width // 4

    def put(row, value):
        w_ref[pl.ds(row, shard_rows), :] = value[:, : 3 * quarter]

    place_rows(size, shard_rows, scal, chunks, put)
    for b in range(4):
        normed, _ = norm_rows(blocks[b][:rows, :].astype(F32))
        h1_ref[b * rows : (b + 1) * rows, :] = normed.astype(BF)
    for j in range(3):
        mixed = dot(h1_ref[...], w_ref[:, j * quarter : (j + 1) * quarter])
        for b in range(4):
            piece = mixed[b * rows : (b + 1) * rows, :]
            if j < 2:
                piece = piece * cos_ref[...] + turned(piece) * sin_ref[...]
            qkv_ref[b * rows : (b + 1) * rows, j * quarter : (j + 1) * quarter] = piece.astype(BF)
    for b in range(4):
        allowed = visible(rows, length, blocks[b][rows:, :])
        block = slice(b * rows, (b + 1) * rows)
        for h in range(quarter // HD):
            query = qkv_ref[block, h * HD : (h + 1) * HD]
            keys = qkv_ref[block, quarter + h * HD : quarter + (h + 1) * HD]
            values = qkv_ref[block, 2 * quarter + h * HD : 2 * quarter + (h + 1) * HD]
            scores = jnp.where(allowed, dot_rt(query, keys) * HD ** (-0.5), -1e30)
            expo = jnp.exp(scores - jnp.max(scores, axis=-1, keepdims=True))
            probs = expo / jnp.sum(expo, axis=-1, keepdims=True)
            p_ref[b * (quarter // HD) + h] = probs
            o_ref[b, :, h * HD : (h + 1) * HD] = dot(probs.astype(BF), values).astype(BF)


def middle(size, rows, width, scal, *refs):
    blocks, cots = refs[:4], refs[4:8]
    o_own, o_far, w_own, w_far, near_ref = refs[8:13]
    full = 4 * rows
    outputs = (
        lambda b: o_own[b],
        lambda b: near_ref[b * rows : (b + 1) * rows],
        lambda b: o_far[b],
        lambda b: near_ref[full + b * rows : full + (b + 1) * rows],
    )
    weights = (w_own, near_ref.at[2 * full : 2 * full + width], w_far, near_ref.at[2 * full + width :])
    x2_ref, h2_ref, o_ref, rows_ref, gm_ref, w_full = refs[13:]
    quarter = width // 4
    members = [scal[2 * size + 1 + m] for m in range(4)]
    for m in range(4):
        w_full[:, lanes(members[m] * quarter, quarter)] = weights[m][...]
        gm_ref[m * rows : (m + 1) * rows, :] = cots[m][...]
        for b in range(4):
            o_ref[b * rows : (b + 1) * rows, lanes(members[m] * quarter, quarter)] = outputs[m](BLOCKS[m][b])
    rows_ref[...] = w_full[pl.ds(pl.multiple_of(members[0] * quarter, quarter), quarter), :]
    for j in range(4):
        columns = slice(j * quarter, (j + 1) * quarter)
        added = dot(o_ref[...], w_full[:, columns])
        for b in range(4):
            x2_ref[b * rows : (b + 1) * rows, columns] = blocks[b][:rows, columns].astype(F32) + added[b * rows : (b + 1) * rows, :]
    for b in range(4):
        block = slice(b * rows, (b + 1) * rows)
        normed, _ = norm_rows(x2_ref[block, :])
        h2_ref[block, :] = normed.astype(BF)


def hidden_units(size, shard_rows, members_units, n_chunks, scal, h2_ref, *refs):
    chunks = refs[:n_chunks]
    up_ref, gate_ref, hid_ref, w_ref = refs[n_chunks:]

    def put(row, value):
        w_ref[pl.ds(row, shard_rows), :] = value

    place_rows(size, shard_rows, scal, chunks, put)
    tile = 256

    @pl.loop(0, members_units // tile)
    def _(i):
        at = pl.multiple_of(i * tile, tile)
        up = dot(h2_ref[...], w_ref[:, pl.ds(at, tile)])
        gate = dot(h2_ref[...], w_ref[:, pl.ds(members_units + at, tile)])
        up_ref[:, pl.ds(at, tile)] = up
        gate_ref[:, pl.ds(at, tile)] = gate
        hid_ref[:, pl.ds(at, tile)] = (gate * jax.nn.sigmoid(gate) * up).astype(BF)


def hidden_back(size, rows, padded, piece, n_chunks, scal, *refs):
    gm_ref = refs[0]
    chunks = refs[1 : 1 + n_chunks]
    up_ref, gate_ref, w_in, ggu_ref, keep_ref, give_ref, down_ref = refs[1 + n_chunks :]
    units = up_ref.shape[1]
    width = gm_ref.shape[1]
    down_ref[...] = jnp.zeros_like(down_ref)

    def store(chip, first, value):
        down_ref[pl.ds(pl.multiple_of(chip * padded + first, PACK), value.shape[0]), :] = value

    place_chunks(size, scal, chunks, store)
    tile = 256

    @pl.loop(0, units // tile)
    def _(i):
        at = pl.multiple_of(i * tile, tile)
        grad = dot_rt(gm_ref[...], down_ref[pl.ds(at, tile), :])
        up = up_ref[:, pl.ds(at, tile)]
        gate = gate_ref[:, pl.ds(at, tile)]
        sig = jax.nn.sigmoid(gate)
        ggu_ref[:, pl.ds(at, tile)] = (grad * (gate * sig)).astype(BF)
        ggu_ref[:, pl.ds(units + at, tile)] = (grad * up * (sig * (1.0 + gate * (1.0 - sig)))).astype(BF)

    @pl.loop(0, width // tile)
    def _(i):
        at = pl.multiple_of(i * tile, tile)
        back = dot_rt(ggu_ref[...], w_in[pl.ds(at, tile), :])
        share(back, rows, keep_ref, give_ref, pl.ds(at, tile))


def share(partial, rows, keep_ref, give_ref, columns):
    keep_ref[0, :, columns] = partial[:rows]
    give_ref[0, :, columns] = partial[rows : 2 * rows].astype(BF)
    keep_ref[1, :, columns] = partial[2 * rows : 3 * rows]
    give_ref[1, :, columns] = partial[3 * rows :].astype(BF)


def last_projection(rows, scal, hid_ref, down_ref, keep_ref, give_ref):
    tile = 256

    @pl.loop(0, down_ref.shape[1] // tile)
    def _(i):
        columns = pl.ds(pl.multiple_of(i * tile, tile), tile)
        share(dot(hid_ref[...], down_ref[:, columns]), rows, keep_ref, give_ref, columns)


def write_parts(size, stride, scal, total, refs):
    for k, ref in enumerate(refs):
        ref[...] = total[pl.ds(pl.multiple_of(scal[k] * stride, PACK), ref.shape[0]), :].astype(BF)


def grad_down_parts(size, padded, scal, hid_ref, gm_ref, *refs):
    total = refs[-1]
    tile = 256

    @pl.loop(0, gm_ref.shape[1] // tile)
    def _(i):
        columns = pl.ds(pl.multiple_of(i * tile, tile), tile)
        total[:, columns] = dot_lt(hid_ref[...], gm_ref[:, columns])

    write_parts(size, padded, scal, total, refs[:-1])


def grad_in_parts(size, double, scal, h2_ref, ggu_ref, *refs):
    total = refs[-1]
    tile = 256

    @pl.loop(0, ggu_ref.shape[1] // tile)
    def _(i):
        columns = pl.ds(pl.multiple_of(i * tile, tile), tile)
        total[:, columns] = dot_lt(h2_ref[...], ggu_ref[:, columns])

    write_parts(size, double, scal, total, refs[:-1])


def middle_back(rows, scal, keep_ref, got_ref, far_ref, x2_ref, cot_own, cot_far, gx2_ref, ga_ref):
    for i, cot in ((0, cot_own), (1, cot_far)):
        upstream = keep_ref[i] + got_ref[i].astype(F32) + far_ref[1 - i].astype(F32)
        normed, inverse = norm_rows(x2_ref[2 * i * rows : (2 * i + 1) * rows, :])
        total = cot[...].astype(F32) + norm_back(normed, inverse, upstream)
        if i == 0:
            gx2_ref[...] = total
        ga_ref[i] = total.astype(BF)


def attention_back(rows, width, scal, ga_own, ga_near, out_rows, qkv_ref, p_ref, w_ref, cos_ref, sin_ref, gqkv_ref, ga_ref, keep_ref, give_ref, go_ref, grad_ref):
    quarter = width // 4
    for b, value in enumerate((ga_own[0], ga_near[0], ga_own[1], ga_near[1])):
        ga_ref[b * rows : (b + 1) * rows, :] = value
    go_ref[...] = dot_rt(ga_ref[...], out_rows[...]).astype(BF)
    for b in range(4):
        block = slice(b * rows, (b + 1) * rows)
        for h in range(quarter // HD):
            head = slice(h * HD, (h + 1) * HD)
            query = qkv_ref[block, h * HD : (h + 1) * HD]
            keys = qkv_ref[block, quarter + h * HD : quarter + (h + 1) * HD]
            values = qkv_ref[block, 2 * quarter + h * HD : 2 * quarter + (h + 1) * HD]
            probs = p_ref[b * (quarter // HD) + h]
            go = go_ref[block, head]
            dprob = dot_rt(go, values)
            centre = jnp.sum(probs * dprob, axis=-1, keepdims=True)
            dscore = (probs * (dprob - centre)).astype(BF)
            grad_ref[0, :, head] = dot(dscore, keys) * HD ** (-0.5)
            grad_ref[1, :, head] = dot_lt(dscore, query) * HD ** (-0.5)
            grad_ref[2, :, head] = dot_lt(probs.astype(BF), go)
        for j in range(3):
            grad = grad_ref[j]
            if j < 2:
                grad = grad * cos_ref[...] - turned(grad) * sin_ref[...]
            gqkv_ref[block, j * quarter : (j + 1) * quarter] = grad.astype(BF)
    for j in range(4):
        columns = slice(j * quarter, (j + 1) * quarter)
        share(dot_rt(gqkv_ref[...], w_ref[columns, :]), rows, keep_ref, give_ref, columns)


def grad_first_parts(size, double, width, scal, h1_ref, gqkv_ref, o_ref, ga_ref, *refs):
    total = refs[-1]
    quarter = width // 4
    for j in range(3):
        columns = slice(j * quarter, (j + 1) * quarter)
        total[:, columns] = dot_lt(h1_ref[...], gqkv_ref[:, columns])
    total[:, 3 * quarter :] = dot_lt(o_ref[...], ga_ref[:, lanes(scal[2 * size + 1] * quarter, quarter)])
    write_parts(size, double, scal, total, refs[:-1])


def split_rows(size, scal, own_ref, right_ref, left_ref, keep_ref, give_ref):
    core = scal[2 * size]
    rows = keep_ref.shape[0]
    for ref, first in ((keep_ref, core), (give_ref, 1 - core)):
        here = pl.ds(pl.multiple_of(first * rows, PACK), rows)
        ref[...] = (own_ref[here, :].astype(F32) + right_ref[here, :].astype(F32) + left_ref[here, :].astype(F32)).astype(BF)


def finish_tokens(rows, scal, keep_ref, got_ref, far_ref, block_ref, gx2_ref, out_ref):
    upstream = keep_ref[0] + got_ref[0].astype(F32) + far_ref[...].astype(F32)
    normed, inverse = norm_rows(block_ref[:rows, :].astype(F32))
    out_ref[...] = gx2_ref[...] + norm_back(normed, inverse, upstream)


def unpack_first(size, width, scal, own_ref, near_ref, far_ref, diagonal_ref, qkv_ref, out_ref):
    quarter = width // 4
    for m, ref in enumerate((own_ref, near_ref, far_ref, diagonal_ref)):
        value = ref[...].astype(F32)
        at = scal[2 * size + 1 + m] * quarter
        for j in range(3):
            qkv_ref[:, lanes(j * width + at, quarter)] = value[:, j * quarter : (j + 1) * quarter]
        out_ref[:, lanes(at, quarter)] = value[:, 3 * quarter :]


def unpack_in(size, units, piece, padded, scal, own_ref, near_ref, far_ref, diagonal_ref, in_ref, held):
    for m, ref in enumerate((own_ref, near_ref, far_ref, diagonal_ref)):
        held[scal[2 * size + 1 + m]] = ref[...].astype(F32)
    for q in range(4):
        for part in range(2):
            for g in range(size):
                start = part * units + (g * 4 + q) * piece
                frm = (part * size + g) * padded
                in_ref[:, start : start + piece] = held[q, :, frm : frm + piece]


def local(tokens, prefix, qkv_weight, out_weight, in_weight, down_weight, cotangent):
    micro, _, length, width = tokens.shape
    rows = micro * length
    size = lax.axis_size("ring")
    ring = Ring(size)
    rep = lax.axis_index("rep")
    core = lax.axis_index("core")
    shard_rows = qkv_weight.shape[0]
    double = 2 * shard_rows
    units = in_weight.shape[1] // 2
    quarter = width // 4
    heads = quarter // HD
    piece = units // (4 * size)
    padded = -(-piece // PACK) * PACK
    while size * padded % 256:
        padded += PACK
    member_units = size * padded
    chunks = size + 1
    table = scalar_table(size)
    scal = lax.dynamic_slice(
        jnp.asarray(table.reshape(-1, table.shape[-1])), ((rep * size + lax.axis_index("ring")) * 2 + core, 0), (1, table.shape[-1])
    )[0]

    position = np.arange(length, dtype=np.float32)[:, None]
    frequency = np.float32(10000.0) ** (-np.arange(0, HD, 2, dtype=np.float32) / np.float32(HD))
    angles = (position * frequency[None, :]).astype(np.float32)
    angles = np.concatenate([angles, angles], axis=-1)
    sign = np.where(np.arange(HD) < HALF, -1.0, 1.0).astype(np.float32)
    cosine = jnp.asarray(np.tile(np.cos(angles), (micro, heads)).astype(np.float32))
    sine = jnp.asarray(np.tile(np.sin(angles) * sign, (micro, heads)).astype(np.float32))

    full_rows = 4 * rows
    pair_low = shape((2, rows, width), BF)
    pair_full = shape((2, rows, width), F32)
    project = 2 * full_rows * width * quarter

    tokens = tokens.reshape(rows, width)
    cot_own = cotangent.reshape(rows, width)
    a_own, a_sib = call(functools.partial(pack_first, size, width), [shape((shard_rows, width), BF)] * 2, [], 0, scal, qkv_weight, out_weight)
    a = Gather(ring, jnp.concatenate([a_own, sibling(a_sib)], axis=0))

    a.state, in_weight = sync(a.state, in_weight)
    a.advance()
    b_own, b_sib = call(
        functools.partial(pack_in, size, units, piece, padded), [shape((shard_rows, 2 * member_units), BF)] * 2, [], 0, scal, in_weight
    )
    b_own, b_sib, tokens = sync(b_own, b_sib, tokens)
    (own,) = call(functools.partial(pack_tokens, rows), [shape((rows + micro, width), BF)], [], 0, prefix, tokens)

    a.state, own, b_own, b_sib = sync(a.state, own, b_own, b_sib)
    a.advance()
    far = across(own)
    near = sibling(own)
    b_got = sibling(b_sib)

    a.state, cot_own, far, near, b_own, b_got, down_weight = sync(a.state, cot_own, far, near, b_own, b_got, down_weight)
    a.advance()
    cot_far = across(cot_own)
    diagonal = sibling(far)
    cot_near = sibling(cot_own)
    b = Gather(ring, jnp.concatenate([b_own, b_got], axis=0))
    c = Gather(ring, lax.dynamic_slice(down_weight, (rep * piece, 0), (piece, width)))

    a.state, b.state, c.state, cot_near, cot_far, diagonal = sync(a.state, b.state, c.state, cot_near, cot_far, diagonal)
    c.advance()
    a_chunks = a.finish()
    cot_diagonal = sibling(cot_far)
    blocks = [own, near, far, diagonal]
    cots = [cot_own, cot_near, cot_far, cot_diagonal]

    a_chunks, b.state, c.state = sync(a_chunks, b.state, c.state)
    b.advance()
    c.advance()
    (out_mine,) = call(functools.partial(gather_out, size, shard_rows, quarter), [shape((width, quarter), BF)], [], 0, scal, *a_chunks)
    out_far = across(out_mine)
    o_own, h1, qkv, probs, qkv_mine = call(
        functools.partial(attention, size, shard_rows, rows, length, width, chunks),
        [
            shape((4, rows, quarter), BF),
            shape((full_rows, width), BF),
            shape((full_rows, 3 * quarter), BF),
            shape((4 * heads, rows, rows), F32),
            shape((width, 3 * quarter), BF),
        ],
        [],
        3 * project,
        scal,
        *blocks,
        *a_chunks,
        cosine,
        sine,
    )

    o_own, out_mine, out_far, b.state, c.state = sync(o_own, out_mine, out_far, b.state, c.state)
    o_far = across(o_own)
    b.advance()
    c.advance()

    o_far, b.state, c.state = sync(o_far, b.state, c.state)
    kept = [o_own.reshape(full_rows, quarter), o_far.reshape(full_rows, quarter), out_mine, out_far]
    near_all = sibling(jnp.concatenate(kept, axis=0))
    b.advance()
    c_chunks = c.finish()
    x2, h2, o_all, out_rows, gm = call(
        functools.partial(middle, size, rows, width),
        [
            shape((full_rows, width), F32),
            shape((full_rows, width), BF),
            shape((full_rows, width), BF),
            shape((quarter, width), BF),
            shape((full_rows, width), BF),
        ],
        [pltpu.VMEM((width, width), BF)],
        4 * project,
        scal,
        *blocks,
        *cots,
        o_own,
        o_far,
        out_mine,
        out_far,
        near_all,
    )

    h2, b.state, c_chunks = sync(h2, b.state, c_chunks)
    b_chunks = b.finish()
    up, gate, hid, in_mine = call(
        functools.partial(hidden_units, size, shard_rows, member_units, chunks),
        [
            shape((full_rows, member_units), F32),
            shape((full_rows, member_units), F32),
            shape((full_rows, member_units), BF),
            shape((width, 2 * member_units), BF),
        ],
        [],
        6 * project,
        scal,
        h2,
        *b_chunks,
    )
    down_parts = call(
        functools.partial(grad_down_parts, size, padded), [shape((piece, width), BF)] * size, [pltpu.VMEM((member_units, width), F32)], 3 * project, scal, hid, gm
    )

    c = Scatter(ring, down_parts)
    c.state, gm, up = sync(c.state, gm, up)
    c.send()
    ggu, u2_keep, u2_give, down_mine = call(
        functools.partial(hidden_back, size, rows, padded, piece, chunks),
        [shape((full_rows, 2 * member_units), BF), pair_full, pair_low, shape((member_units, width), BF)],
        [],
        9 * project,
        scal,
        gm,
        *c_chunks,
        up,
        gate,
        in_mine,
    )

    u2_give, c.got = sync(u2_give, c.got)
    u2_got = sibling(u2_give)
    c.add()
    c.send()
    u2_low = (u2_keep + u2_got.astype(F32)).astype(BF)

    u2_low, ggu = sync(u2_low, ggu)
    u2_far = across(u2_low)
    in_parts = call(
        functools.partial(grad_in_parts, size, double),
        [shape((double, 2 * member_units), BF)] * size,
        [pltpu.VMEM((width, 2 * member_units), F32)],
        6 * project,
        scal,
        h2,
        ggu,
    )

    b = Scatter(ring, in_parts)
    b.state, c.got, hid = sync(b.state, c.got, hid)
    b.send()
    c.add()
    c.send()
    y_keep, y_give = call(functools.partial(last_projection, rows), [pair_full, pair_low], [], 3 * project, scal, hid, down_mine)

    y_give, c.got, b.got = sync(y_give, c.got, b.got)
    b.add()
    b.send()
    c.add()
    c.send()
    gx2, ga = call(
        functools.partial(middle_back, rows), [shape((rows, width), F32), pair_low], [], 0, scal, u2_keep, u2_got, u2_far, x2, cots[0], cots[2]
    )
    ga_near = sibling(ga)
    y_got = sibling(y_give)
    y_low = (y_keep[1] + y_got[1].astype(F32)).astype(BF)

    y_low, ga_near = sync(y_low, ga_near)
    y_far = across(y_low)
    gqkv, ga_all, u1_keep, u1_give = call(
        functools.partial(attention_back, rows, width),
        [shape((full_rows, 3 * quarter), BF), shape((full_rows, width), BF), pair_full, pair_low],
        [pltpu.VMEM((full_rows, quarter), BF), pltpu.VMEM((3, rows, quarter), F32)],
        7 * project,
        scal,
        ga,
        ga_near,
        out_rows,
        qkv,
        probs,
        qkv_mine,
        cosine,
        sine,
    )

    gqkv, u1_give, c.got, b.got, y_far = sync(gqkv, u1_give, c.got, b.got, y_far)
    b.add()
    b.send()
    u1_got = sibling(u1_give)
    first_parts = call(
        functools.partial(grad_first_parts, size, double, width),
        [shape((double, width), BF)] * size,
        [pltpu.VMEM((width, width), F32)],
        4 * project,
        scal,
        h1,
        gqkv,
        o_all,
        ga_all,
    )
    down_low = sum(v.astype(F32) for v in c.run()).astype(BF)

    a = Scatter(ring, first_parts)
    a.state, u1_got, down_low = sync(a.state, u1_got, down_low)
    a.send()
    u1_low = (u1_keep[1] + u1_got[1].astype(F32)).astype(BF)
    u1_far = across(u1_low)

    a.got, b.got, u1_far = sync(a.got, b.got, u1_far)
    a.add()
    a.send()
    b.add()
    b.send()
    down_other = across(down_low)

    while a.step < ring.half - 2:
        (a.got,) = sync(a.got)
        a.add()
        a.send()

    def halves(summed):
        columns = summed[0].shape[1]
        return call(functools.partial(split_rows, size), [shape((shard_rows, columns), BF)] * 2, [], 0, scal, *summed)

    b_sum = b.run()
    a.got, b_sum, down_other = sync(a.got, b_sum, down_other)
    a.add()
    a.send()
    in_keep, in_give = halves(b_sum)
    in_near = sibling(in_give)
    in_pair = jnp.stack([in_keep, in_near])
    in_other = across(in_pair)
    a_sum = a.run()
    first_keep, first_give = halves(a_sum)
    first_keep, first_give, in_other = sync(first_keep, first_give, in_other)
    first_far = across(first_keep)
    first_near = sibling(first_give)
    first_diagonal = across(first_near)
    u1_far, y_far, down_other, in_near, first_near = sync(u1_far, y_far, down_other, in_near, first_near)
    (grad_tokens,) = call(
        functools.partial(finish_tokens, rows), [shape((rows, width), F32)], [], 0, scal, u1_keep, u1_got, u1_far, own, gx2
    )
    result = (x2[:rows] + (y_keep[0] + y_got[0].astype(F32) + y_far.astype(F32))).astype(BF)
    grad_down = jnp.where(rep == 0, jnp.concatenate([down_low, down_other]), jnp.concatenate([down_other, down_low])).astype(F32)
    (grad_in,) = call(
        functools.partial(unpack_in, size, units, piece, padded),
        [shape((shard_rows, 2 * units), F32)],
        [pltpu.VMEM((4, shard_rows, 2 * member_units), F32)],
        0,
        scal,
        in_keep,
        in_near,
        in_other[0],
        in_other[1],
    )
    grad_qkv, grad_out = call(
        functools.partial(unpack_first, size, width),
        [shape((shard_rows, 3 * width), F32), shape((shard_rows, width), F32)],
        [],
        0,
        scal,
        first_keep,
        first_near,
        first_far,
        first_diagonal,
    )
    return (
        result.reshape(micro, 1, length, width),
        grad_tokens.reshape(micro, 1, length, width),
        grad_qkv,
        grad_out,
        grad_in,
        grad_down,
    )


def solution(mesh):
    inner = Mesh(mesh.devices.reshape(mesh.shape["rep"], mesh.shape["shard"] // 2, 2), ("rep", "ring", "core"))
    everyone = ("rep", "ring", "core")
    group = ("ring", "core")
    sequences = P(None, everyone, None, None)
    weights = P(group, None)
    return jax.shard_map(
        local,
        mesh=inner,
        in_specs=(sequences, P(None, everyone), weights, weights, weights, weights, sequences),
        out_specs=(sequences, sequences, weights, weights, weights, weights),
        check_vma=False,
    )
```

```python
import functools

import jax
import jax.numpy as jnp
import numpy as np
from jax import lax
from jax.experimental import pallas as pl
from jax.experimental.pallas import tpu as pltpu
from jax.sharding import Mesh, PartitionSpec as P

H = 16
HD = 64
HALF = HD // 2
LANES = 128
PACK = 16
BF = jnp.bfloat16
F32 = jnp.float32
SWAP = ((0, 1), (1, 0))
MIB = 1 << 20
BLOCKS = ((0, 1, 2, 3), (1, 0, 3, 2), (2, 3, 0, 1), (3, 2, 1, 0))


def dot(left, right):
    return jnp.dot(left, right, preferred_element_type=F32)


def dot_rt(left, right):
    return lax.dot_general(left, right, (((1,), (1,)), ((), ())), preferred_element_type=F32)


def dot_lt(left, right):
    return lax.dot_general(left, right, (((0,), (0,)), ((), ())), preferred_element_type=F32)


def norm_rows(values):
    centre = values - jnp.mean(values, axis=-1, keepdims=True)
    inverse = lax.rsqrt(jnp.mean(centre * centre, axis=-1, keepdims=True) + 1e-05)
    return (centre * inverse, inverse)


def norm_back(normed, inverse, upstream):
    return inverse * (
        upstream
        - jnp.mean(upstream, axis=-1, keepdims=True)
        - normed * jnp.mean(upstream * normed, axis=-1, keepdims=True)
    )


def across(value):
    return lax.ppermute(value, "rep", SWAP)


def sibling(value):
    return lax.ppermute(value, "core", SWAP)


def order_of(size):
    return list(range(0, size, 2)) + list(range(size - 1, 0, -2))


def scalar_table(size):
    order = order_of(size)
    place = np.argsort(order)
    table = np.zeros((2, size, 2, 2 * size + 5), np.int32)
    for rep in range(2):
        for g in range(size):
            for core in range(2):
                at = [order[(place[g] + k) % size] for k in range(size)]
                of = [(place[o] - place[g]) % size for o in range(size)]
                members = [2 * core + rep, 2 * (1 - core) + rep, 2 * core + 1 - rep, 2 * (1 - core) + 1 - rep]
                table[rep, g, core] = at + of + [core] + members
    return table


def upper_half(rows):
    return -(-(rows // 2) // PACK) * PACK


class Ring:
    def __init__(self, size):
        self.size = size
        self.half = size // 2
        order = order_of(size)
        self.right = [(order[i], order[(i + 1) % size]) for i in range(size)]
        self.left = [(b, a) for a, b in self.right]

    def exchange(self, pair):
        return lax.ppermute(pair[0], "ring", self.right), lax.ppermute(pair[1], "ring", self.left)


class Gather:
    def __init__(self, ring, chunk):
        self.ring = ring
        self.step = 0
        self.got = {0: chunk}
        self.cut = upper_half(chunk.shape[0])
        self.state = (chunk, chunk)

    def advance(self):
        if self.step == self.ring.half:
            return
        self.step += 1
        if self.step == self.ring.half:
            self.far = self.ring.exchange((self.state[0][: self.cut], self.state[1][self.cut :]))
            self.state = ()
            return
        self.state = self.ring.exchange(self.state)
        self.got[self.ring.size - self.step], self.got[self.step] = self.state

    def finish(self):
        while self.step < self.ring.half:
            self.advance()
        return [self.got[k] for k in range(self.ring.size) if k != self.ring.half] + list(self.far)


def ring_add(cut, right_term, left_term, right_got, left_got, right_ref, left_ref):
    if cut is None:
        right_ref[...] = (right_term[...].astype(F32) + right_got[...].astype(F32)).astype(BF)
        left_ref[...] = (left_term[...].astype(F32) + left_got[...].astype(F32)).astype(BF)
    else:
        right_ref[:cut] = (right_term[:cut].astype(F32) + right_got[...].astype(F32)).astype(BF)
        right_ref[cut:] = right_term[cut:]
        left_ref[:cut] = left_term[:cut]
        left_ref[cut:] = (left_term[cut:].astype(F32) + left_got[...].astype(F32)).astype(BF)


class Scatter:
    def __init__(self, ring, parts):
        self.ring = ring
        self.step = 0
        self.parts = parts
        self.cut = upper_half(parts[0].shape[0])
        far = parts[ring.half]
        self.state = (far[: self.cut], far[self.cut :])

    def send(self):
        self.got = self.ring.exchange(self.state)

    def add(self):
        ring = self.ring
        self.step += 1
        place = ring.half - self.step
        terms = (self.parts[place], self.parts[ring.size - place])
        body = functools.partial(ring_add, self.cut if self.step == 1 else None)
        self.state = tuple(call(body, [shape(t.shape, BF) for t in terms], [], 0, *terms, *self.got, smem=0))

    def run(self):
        while self.step < self.ring.half - 1:
            self.add()
            self.send()
        return self.parts[0], *self.got


def sync(*values):
    return lax.optimization_barrier(values)


def call(body, outs, scratch, flops, *args, smem=1):
    nbytes = sum(a.size * a.dtype.itemsize for a in args) + sum(o.size * o.dtype.itemsize for o in outs)
    return pl.pallas_call(
        body,
        name=body.func.__name__,
        out_shape=outs,
        in_specs=[pl.BlockSpec(memory_space=pltpu.SMEM)] * smem + [pl.BlockSpec(memory_space=pltpu.VMEM)] * (len(args) - smem),
        out_specs=[pl.BlockSpec(memory_space=pltpu.VMEM)] * len(outs),
        scratch_shapes=scratch,
        compiler_params=pltpu.CompilerParams(vmem_limit_bytes=12 * MIB),
        cost_estimate=pl.CostEstimate(flops=flops, bytes_accessed=nbytes, transcendentals=0),
    )(*args)


def shape(dims, dtype):
    return jax.ShapeDtypeStruct(dims, dtype)


def lanes(start, size):
    return pl.ds(pl.multiple_of(start, LANES), size)


def pack_tokens(rows, prefix_ref, tokens_ref, own_ref):
    own_ref[:rows, :] = tokens_ref[...]
    for m in range(own_ref.shape[0] - rows):
        own_ref[rows + m : rows + m + 1, :] = jnp.broadcast_to(prefix_ref[m : m + 1, :].astype(F32), (1, own_ref.shape[1])).astype(BF)


def pack_first(size, width, scal, qkv_ref, out_ref, own_ref, sib_ref):
    quarter = width // 4
    for ref, member in ((own_ref, scal[2 * size + 1]), (sib_ref, scal[2 * size + 2])):
        for j in range(3):
            ref[:, j * quarter : (j + 1) * quarter] = qkv_ref[:, lanes(j * width + member * quarter, quarter)]
        ref[:, 3 * quarter :] = out_ref[:, lanes(member * quarter, quarter)]


def pack_in(size, units, piece, padded, scal, in_ref, down_ref, own_ref, sib_ref, rows_ref):
    rep = scal[2 * size + 1] - 2 * scal[2 * size]
    for r in range(2):

        @pl.when(rep == r)
        def _(r=r):
            rows_ref[...] = down_ref[r * piece : (r + 1) * piece, :]

    for ref, member in ((own_ref, scal[2 * size + 1]), (sib_ref, scal[2 * size + 2])):
        ref[...] = jnp.zeros_like(ref)
        for q in range(4):

            @pl.when(member == q)
            def _(ref=ref, q=q):
                for part in range(2):
                    for g in range(size):
                        start = part * units + (g * 4 + q) * piece
                        to = (part * size + g) * padded
                        ref[:, to : to + piece] = in_ref[:, start : start + piece]


def place_chunks(size, scal, chunk_refs, store):
    half = size // 2
    places = [k for k in range(size) if k != half]
    for k, ref in zip(places, chunk_refs, strict=False):
        store(scal[k], 0, ref[...])
    top, bottom = chunk_refs[-2:]
    store(scal[half], 0, top[...])
    store(scal[half], top.shape[0], bottom[...])


def place_rows(size, shard_rows, scal, chunk_refs, put):
    core = scal[2 * size]

    def store(chip, first, value):
        for lower in range(2):
            begin = lower * shard_rows - first
            if begin < 0 or begin >= value.shape[0]:
                continue
            row = chip * (2 * shard_rows) + (core if lower == 0 else 1 - core) * shard_rows
            put(pl.multiple_of(row, PACK), value[begin : begin + shard_rows])

    place_chunks(size, scal, chunk_refs, store)


def turned(values):
    lane = lax.broadcasted_iota(jnp.int32, values.shape, 1) % HD
    wide = values.shape[1]
    return jnp.where(lane < HALF, pltpu.roll(values, wide - HALF, 1), pltpu.roll(values, HALF, 1))


def visible(rows, length, limits):
    query = lax.broadcasted_iota(jnp.int32, (rows, rows), 0)
    key = lax.broadcasted_iota(jnp.int32, (rows, rows), 1)
    inside = (key % length).astype(F32)
    limit = jnp.zeros((rows, rows), F32)
    for s in range(rows // length):
        limit = jnp.where(key // length == s, limits[s : s + 1, :rows].astype(F32), limit)
    return (query // length == key // length) & ((key <= query) | (inside < limit))


def gather_out(size, shard_rows, quarter, scal, *refs):
    out_ref = refs[-1]

    def put(row, value):
        out_ref[pl.ds(row, shard_rows), :] = value[:, 3 * quarter :]

    place_rows(size, shard_rows, scal, refs[:-1], put)


def attention(size, shard_rows, rows, length, width, n_chunks, scal, *refs):
    blocks = refs[:4]
    chunks = refs[4 : 4 + n_chunks]
    cos_ref, sin_ref, o_ref, h1_ref, qkv_ref, p_ref, w_ref = refs[4 + n_chunks :]
    quarter = width // 4

    def put(row, value):
        w_ref[pl.ds(row, shard_rows), :] = value[:, : 3 * quarter]

    place_rows(size, shard_rows, scal, chunks, put)
    for b in range(4):
        normed, _ = norm_rows(blocks[b][:rows, :].astype(F32))
        h1_ref[b * rows : (b + 1) * rows, :] = normed.astype(BF)
    for j in range(3):
        mixed = dot(h1_ref[...], w_ref[:, j * quarter : (j + 1) * quarter])
        for b in range(4):
            piece = mixed[b * rows : (b + 1) * rows, :]
            if j < 2:
                piece = piece * cos_ref[...] + turned(piece) * sin_ref[...]
            qkv_ref[b * rows : (b + 1) * rows, j * quarter : (j + 1) * quarter] = piece.astype(BF)
    for b in range(4):
        allowed = visible(rows, length, blocks[b][rows:, :])
        block = slice(b * rows, (b + 1) * rows)
        for h in range(quarter // HD):
            query = qkv_ref[block, h * HD : (h + 1) * HD]
            keys = qkv_ref[block, quarter + h * HD : quarter + (h + 1) * HD]
            values = qkv_ref[block, 2 * quarter + h * HD : 2 * quarter + (h + 1) * HD]
            scores = jnp.where(allowed, dot_rt(query, keys) * HD ** (-0.5), -1e30)
            expo = jnp.exp(scores - jnp.max(scores, axis=-1, keepdims=True))
            probs = expo / jnp.sum(expo, axis=-1, keepdims=True)
            p_ref[b * (quarter // HD) + h] = probs
            o_ref[b, :, h * HD : (h + 1) * HD] = dot(probs.astype(BF), values).astype(BF)


def middle(size, rows, width, scal, *refs):
    blocks = refs[:4]
    o_own, o_far, w_own, w_far, near_ref = refs[4:9]
    full = 4 * rows
    outputs = (
        lambda b: o_own[b],
        lambda b: near_ref[b * rows : (b + 1) * rows],
        lambda b: o_far[b],
        lambda b: near_ref[full + b * rows : full + (b + 1) * rows],
    )
    weights = (w_own, near_ref.at[2 * full : 2 * full + width], w_far, near_ref.at[2 * full + width :])
    x2_ref, h2_ref, o_ref, rows_ref, w_full = refs[9:]
    quarter = width // 4
    members = [scal[2 * size + 1 + m] for m in range(4)]
    for m in range(4):
        w_full[:, lanes(members[m] * quarter, quarter)] = weights[m][...]
        for b in range(4):
            o_ref[b * rows : (b + 1) * rows, lanes(members[m] * quarter, quarter)] = outputs[m](BLOCKS[m][b])
    rows_ref[...] = w_full[pl.ds(pl.multiple_of(members[0] * quarter, quarter), quarter), :]
    for j in range(4):
        columns = slice(j * quarter, (j + 1) * quarter)
        added = dot(o_ref[...], w_full[:, columns])
        for b in range(4):
            x2_ref[b * rows : (b + 1) * rows, columns] = blocks[b][:rows, columns].astype(F32) + added[b * rows : (b + 1) * rows, :]
    for b in range(4):
        block = slice(b * rows, (b + 1) * rows)
        normed, _ = norm_rows(x2_ref[block, :])
        h2_ref[block, :] = normed.astype(BF)


def hidden_units(size, shard_rows, members_units, n_chunks, scal, h2_ref, *refs):
    chunks = refs[:n_chunks]
    up_ref, gate_ref, hid_ref, w_ref = refs[n_chunks:]

    def put(row, value):
        w_ref[pl.ds(row, shard_rows), :] = value

    place_rows(size, shard_rows, scal, chunks, put)
    tile = 256

    @pl.loop(0, members_units // tile)
    def _(i):
        at = pl.multiple_of(i * tile, tile)
        up = dot(h2_ref[...], w_ref[:, pl.ds(at, tile)])
        gate = dot(h2_ref[...], w_ref[:, pl.ds(members_units + at, tile)])
        up_ref[:, pl.ds(at, tile)] = up
        gate_ref[:, pl.ds(at, tile)] = gate
        hid_ref[:, pl.ds(at, tile)] = (gate * jax.nn.sigmoid(gate) * up).astype(BF)


def hidden_back(size, rows, padded, piece, n_chunks, scal, *refs):
    gm_ref = refs[0]
    chunks = refs[1 : 1 + n_chunks]
    up_ref, gate_ref, w_in, ggu_ref, keep_ref, give_ref, down_ref = refs[1 + n_chunks :]
    units = up_ref.shape[1]
    width = gm_ref.shape[1]
    down_ref[...] = jnp.zeros_like(down_ref)

    def store(chip, first, value):
        down_ref[pl.ds(pl.multiple_of(chip * padded + first, PACK), value.shape[0]), :] = value

    place_chunks(size, scal, chunks, store)
    tile = 256

    @pl.loop(0, units // tile)
    def _(i):
        at = pl.multiple_of(i * tile, tile)
        grad = dot_rt(gm_ref[...], down_ref[pl.ds(at, tile), :])
        up = up_ref[:, pl.ds(at, tile)]
        gate = gate_ref[:, pl.ds(at, tile)]
        sig = jax.nn.sigmoid(gate)
        ggu_ref[:, pl.ds(at, tile)] = (grad * (gate * sig)).astype(BF)
        ggu_ref[:, pl.ds(units + at, tile)] = (grad * up * (sig * (1.0 + gate * (1.0 - sig)))).astype(BF)

    @pl.loop(0, width // tile)
    def _(i):
        at = pl.multiple_of(i * tile, tile)
        back = dot_rt(ggu_ref[...], w_in[pl.ds(at, tile), :])
        share(back, rows, keep_ref, give_ref, pl.ds(at, tile))


def share(partial, rows, keep_ref, give_ref, columns):
    keep_ref[0, :, columns] = partial[:rows]
    give_ref[0, :, columns] = partial[rows : 2 * rows].astype(BF)
    keep_ref[1, :, columns] = partial[2 * rows : 3 * rows]
    give_ref[1, :, columns] = partial[3 * rows :].astype(BF)


def last_projection(rows, scal, hid_ref, down_ref, keep_ref, give_ref):
    tile = 256

    @pl.loop(0, down_ref.shape[1] // tile)
    def _(i):
        columns = pl.ds(pl.multiple_of(i * tile, tile), tile)
        share(dot(hid_ref[...], down_ref[:, columns]), rows, keep_ref, give_ref, columns)


def write_parts(size, stride, scal, total, refs):
    for k, ref in enumerate(refs):
        ref[...] = total[pl.ds(pl.multiple_of(scal[k] * stride, PACK), ref.shape[0]), :].astype(BF)


def grad_down_parts(size, rows, padded, scal, hid_ref, *refs):
    gm_ref, total = refs[-2:]
    for b in range(4):
        gm_ref[b * rows : (b + 1) * rows, :] = refs[b][...]
    tile = 256

    @pl.loop(0, gm_ref.shape[1] // tile)
    def _(i):
        columns = pl.ds(pl.multiple_of(i * tile, tile), tile)
        total[:, columns] = dot_lt(hid_ref[...], gm_ref[:, columns])

    write_parts(size, padded, scal, total, refs[4:-2])


def grad_in_parts(size, double, scal, h2_ref, ggu_ref, *refs):
    total = refs[-1]
    tile = 256

    @pl.loop(0, ggu_ref.shape[1] // tile)
    def _(i):
        columns = pl.ds(pl.multiple_of(i * tile, tile), tile)
        total[:, columns] = dot_lt(h2_ref[...], ggu_ref[:, columns])

    write_parts(size, double, scal, total, refs[:-1])


def middle_back(rows, scal, keep_ref, got_ref, far_first, far_second, x2_ref, cot_own, cot_far, gx2_ref, ga_ref):
    for i, cot in ((0, cot_own), (1, cot_far)):
        upstream = keep_ref[i] + got_ref[i].astype(F32) + (far_second, far_first)[i][...].astype(F32)
        normed, inverse = norm_rows(x2_ref[2 * i * rows : (2 * i + 1) * rows, :])
        total = cot[...].astype(F32) + norm_back(normed, inverse, upstream)
        if i == 0:
            gx2_ref[...] = total
        ga_ref[i] = total.astype(BF)


def attention_back(rows, width, scal, ga_own, ga_near, out_rows, qkv_ref, p_ref, w_ref, cos_ref, sin_ref, gqkv_ref, ga_ref, keep_ref, give_ref, go_ref, grad_ref):
    quarter = width // 4
    for b, value in enumerate((ga_own[0], ga_near[0], ga_own[1], ga_near[1])):
        ga_ref[b * rows : (b + 1) * rows, :] = value
    go_ref[...] = dot_rt(ga_ref[...], out_rows[...]).astype(BF)
    for b in range(4):
        block = slice(b * rows, (b + 1) * rows)
        for h in range(quarter // HD):
            head = slice(h * HD, (h + 1) * HD)
            query = qkv_ref[block, h * HD : (h + 1) * HD]
            keys = qkv_ref[block, quarter + h * HD : quarter + (h + 1) * HD]
            values = qkv_ref[block, 2 * quarter + h * HD : 2 * quarter + (h + 1) * HD]
            probs = p_ref[b * (quarter // HD) + h]
            go = go_ref[block, head]
            dprob = dot_rt(go, values)
            centre = jnp.sum(probs * dprob, axis=-1, keepdims=True)
            dscore = (probs * (dprob - centre)).astype(BF)
            grad_ref[0, :, head] = dot(dscore, keys) * HD ** (-0.5)
            grad_ref[1, :, head] = dot_lt(dscore, query) * HD ** (-0.5)
            grad_ref[2, :, head] = dot_lt(probs.astype(BF), go)
        for j in range(3):
            grad = grad_ref[j]
            if j < 2:
                grad = grad * cos_ref[...] - turned(grad) * sin_ref[...]
            gqkv_ref[block, j * quarter : (j + 1) * quarter] = grad.astype(BF)
    for j in range(4):
        columns = slice(j * quarter, (j + 1) * quarter)
        share(dot_rt(gqkv_ref[...], w_ref[columns, :]), rows, keep_ref, give_ref, columns)


def grad_first_parts(size, double, width, scal, h1_ref, gqkv_ref, o_ref, ga_ref, *refs):
    total = refs[-1]
    quarter = width // 4
    for j in range(3):
        columns = slice(j * quarter, (j + 1) * quarter)
        total[:, columns] = dot_lt(h1_ref[...], gqkv_ref[:, columns])
    total[:, 3 * quarter :] = dot_lt(o_ref[...], ga_ref[:, lanes(scal[2 * size + 1] * quarter, quarter)])
    write_parts(size, double, scal, total, refs[:-1])


def split_rows(size, scal, own_ref, right_ref, left_ref, keep_ref, give_ref):
    core = scal[2 * size]
    rows = keep_ref.shape[0]
    for ref, first in ((keep_ref, core), (give_ref, 1 - core)):
        here = pl.ds(pl.multiple_of(first * rows, PACK), rows)
        ref[...] = (own_ref[here, :].astype(F32) + right_ref[here, :].astype(F32) + left_ref[here, :].astype(F32)).astype(BF)


def finish_tokens(rows, scal, keep_ref, got_ref, far_ref, block_ref, gx2_ref, out_ref):
    upstream = keep_ref[0] + got_ref[0].astype(F32) + far_ref[...].astype(F32)
    normed, inverse = norm_rows(block_ref[:rows, :].astype(F32))
    out_ref[...] = gx2_ref[...] + norm_back(normed, inverse, upstream)


def unpack_down(size, piece, scal, low_ref, other_ref, out_ref):
    rep = scal[2 * size + 1] - 2 * scal[2 * size]
    for r in range(2):

        @pl.when(rep == r)
        def _(r=r):
            out_ref[r * piece : (r + 1) * piece, :] = low_ref[...].astype(F32)
            out_ref[(1 - r) * piece : (2 - r) * piece, :] = other_ref[...].astype(F32)


def unpack_first(size, width, scal, own_ref, near_ref, far_ref, diagonal_ref, qkv_ref, out_ref):
    quarter = width // 4
    for m, ref in enumerate((own_ref, near_ref, far_ref, diagonal_ref)):
        value = ref[...].astype(F32)
        at = scal[2 * size + 1 + m] * quarter
        for j in range(3):
            qkv_ref[:, lanes(j * width + at, quarter)] = value[:, j * quarter : (j + 1) * quarter]
        out_ref[:, lanes(at, quarter)] = value[:, 3 * quarter :]


def unpack_in(size, units, piece, padded, scal, own_ref, near_ref, far_ref, diagonal_ref, in_ref, held):
    for m, ref in enumerate((own_ref, near_ref, far_ref, diagonal_ref)):
        held[scal[2 * size + 1 + m]] = ref[...].astype(F32)
    for q in range(4):
        for part in range(2):
            for g in range(size):
                start = part * units + (g * 4 + q) * piece
                frm = (part * size + g) * padded
                in_ref[:, start : start + piece] = held[q, :, frm : frm + piece]


def local(tokens, prefix, qkv_weight, out_weight, in_weight, down_weight, cotangent):
    micro, _, length, width = tokens.shape
    rows = micro * length
    size = lax.axis_size("ring")
    ring = Ring(size)
    rep = lax.axis_index("rep")
    core = lax.axis_index("core")
    shard_rows = qkv_weight.shape[0]
    double = 2 * shard_rows
    units = in_weight.shape[1] // 2
    quarter = width // 4
    heads = quarter // HD
    piece = units // (4 * size)
    padded = -(-piece // PACK) * PACK
    while size * padded % 256:
        padded += PACK
    member_units = size * padded
    chunks = size + 1
    table = scalar_table(size)
    scal = lax.dynamic_slice(
        jnp.asarray(table.reshape(-1, table.shape[-1])), ((rep * size + lax.axis_index("ring")) * 2 + core, 0), (1, table.shape[-1])
    )[0]

    position = np.arange(length, dtype=np.float32)[:, None]
    frequency = np.float32(10000.0) ** (-np.arange(0, HD, 2, dtype=np.float32) / np.float32(HD))
    angles = (position * frequency[None, :]).astype(np.float32)
    angles = np.concatenate([angles, angles], axis=-1)
    sign = np.where(np.arange(HD) < HALF, -1.0, 1.0).astype(np.float32)
    cosine = jnp.asarray(np.tile(np.cos(angles), (micro, heads)).astype(np.float32))
    sine = jnp.asarray(np.tile(np.sin(angles) * sign, (micro, heads)).astype(np.float32))

    full_rows = 4 * rows
    pair_low = shape((2, rows, width), BF)
    pair_full = shape((2, rows, width), F32)
    project = 2 * full_rows * width * quarter

    tokens = tokens.reshape(rows, width)
    cot_own = cotangent.reshape(rows, width)
    a_own, a_sib = call(functools.partial(pack_first, size, width), [shape((shard_rows, width), BF)] * 2, [], 0, scal, qkv_weight, out_weight)
    a = Gather(ring, jnp.concatenate([a_own, sibling(a_sib)], axis=0))

    a.state, in_weight = sync(a.state, in_weight)
    a.advance()
    b_own, b_sib, down_rows = call(
        functools.partial(pack_in, size, units, piece, padded),
        [shape((shard_rows, 2 * member_units), BF)] * 2 + [shape((piece, width), BF)],
        [],
        0,
        scal,
        in_weight,
        down_weight,
    )
    b_own, b_sib, tokens = sync(b_own, b_sib, tokens)
    (own,) = call(functools.partial(pack_tokens, rows), [shape((rows + micro, width), BF)], [], 0, prefix, tokens, smem=0)

    a.state, own, b_own, b_sib = sync(a.state, own, b_own, b_sib)
    a.advance()
    far = across(own)
    near = sibling(own)
    b_got = sibling(b_sib)
    b = Gather(ring, jnp.concatenate([b_own, b_got], axis=0))

    a.state, cot_own, far, near, b.state = sync(a.state, cot_own, far, near, b.state)
    a.advance()
    b.advance()
    cot_far = across(cot_own)

    while a.step < ring.half - 1:
        (a.state,) = sync(a.state)
        a.advance()
    a.state, far, cot_own, cot_far, down_rows = sync(a.state, far, cot_own, cot_far, down_rows)
    a_chunks = a.finish()
    diagonal = sibling(far)
    cot_near = sibling(cot_own)
    c = Gather(ring, down_rows)

    a_chunks, b.state, c.state, diagonal, cot_near = sync(a_chunks, b.state, c.state, diagonal, cot_near)
    blocks = [own, near, far, diagonal]
    b.advance()
    c.advance()
    (out_mine,) = call(functools.partial(gather_out, size, shard_rows, quarter), [shape((width, quarter), BF)], [], 0, scal, *a_chunks)
    out_far = across(out_mine)
    o_own, h1, qkv, probs, qkv_mine = call(
        functools.partial(attention, size, shard_rows, rows, length, width, chunks),
        [
            shape((4, rows, quarter), BF),
            shape((full_rows, width), BF),
            shape((full_rows, 3 * quarter), BF),
            shape((4 * heads, rows, rows), F32),
            shape((width, 3 * quarter), BF),
        ],
        [],
        3 * project,
        scal,
        *blocks,
        *a_chunks,
        cosine,
        sine,
    )

    o_own, out_mine, b.state, c.state = sync(o_own, out_mine, b.state, c.state)
    o_far = across(o_own)
    b.advance()
    c.advance()

    o_far, out_far, b.state, c.state = sync(o_far, out_far, b.state, c.state)
    kept = [o_own.reshape(full_rows, quarter), o_far.reshape(full_rows, quarter), out_mine, out_far]
    near_all = sibling(jnp.concatenate(kept, axis=0))
    b_chunks = b.finish()
    c.advance()
    x2, h2, o_all, out_rows = call(
        functools.partial(middle, size, rows, width),
        [
            shape((full_rows, width), F32),
            shape((full_rows, width), BF),
            shape((full_rows, width), BF),
            shape((quarter, width), BF),
        ],
        [pltpu.VMEM((width, width), BF)],
        4 * project,
        scal,
        *blocks,
        o_own,
        o_far,
        out_mine,
        out_far,
        near_all,
    )

    h2, b_chunks, cot_far = sync(h2, b_chunks, cot_far)
    cot_diagonal = sibling(cot_far)
    up, gate, hid, in_mine = call(
        functools.partial(hidden_units, size, shard_rows, member_units, chunks),
        [
            shape((full_rows, member_units), F32),
            shape((full_rows, member_units), F32),
            shape((full_rows, member_units), BF),
            shape((width, 2 * member_units), BF),
        ],
        [],
        6 * project,
        scal,
        h2,
        *b_chunks,
    )
    hid, c.state, cot_diagonal = sync(hid, c.state, cot_diagonal)
    c_chunks = c.finish()
    *down_parts, gm = call(
        functools.partial(grad_down_parts, size, rows, padded),
        [shape((piece, width), BF)] * size + [shape((full_rows, width), BF)],
        [pltpu.VMEM((member_units, width), F32)],
        3 * project,
        scal,
        hid,
        cot_own,
        cot_near,
        cot_far,
        cot_diagonal,
    )

    c = Scatter(ring, down_parts)
    c.state, gm, up, c_chunks = sync(c.state, gm, up, c_chunks)
    c.send()
    ggu, u2_keep, u2_give, down_mine = call(
        functools.partial(hidden_back, size, rows, padded, piece, chunks),
        [shape((full_rows, 2 * member_units), BF), pair_full, pair_low, shape((member_units, width), BF)],
        [],
        9 * project,
        scal,
        gm,
        *c_chunks,
        up,
        gate,
        in_mine,
    )

    u2_give, c.got = sync(u2_give, c.got)
    u2_got = sibling(u2_give)
    c.add()
    c.send()
    u2_low = (u2_keep + u2_got.astype(F32)).astype(BF)

    u2_low, ggu = sync(u2_low, ggu)
    u2_first = across(u2_low[0])
    in_parts = call(
        functools.partial(grad_in_parts, size, double),
        [shape((double, 2 * member_units), BF)] * size,
        [pltpu.VMEM((width, 2 * member_units), F32)],
        6 * project,
        scal,
        h2,
        ggu,
    )

    b = Scatter(ring, in_parts)
    b.state, c.got, u2_first, u2_low, hid = sync(b.state, c.got, u2_first, u2_low, hid)
    b.send()
    c.add()
    c.send()
    u2_second = across(u2_low[1])
    y_keep, y_give = call(functools.partial(last_projection, rows), [pair_full, pair_low], [], 3 * project, scal, hid, down_mine)

    y_give, c.got, b.got, u2_second = sync(y_give, c.got, b.got, u2_second)
    b.add()
    b.send()
    c.add()
    c.send()
    gx2, ga = call(
        functools.partial(middle_back, rows),
        [shape((rows, width), F32), pair_low],
        [],
        0,
        scal,
        u2_keep,
        u2_got,
        u2_first,
        u2_second,
        x2,
        cot_own,
        cot_far,
    )
    ga_near = sibling(ga)
    gqkv, ga_all, u1_keep, u1_give = call(
        functools.partial(attention_back, rows, width),
        [shape((full_rows, 3 * quarter), BF), shape((full_rows, width), BF), pair_full, pair_low],
        [pltpu.VMEM((full_rows, quarter), BF), pltpu.VMEM((3, rows, quarter), F32)],
        7 * project,
        scal,
        ga,
        ga_near,
        out_rows,
        qkv,
        probs,
        qkv_mine,
        cosine,
        sine,
    )

    gqkv, u1_give, b.got, c.got = sync(gqkv, u1_give, b.got, c.got)
    b.add()
    b.send()
    u1_got = sibling(u1_give)
    first_parts = call(
        functools.partial(grad_first_parts, size, double, width),
        [shape((double, width), BF)] * size,
        [pltpu.VMEM((width, width), F32)],
        4 * project,
        scal,
        h1,
        gqkv,
        o_all,
        ga_all,
    )
    down_low = sum(v.astype(F32) for v in c.run()).astype(BF)

    a = Scatter(ring, first_parts)
    a.state, u1_got, down_low = sync(a.state, u1_got, down_low)
    a.send()
    u1_low = (u1_keep[1] + u1_got[1].astype(F32)).astype(BF)
    u1_far = across(u1_low)

    a.got, b.got, u1_far, y_give = sync(a.got, b.got, u1_far, y_give)
    a.add()
    a.send()
    b.add()
    b.send()
    down_other = across(down_low)
    y_got = sibling(y_give)

    while a.step < ring.half - 2:
        a.got, down_other = sync(a.got, down_other)
        a.add()
        a.send()
    y_low = (y_keep[1] + y_got[1].astype(F32)).astype(BF)
    y_far = across(y_low)

    def halves(summed):
        columns = summed[0].shape[1]
        return call(functools.partial(split_rows, size), [shape((shard_rows, columns), BF)] * 2, [], 0, scal, *summed)

    in_keep, in_give = halves(b.run())
    a.got, in_keep, in_give = sync(a.got, in_keep, in_give)
    a.add()
    a.send()
    in_far = across(in_keep)
    in_near = sibling(in_give)
    in_diagonal = across(in_near)
    first_keep, first_give = halves(a.run())
    first_keep, first_give, in_far = sync(first_keep, first_give, in_far)
    first_far = across(first_keep)
    first_near = sibling(first_give)
    first_diagonal = across(first_near)
    u1_far, y_far, down_other, in_near, first_near = sync(u1_far, y_far, down_other, in_near, first_near)
    (grad_tokens,) = call(
        functools.partial(finish_tokens, rows), [shape((rows, width), F32)], [], 0, scal, u1_keep, u1_got, u1_far, own, gx2
    )
    result = (x2[:rows] + (y_keep[0] + y_got[0].astype(F32) + y_far.astype(F32))).astype(BF)
    (grad_down,) = call(functools.partial(unpack_down, size, piece), [shape((2 * piece, width), F32)], [], 0, scal, down_low, down_other)
    (grad_in,) = call(
        functools.partial(unpack_in, size, units, piece, padded),
        [shape((shard_rows, 2 * units), F32)],
        [pltpu.VMEM((4, shard_rows, 2 * member_units), F32)],
        0,
        scal,
        in_keep,
        in_near,
        in_far,
        in_diagonal,
    )
    grad_qkv, grad_out = call(
        functools.partial(unpack_first, size, width),
        [shape((shard_rows, 3 * width), F32), shape((shard_rows, width), F32)],
        [],
        0,
        scal,
        first_keep,
        first_near,
        first_far,
        first_diagonal,
    )
    return (
        result.reshape(micro, 1, length, width),
        grad_tokens.reshape(micro, 1, length, width),
        grad_qkv,
        grad_out,
        grad_in,
        grad_down,
    )


def solution(mesh):
    inner = Mesh(mesh.devices.reshape(mesh.shape["rep"], mesh.shape["shard"] // 2, 2), ("rep", "ring", "core"))
    everyone = ("rep", "ring", "core")
    group = ("ring", "core")
    sequences = P(None, everyone, None, None)
    weights = P(group, None)
    return jax.shard_map(
        local,
        mesh=inner,
        in_specs=(sequences, P(None, everyone), weights, weights, weights, weights, sequences),
        out_specs=(sequences, sequences, weights, weights, weights, weights),
        check_vma=False,
    )
```

```python
import functools

import jax
import jax.numpy as jnp
import numpy as np
from jax import lax
from jax.experimental import pallas as pl
from jax.experimental.pallas import tpu as pltpu
from jax.sharding import Mesh, PartitionSpec as P

H = 16
HD = 64
HALF = HD // 2
LANES = 128
PACK = 16
BF = jnp.bfloat16
F32 = jnp.float32
SWAP = ((0, 1), (1, 0))
MIB = 1 << 20
BLOCKS = ((0, 1, 2, 3), (1, 0, 3, 2), (2, 3, 0, 1), (3, 2, 1, 0))


def dot(left, right):
    return jnp.dot(left, right, preferred_element_type=F32)


def dot_rt(left, right):
    return lax.dot_general(left, right, (((1,), (1,)), ((), ())), preferred_element_type=F32)


def dot_lt(left, right):
    return lax.dot_general(left, right, (((0,), (0,)), ((), ())), preferred_element_type=F32)


def norm_rows(values):
    centre = values - jnp.mean(values, axis=-1, keepdims=True)
    inverse = lax.rsqrt(jnp.mean(centre * centre, axis=-1, keepdims=True) + 1e-05)
    return (centre * inverse, inverse)


def norm_back(normed, inverse, upstream):
    return inverse * (
        upstream
        - jnp.mean(upstream, axis=-1, keepdims=True)
        - normed * jnp.mean(upstream * normed, axis=-1, keepdims=True)
    )


def across(value):
    return lax.ppermute(value, "rep", SWAP)


def sibling(value):
    return lax.ppermute(value, "core", SWAP)


def order_of(size):
    return list(range(0, size, 2)) + list(range(size - 1, 0, -2))


def scalar_table(size):
    order = order_of(size)
    place = np.argsort(order)
    table = np.zeros((2, size, 2, 2 * size + 5), np.int32)
    for rep in range(2):
        for g in range(size):
            for core in range(2):
                at = [order[(place[g] + k) % size] for k in range(size)]
                of = [(place[o] - place[g]) % size for o in range(size)]
                members = [2 * core + rep, 2 * (1 - core) + rep, 2 * core + 1 - rep, 2 * (1 - core) + 1 - rep]
                table[rep, g, core] = at + of + [core] + members
    return table


def upper_half(rows):
    return -(-(rows // 2) // PACK) * PACK


class Ring:
    def __init__(self, size):
        self.size = size
        self.half = size // 2
        order = order_of(size)
        self.right = [(order[i], order[(i + 1) % size]) for i in range(size)]
        self.left = [(b, a) for a, b in self.right]

    def exchange(self, pair):
        return lax.ppermute(pair[0], "ring", self.right), lax.ppermute(pair[1], "ring", self.left)


class Gather:
    def __init__(self, ring, chunk):
        self.ring = ring
        self.step = 0
        self.got = {0: chunk}
        self.cut = upper_half(chunk.shape[0])
        self.state = (chunk, chunk)

    def advance(self):
        if self.step == self.ring.half:
            return
        self.step += 1
        if self.step == self.ring.half:
            self.far = self.ring.exchange((self.state[0][: self.cut], self.state[1][self.cut :]))
            self.state = ()
            return
        self.state = self.ring.exchange(self.state)
        self.got[self.ring.size - self.step], self.got[self.step] = self.state

    def finish(self):
        while self.step < self.ring.half:
            self.advance()
        return [self.got[k] for k in range(self.ring.size) if k != self.ring.half] + list(self.far)


def ring_add(cut, right_term, left_term, right_got, left_got, right_ref, left_ref):
    if cut is None:
        right_ref[...] = (right_term[...].astype(F32) + right_got[...].astype(F32)).astype(BF)
        left_ref[...] = (left_term[...].astype(F32) + left_got[...].astype(F32)).astype(BF)
    else:
        right_ref[:cut] = (right_term[:cut].astype(F32) + right_got[...].astype(F32)).astype(BF)
        right_ref[cut:] = right_term[cut:]
        left_ref[:cut] = left_term[:cut]
        left_ref[cut:] = (left_term[cut:].astype(F32) + left_got[...].astype(F32)).astype(BF)


class Scatter:
    def __init__(self, ring, parts):
        self.ring = ring
        self.step = 0
        self.parts = parts
        self.cut = upper_half(parts[0].shape[0])
        far = parts[ring.half]
        self.state = (far[: self.cut], far[self.cut :])

    def send(self):
        self.got = self.ring.exchange(self.state)

    def add(self):
        ring = self.ring
        self.step += 1
        place = ring.half - self.step
        terms = (self.parts[place], self.parts[ring.size - place])
        body = functools.partial(ring_add, self.cut if self.step == 1 else None)
        self.state = tuple(call(body, [shape(t.shape, BF) for t in terms], [], 16000000000, *terms, *self.got, smem=0))

    def run(self):
        while self.step < self.ring.half - 1:
            self.add()
            self.send()
        return self.parts[0], *self.got


def sync(*values):
    return lax.optimization_barrier(values)


def call(body, outs, scratch, flops, *args, smem=1, still=0):
    nbytes = sum(a.size * a.dtype.itemsize for a in args) + sum(o.size * o.dtype.itemsize for o in outs)
    spaces = [pltpu.SMEM] * smem + [pl.ANY] * still + [pltpu.VMEM] * (len(args) - smem - still)
    return pl.pallas_call(
        body,
        name=body.func.__name__,
        out_shape=outs,
        in_specs=[pl.BlockSpec(memory_space=space) for space in spaces],
        out_specs=[pl.BlockSpec(memory_space=pltpu.VMEM)] * len(outs),
        scratch_shapes=scratch,
        compiler_params=pltpu.CompilerParams(vmem_limit_bytes=12 * MIB),
        cost_estimate=pl.CostEstimate(flops=flops, bytes_accessed=nbytes, transcendentals=0),
    )(*args)


def shape(dims, dtype):
    return jax.ShapeDtypeStruct(dims, dtype)


def lanes(start, size):
    return pl.ds(pl.multiple_of(start, LANES), size)


def pack_tokens(rows, prefix_ref, tokens_ref, own_ref):
    own_ref[:rows, :] = tokens_ref[...]
    for m in range(own_ref.shape[0] - rows):
        own_ref[rows + m : rows + m + 1, :] = jnp.broadcast_to(prefix_ref[m : m + 1, :].astype(F32), (1, own_ref.shape[1])).astype(BF)


def pack_first(size, width, scal, qkv_ref, out_ref, own_ref, sib_ref, sems):
    quarter = width // 4
    copies = []
    for ref, member in ((own_ref, scal[2 * size + 1]), (sib_ref, scal[2 * size + 2])):
        for j in range(4):
            source = qkv_ref.at[:, lanes(j * width + member * quarter, quarter)] if j < 3 else out_ref.at[:, lanes(member * quarter, quarter)]
            copies.append(pltpu.make_async_copy(source, ref.at[:, j * quarter : (j + 1) * quarter], sems.at[len(copies)]))
            copies[-1].start()
    for copy in copies:
        copy.wait()


def pack_in(size, units, piece, padded, scal, in_ref, down_ref, own_ref, sib_ref, rows_ref):
    rep = scal[2 * size + 1] - 2 * scal[2 * size]
    for r in range(2):

        @pl.when(rep == r)
        def _(r=r):
            rows_ref[...] = down_ref[r * piece : (r + 1) * piece, :]

    for ref, member in ((own_ref, scal[2 * size + 1]), (sib_ref, scal[2 * size + 2])):
        ref[...] = jnp.zeros_like(ref)
        for q in range(4):

            @pl.when(member == q)
            def _(ref=ref, q=q):
                for part in range(2):
                    for g in range(size):
                        start = part * units + (g * 4 + q) * piece
                        to = (part * size + g) * padded
                        ref[:, to : to + piece] = in_ref[:, start : start + piece]


def place_chunks(size, scal, chunk_refs, store):
    half = size // 2
    places = [k for k in range(size) if k != half]
    for k, ref in zip(places, chunk_refs, strict=False):
        store(scal[k], 0, ref[...])
    top, bottom = chunk_refs[-2:]
    store(scal[half], 0, top[...])
    store(scal[half], top.shape[0], bottom[...])


def place_rows(size, shard_rows, scal, chunk_refs, put):
    core = scal[2 * size]

    def store(chip, first, value):
        for lower in range(2):
            begin = lower * shard_rows - first
            if begin < 0 or begin >= value.shape[0]:
                continue
            row = chip * (2 * shard_rows) + (core if lower == 0 else 1 - core) * shard_rows
            put(pl.multiple_of(row, PACK), value[begin : begin + shard_rows])

    place_chunks(size, scal, chunk_refs, store)


def turned(values):
    lane = lax.broadcasted_iota(jnp.int32, values.shape, 1) % HD
    wide = values.shape[1]
    return jnp.where(lane < HALF, pltpu.roll(values, wide - HALF, 1), pltpu.roll(values, HALF, 1))


def visible(rows, length, limits):
    query = lax.broadcasted_iota(jnp.int32, (rows, rows), 0)
    key = lax.broadcasted_iota(jnp.int32, (rows, rows), 1)
    inside = (key % length).astype(F32)
    limit = jnp.zeros((rows, rows), F32)
    for s in range(rows // length):
        limit = jnp.where(key // length == s, limits[s : s + 1, :rows].astype(F32), limit)
    return (query // length == key // length) & ((key <= query) | (inside < limit))


def gather_out(size, shard_rows, quarter, scal, *refs):
    out_ref = refs[-1]

    def put(row, value):
        out_ref[pl.ds(row, shard_rows), :] = value[:, 3 * quarter :]

    place_rows(size, shard_rows, scal, refs[:-1], put)


def attention(size, shard_rows, rows, length, width, n_chunks, scal, *refs):
    blocks = refs[:4]
    chunks = refs[4 : 4 + n_chunks]
    cos_ref, sin_ref, o_ref, h1_ref, qkv_ref, p_ref, w_ref = refs[4 + n_chunks :]
    quarter = width // 4

    def put(row, value):
        w_ref[pl.ds(row, shard_rows), :] = value[:, : 3 * quarter]

    place_rows(size, shard_rows, scal, chunks, put)
    for b in range(4):
        normed, _ = norm_rows(blocks[b][:rows, :].astype(F32))
        h1_ref[b * rows : (b + 1) * rows, :] = normed.astype(BF)
    for j in range(3):
        mixed = dot(h1_ref[...], w_ref[:, j * quarter : (j + 1) * quarter])
        for b in range(4):
            piece = mixed[b * rows : (b + 1) * rows, :]
            if j < 2:
                piece = piece * cos_ref[...] + turned(piece) * sin_ref[...]
            qkv_ref[b * rows : (b + 1) * rows, j * quarter : (j + 1) * quarter] = piece.astype(BF)
    for b in range(4):
        allowed = visible(rows, length, blocks[b][rows:, :])
        block = slice(b * rows, (b + 1) * rows)
        for h in range(quarter // HD):
            query = qkv_ref[block, h * HD : (h + 1) * HD]
            keys = qkv_ref[block, quarter + h * HD : quarter + (h + 1) * HD]
            values = qkv_ref[block, 2 * quarter + h * HD : 2 * quarter + (h + 1) * HD]
            scores = jnp.where(allowed, dot_rt(query, keys) * HD ** (-0.5), -1e30)
            expo = jnp.exp(scores - jnp.max(scores, axis=-1, keepdims=True))
            probs = expo / jnp.sum(expo, axis=-1, keepdims=True)
            p_ref[b * (quarter // HD) + h] = probs
            o_ref[b, :, h * HD : (h + 1) * HD] = dot(probs.astype(BF), values).astype(BF)


def middle(size, rows, width, scal, *refs):
    blocks = refs[:4]
    o_own, o_far, w_own, w_far, near_ref = refs[4:9]
    full = 4 * rows
    outputs = (
        lambda b: o_own[b],
        lambda b: near_ref[b * rows : (b + 1) * rows],
        lambda b: o_far[b],
        lambda b: near_ref[full + b * rows : full + (b + 1) * rows],
    )
    weights = (w_own, near_ref.at[2 * full : 2 * full + width], w_far, near_ref.at[2 * full + width :])
    x2_ref, h2_ref, o_ref, rows_ref, w_full = refs[9:]
    quarter = width // 4
    members = [scal[2 * size + 1 + m] for m in range(4)]
    for m in range(4):
        w_full[:, lanes(members[m] * quarter, quarter)] = weights[m][...]
        for b in range(4):
            o_ref[b * rows : (b + 1) * rows, lanes(members[m] * quarter, quarter)] = outputs[m](BLOCKS[m][b])
    rows_ref[...] = w_full[pl.ds(pl.multiple_of(members[0] * quarter, quarter), quarter), :]
    for j in range(4):
        columns = slice(j * quarter, (j + 1) * quarter)
        added = dot(o_ref[...], w_full[:, columns])
        for b in range(4):
            x2_ref[b * rows : (b + 1) * rows, columns] = blocks[b][:rows, columns].astype(F32) + added[b * rows : (b + 1) * rows, :]
    for b in range(4):
        block = slice(b * rows, (b + 1) * rows)
        normed, _ = norm_rows(x2_ref[block, :])
        h2_ref[block, :] = normed.astype(BF)


def hidden_units(size, shard_rows, members_units, n_chunks, scal, h2_ref, *refs):
    chunks = refs[:n_chunks]
    up_ref, gate_ref, hid_ref, w_ref = refs[n_chunks:]

    def put(row, value):
        w_ref[pl.ds(row, shard_rows), :] = value

    place_rows(size, shard_rows, scal, chunks, put)
    tile = 256

    @pl.loop(0, members_units // tile)
    def _(i):
        at = pl.multiple_of(i * tile, tile)
        up = dot(h2_ref[...], w_ref[:, pl.ds(at, tile)])
        gate = dot(h2_ref[...], w_ref[:, pl.ds(members_units + at, tile)])
        up_ref[:, pl.ds(at, tile)] = up
        gate_ref[:, pl.ds(at, tile)] = gate
        hid_ref[:, pl.ds(at, tile)] = (gate * jax.nn.sigmoid(gate) * up).astype(BF)


def hidden_back(size, rows, padded, piece, n_chunks, scal, *refs):
    gm_ref = refs[0]
    chunks = refs[1 : 1 + n_chunks]
    up_ref, gate_ref, w_in, ggu_ref, keep_ref, give_ref, down_ref = refs[1 + n_chunks :]
    units = up_ref.shape[1]
    width = gm_ref.shape[1]
    down_ref[...] = jnp.zeros_like(down_ref)

    def store(chip, first, value):
        down_ref[pl.ds(pl.multiple_of(chip * padded + first, PACK), value.shape[0]), :] = value

    place_chunks(size, scal, chunks, store)
    tile = 256

    @pl.loop(0, units // tile)
    def _(i):
        at = pl.multiple_of(i * tile, tile)
        grad = dot_rt(gm_ref[...], down_ref[pl.ds(at, tile), :])
        up = up_ref[:, pl.ds(at, tile)]
        gate = gate_ref[:, pl.ds(at, tile)]
        sig = jax.nn.sigmoid(gate)
        ggu_ref[:, pl.ds(at, tile)] = (grad * (gate * sig)).astype(BF)
        ggu_ref[:, pl.ds(units + at, tile)] = (grad * up * (sig * (1.0 + gate * (1.0 - sig)))).astype(BF)

    @pl.loop(0, width // tile)
    def _(i):
        at = pl.multiple_of(i * tile, tile)
        back = dot_rt(ggu_ref[...], w_in[pl.ds(at, tile), :])
        share(back, rows, keep_ref, give_ref, pl.ds(at, tile))


def share(partial, rows, keep_ref, give_ref, columns):
    keep_ref[0, :, columns] = partial[:rows]
    give_ref[0, :, columns] = partial[rows : 2 * rows].astype(BF)
    keep_ref[1, :, columns] = partial[2 * rows : 3 * rows]
    give_ref[1, :, columns] = partial[3 * rows :].astype(BF)


def last_projection(rows, scal, hid_ref, down_ref, keep_ref, give_ref):
    tile = 256

    @pl.loop(0, down_ref.shape[1] // tile)
    def _(i):
        columns = pl.ds(pl.multiple_of(i * tile, tile), tile)
        share(dot(hid_ref[...], down_ref[:, columns]), rows, keep_ref, give_ref, columns)


def write_parts(size, stride, scal, total, refs):
    for k, ref in enumerate(refs):
        ref[...] = total[pl.ds(pl.multiple_of(scal[k] * stride, PACK), ref.shape[0]), :].astype(BF)


def grad_down_parts(size, rows, padded, scal, hid_ref, *refs):
    gm_ref, total = refs[-2:]
    for b in range(4):
        gm_ref[b * rows : (b + 1) * rows, :] = refs[b][...]
    tile = 256

    @pl.loop(0, gm_ref.shape[1] // tile)
    def _(i):
        columns = pl.ds(pl.multiple_of(i * tile, tile), tile)
        total[:, columns] = dot_lt(hid_ref[...], gm_ref[:, columns])

    write_parts(size, padded, scal, total, refs[4:-2])


def grad_in_parts(size, double, scal, h2_ref, ggu_ref, *refs):
    total = refs[-1]
    tile = 256

    @pl.loop(0, ggu_ref.shape[1] // tile)
    def _(i):
        columns = pl.ds(pl.multiple_of(i * tile, tile), tile)
        total[:, columns] = dot_lt(h2_ref[...], ggu_ref[:, columns])

    write_parts(size, double, scal, total, refs[:-1])


def middle_back(rows, scal, keep_ref, got_ref, far_first, far_second, x2_ref, cot_own, cot_far, gx2_ref, ga_ref):
    for i, cot in ((0, cot_own), (1, cot_far)):
        upstream = keep_ref[i] + got_ref[i].astype(F32) + (far_second, far_first)[i][...].astype(F32)
        normed, inverse = norm_rows(x2_ref[2 * i * rows : (2 * i + 1) * rows, :])
        total = cot[...].astype(F32) + norm_back(normed, inverse, upstream)
        if i == 0:
            gx2_ref[...] = total
        ga_ref[i] = total.astype(BF)


def attention_back(rows, width, scal, ga_own, ga_near, out_rows, qkv_ref, p_ref, w_ref, cos_ref, sin_ref, gqkv_ref, ga_ref, keep_ref, give_ref, go_ref, grad_ref):
    quarter = width // 4
    for b, value in enumerate((ga_own[0], ga_near[0], ga_own[1], ga_near[1])):
        ga_ref[b * rows : (b + 1) * rows, :] = value
    go_ref[...] = dot_rt(ga_ref[...], out_rows[...]).astype(BF)
    for b in range(4):
        block = slice(b * rows, (b + 1) * rows)
        for h in range(quarter // HD):
            head = slice(h * HD, (h + 1) * HD)
            query = qkv_ref[block, h * HD : (h + 1) * HD]
            keys = qkv_ref[block, quarter + h * HD : quarter + (h + 1) * HD]
            values = qkv_ref[block, 2 * quarter + h * HD : 2 * quarter + (h + 1) * HD]
            probs = p_ref[b * (quarter // HD) + h]
            go = go_ref[block, head]
            dprob = dot_rt(go, values)
            centre = jnp.sum(probs * dprob, axis=-1, keepdims=True)
            dscore = (probs * (dprob - centre)).astype(BF)
            grad_ref[0, :, head] = dot(dscore, keys) * HD ** (-0.5)
            grad_ref[1, :, head] = dot_lt(dscore, query) * HD ** (-0.5)
            grad_ref[2, :, head] = dot_lt(probs.astype(BF), go)
        for j in range(3):
            grad = grad_ref[j]
            if j < 2:
                grad = grad * cos_ref[...] - turned(grad) * sin_ref[...]
            gqkv_ref[block, j * quarter : (j + 1) * quarter] = grad.astype(BF)
    for j in range(4):
        columns = slice(j * quarter, (j + 1) * quarter)
        share(dot_rt(gqkv_ref[...], w_ref[columns, :]), rows, keep_ref, give_ref, columns)


def grad_first_parts(size, double, width, scal, h1_ref, gqkv_ref, o_ref, ga_ref, *refs):
    total = refs[-1]
    quarter = width // 4
    for j in range(3):
        columns = slice(j * quarter, (j + 1) * quarter)
        total[:, columns] = dot_lt(h1_ref[...], gqkv_ref[:, columns])
    total[:, 3 * quarter :] = dot_lt(o_ref[...], ga_ref[:, lanes(scal[2 * size + 1] * quarter, quarter)])
    write_parts(size, double, scal, total, refs[:-1])


def split_rows(size, scal, own_ref, right_ref, left_ref, keep_ref, give_ref):
    core = scal[2 * size]
    rows = keep_ref.shape[0]
    for ref, first in ((keep_ref, core), (give_ref, 1 - core)):
        here = pl.ds(pl.multiple_of(first * rows, PACK), rows)
        ref[...] = (own_ref[here, :].astype(F32) + right_ref[here, :].astype(F32) + left_ref[here, :].astype(F32)).astype(BF)


def finish_tokens(rows, scal, keep_ref, got_ref, far_ref, block_ref, gx2_ref, out_ref):
    upstream = keep_ref[0] + got_ref[0].astype(F32) + far_ref[...].astype(F32)
    normed, inverse = norm_rows(block_ref[:rows, :].astype(F32))
    out_ref[...] = gx2_ref[...] + norm_back(normed, inverse, upstream)


def unpack_down(size, piece, scal, low_ref, other_ref, out_ref):
    rep = scal[2 * size + 1] - 2 * scal[2 * size]
    for r in range(2):

        @pl.when(rep == r)
        def _(r=r):
            out_ref[r * piece : (r + 1) * piece, :] = low_ref[...].astype(F32)
            out_ref[(1 - r) * piece : (2 - r) * piece, :] = other_ref[...].astype(F32)


def unpack_first(size, width, scal, own_ref, near_ref, far_ref, diagonal_ref, qkv_ref, out_ref):
    quarter = width // 4
    for m, ref in enumerate((own_ref, near_ref, far_ref, diagonal_ref)):
        value = ref[...].astype(F32)
        at = scal[2 * size + 1 + m] * quarter
        for j in range(3):
            qkv_ref[:, lanes(j * width + at, quarter)] = value[:, j * quarter : (j + 1) * quarter]
        out_ref[:, lanes(at, quarter)] = value[:, 3 * quarter :]


def unpack_in(size, units, piece, padded, scal, own_ref, near_ref, far_ref, diagonal_ref, in_ref, held):
    for m, ref in enumerate((own_ref, near_ref, far_ref, diagonal_ref)):
        held[scal[2 * size + 1 + m]] = ref[...].astype(F32)
    for q in range(4):
        for part in range(2):
            for g in range(size):
                start = part * units + (g * 4 + q) * piece
                frm = (part * size + g) * padded
                in_ref[:, start : start + piece] = held[q, :, frm : frm + piece]


def local(tokens, prefix, qkv_weight, out_weight, in_weight, down_weight, cotangent):
    micro, _, length, width = tokens.shape
    rows = micro * length
    size = lax.axis_size("ring")
    ring = Ring(size)
    rep = lax.axis_index("rep")
    core = lax.axis_index("core")
    shard_rows = qkv_weight.shape[0]
    double = 2 * shard_rows
    units = in_weight.shape[1] // 2
    quarter = width // 4
    heads = quarter // HD
    piece = units // (4 * size)
    padded = -(-piece // PACK) * PACK
    while size * padded % 256:
        padded += PACK
    member_units = size * padded
    chunks = size + 1
    table = scalar_table(size)
    scal = lax.dynamic_slice(
        jnp.asarray(table.reshape(-1, table.shape[-1])), ((rep * size + lax.axis_index("ring")) * 2 + core, 0), (1, table.shape[-1])
    )[0]

    position = np.arange(length, dtype=np.float32)[:, None]
    frequency = np.float32(10000.0) ** (-np.arange(0, HD, 2, dtype=np.float32) / np.float32(HD))
    angles = (position * frequency[None, :]).astype(np.float32)
    angles = np.concatenate([angles, angles], axis=-1)
    sign = np.where(np.arange(HD) < HALF, -1.0, 1.0).astype(np.float32)
    cosine = jnp.asarray(np.tile(np.cos(angles), (micro, heads)).astype(np.float32))
    sine = jnp.asarray(np.tile(np.sin(angles) * sign, (micro, heads)).astype(np.float32))

    full_rows = 4 * rows
    pair_low = shape((2, rows, width), BF)
    pair_full = shape((2, rows, width), F32)
    project = 2 * full_rows * width * quarter

    tokens = tokens.reshape(rows, width)
    cot_own = cotangent.reshape(rows, width)
    a_own, a_sib = call(
        functools.partial(pack_first, size, width),
        [shape((shard_rows, width), BF)] * 2,
        [pltpu.SemaphoreType.DMA((8,))],
        0,
        scal,
        qkv_weight,
        out_weight,
        still=2,
    )
    a = Gather(ring, jnp.concatenate([a_own, sibling(a_sib)], axis=0))

    a.state, in_weight, tokens, cot_own = sync(a.state, in_weight, tokens, cot_own)
    a.advance()
    b_own, b_sib, down_rows = call(
        functools.partial(pack_in, size, units, piece, padded),
        [shape((shard_rows, 2 * member_units), BF)] * 2 + [shape((piece, width), BF)],
        [],
        0,
        scal,
        in_weight,
        down_weight,
    )
    c = Gather(ring, down_rows)
    c.advance()
    b_got = sibling(b_sib)
    (own,) = call(functools.partial(pack_tokens, rows), [shape((rows + micro, width), BF)], [], 0, prefix, tokens, smem=0)
    near = sibling(own)
    cot_near = sibling(cot_own)

    a.state, own, b_own, b_got, near, cot_near = sync(a.state, own, b_own, b_got, near, cot_near)
    a.advance()
    far = across(own)
    b = Gather(ring, jnp.concatenate([b_own, b_got], axis=0))

    (a.state,) = sync(a.state)
    a.advance()
    far, cot_own, b.state, c.state = sync(far, cot_own, b.state, c.state)
    cot_far = across(cot_own)
    b.advance()

    while a.step < ring.half - 1:
        (a.state,) = sync(a.state)
        a.advance()
    a.state, far, cot_far = sync(a.state, far, cot_far)
    a_chunks = a.finish()
    diagonal = sibling(far)

    a_chunks, b.state, c.state, diagonal = sync(a_chunks, b.state, c.state, diagonal)
    blocks = [own, near, far, diagonal]
    b.advance()
    c.advance()
    (out_mine,) = call(functools.partial(gather_out, size, shard_rows, quarter), [shape((width, quarter), BF)], [], 0, scal, *a_chunks)
    out_far = across(out_mine)
    o_own, h1, qkv, probs, qkv_mine = call(
        functools.partial(attention, size, shard_rows, rows, length, width, chunks),
        [
            shape((4, rows, quarter), BF),
            shape((full_rows, width), BF),
            shape((full_rows, 3 * quarter), BF),
            shape((4 * heads, rows, rows), F32),
            shape((width, 3 * quarter), BF),
        ],
        [],
        3 * project,
        scal,
        *blocks,
        *a_chunks,
        cosine,
        sine,
    )

    o_own, out_mine, b.state, c.state = sync(o_own, out_mine, b.state, c.state)
    o_far = across(o_own)
    b.advance()
    c.advance()

    o_far, out_far, b.state, c.state = sync(o_far, out_far, b.state, c.state)
    kept = [o_own.reshape(full_rows, quarter), o_far.reshape(full_rows, quarter), out_mine, out_far]
    near_all = sibling(jnp.concatenate(kept, axis=0))
    b_chunks = b.finish()
    c_chunks = c.finish()
    x2, h2, o_all, out_rows = call(
        functools.partial(middle, size, rows, width),
        [
            shape((full_rows, width), F32),
            shape((full_rows, width), BF),
            shape((full_rows, width), BF),
            shape((quarter, width), BF),
        ],
        [pltpu.VMEM((width, width), BF)],
        4 * project,
        scal,
        *blocks,
        o_own,
        o_far,
        out_mine,
        out_far,
        near_all,
    )

    h2, b_chunks, c_chunks, cot_far = sync(h2, b_chunks, c_chunks, cot_far)
    cot_diagonal = sibling(cot_far)
    up, gate, hid, in_mine = call(
        functools.partial(hidden_units, size, shard_rows, member_units, chunks),
        [
            shape((full_rows, member_units), F32),
            shape((full_rows, member_units), F32),
            shape((full_rows, member_units), BF),
            shape((width, 2 * member_units), BF),
        ],
        [],
        6 * project,
        scal,
        h2,
        *b_chunks,
    )
    hid, cot_diagonal = sync(hid, cot_diagonal)
    *down_parts, gm = call(
        functools.partial(grad_down_parts, size, rows, padded),
        [shape((piece, width), BF)] * size + [shape((full_rows, width), BF)],
        [pltpu.VMEM((member_units, width), F32)],
        3 * project,
        scal,
        hid,
        cot_own,
        cot_near,
        cot_far,
        cot_diagonal,
    )

    c = Scatter(ring, down_parts)
    c.state, gm, up, c_chunks = sync(c.state, gm, up, c_chunks)
    c.send()
    ggu, u2_keep, u2_give, down_mine = call(
        functools.partial(hidden_back, size, rows, padded, piece, chunks),
        [shape((full_rows, 2 * member_units), BF), pair_full, pair_low, shape((member_units, width), BF)],
        [],
        9 * project,
        scal,
        gm,
        *c_chunks,
        up,
        gate,
        in_mine,
    )

    u2_give, c.got = sync(u2_give, c.got)
    u2_got = sibling(u2_give)
    c.add()
    c.send()
    u2_low = (u2_keep + u2_got.astype(F32)).astype(BF)

    u2_low, ggu = sync(u2_low, ggu)
    u2_first = across(u2_low[0])
    in_parts = call(
        functools.partial(grad_in_parts, size, double),
        [shape((double, 2 * member_units), BF)] * size,
        [pltpu.VMEM((width, 2 * member_units), F32)],
        6 * project,
        scal,
        h2,
        ggu,
    )

    b = Scatter(ring, in_parts)
    b.state, c.got, u2_first, u2_low, hid = sync(b.state, c.got, u2_first, u2_low, hid)
    b.send()
    c.add()
    c.send()
    u2_second = across(u2_low[1])
    y_keep, y_give = call(functools.partial(last_projection, rows), [pair_full, pair_low], [], 3 * project, scal, hid, down_mine)

    y_give, c.got, b.got, u2_second = sync(y_give, c.got, b.got, u2_second)
    b.add()
    b.send()
    c.add()
    c.send()
    gx2, ga = call(
        functools.partial(middle_back, rows),
        [shape((rows, width), F32), pair_low],
        [],
        0,
        scal,
        u2_keep,
        u2_got,
        u2_first,
        u2_second,
        x2,
        cot_own,
        cot_far,
    )
    ga_near = sibling(ga)
    gqkv, ga_all, u1_keep, u1_give = call(
        functools.partial(attention_back, rows, width),
        [shape((full_rows, 3 * quarter), BF), shape((full_rows, width), BF), pair_full, pair_low],
        [pltpu.VMEM((full_rows, quarter), BF), pltpu.VMEM((3, rows, quarter), F32)],
        7 * project,
        scal,
        ga,
        ga_near,
        out_rows,
        qkv,
        probs,
        qkv_mine,
        cosine,
        sine,
    )

    gqkv, u1_give, b.got, c.got = sync(gqkv, u1_give, b.got, c.got)
    b.add()
    b.send()
    u1_got = sibling(u1_give)
    first_parts = call(
        functools.partial(grad_first_parts, size, double, width),
        [shape((double, width), BF)] * size,
        [pltpu.VMEM((width, width), F32)],
        4 * project,
        scal,
        h1,
        gqkv,
        o_all,
        ga_all,
    )
    down_low = sum(v.astype(F32) for v in c.run()).astype(BF)

    a = Scatter(ring, first_parts)
    a.state, u1_got, down_low = sync(a.state, u1_got, down_low)
    a.send()
    u1_low = (u1_keep[1] + u1_got[1].astype(F32)).astype(BF)
    u1_far = across(u1_low)

    a.got, b.got, u1_far, y_give = sync(a.got, b.got, u1_far, y_give)
    a.add()
    a.send()
    b.add()
    b.send()
    down_other = across(down_low)
    y_got = sibling(y_give)

    while a.step < ring.half - 2:
        a.got, down_other = sync(a.got, down_other)
        a.add()
        a.send()
    y_low = (y_keep[1] + y_got[1].astype(F32)).astype(BF)
    y_far = across(y_low)

    def halves(summed):
        columns = summed[0].shape[1]
        return call(functools.partial(split_rows, size), [shape((shard_rows, columns), BF)] * 2, [], 0, scal, *summed)

    in_keep, in_give = halves(b.run())
    in_near = sibling(in_give)
    a.got, in_keep, in_near, y_far = sync(a.got, in_keep, in_near, y_far)
    a.add()
    a.send()
    in_far = across(in_keep)
    in_diagonal = across(in_near)
    first_keep, first_give = halves(a.run())
    first_keep, first_give, in_far = sync(first_keep, first_give, in_far)
    first_far = across(first_keep)
    first_near = sibling(first_give)
    first_diagonal = across(first_near)
    u1_far, y_far, down_other, in_keep, first_near = sync(u1_far, y_far, down_other, in_keep, first_near)
    (grad_tokens,) = call(
        functools.partial(finish_tokens, rows), [shape((rows, width), F32)], [], 0, scal, u1_keep, u1_got, u1_far, own, gx2
    )
    result = (x2[:rows] + (y_keep[0] + y_got[0].astype(F32) + y_far.astype(F32))).astype(BF)
    (grad_down,) = call(functools.partial(unpack_down, size, piece), [shape((2 * piece, width), F32)], [], 0, scal, down_low, down_other)
    (grad_in,) = call(
        functools.partial(unpack_in, size, units, piece, padded),
        [shape((shard_rows, 2 * units), F32)],
        [pltpu.VMEM((4, shard_rows, 2 * member_units), F32)],
        0,
        scal,
        in_keep,
        in_near,
        in_far,
        in_diagonal,
    )
    grad_qkv, grad_out = call(
        functools.partial(unpack_first, size, width),
        [shape((shard_rows, 3 * width), F32), shape((shard_rows, width), F32)],
        [],
        0,
        scal,
        first_keep,
        first_near,
        first_far,
        first_diagonal,
    )
    return (
        result.reshape(micro, 1, length, width),
        grad_tokens.reshape(micro, 1, length, width),
        grad_qkv,
        grad_out,
        grad_in,
        grad_down,
    )


def solution(mesh):
    inner = Mesh(mesh.devices.reshape(mesh.shape["rep"], mesh.shape["shard"] // 2, 2), ("rep", "ring", "core"))
    everyone = ("rep", "ring", "core")
    group = ("ring", "core")
    sequences = P(None, everyone, None, None)
    weights = P(group, None)
    return jax.shard_map(
        local,
        mesh=inner,
        in_specs=(sequences, P(None, everyone), weights, weights, weights, weights, sequences),
        out_specs=(sequences, sequences, weights, weights, weights, weights),
        check_vma=False,
    )
```

```python
import functools

import jax
import jax.numpy as jnp
import numpy as np
from jax import lax
from jax.experimental import pallas as pl
from jax.experimental.pallas import tpu as pltpu
from jax.sharding import Mesh, PartitionSpec as P

H = 16
HD = 64
HALF = HD // 2
LANES = 128
PACK = 16
ROWS = 8
BF = jnp.bfloat16
F32 = jnp.float32
SWAP = ((0, 1), (1, 0))
MIB = 1 << 20
WEIGHT = {'ring_add': 16000000000, 'unpack_in': 4000000000, 'pack_in': 0, 'hidden_back': 32000000000, 'grad_first_parts': 32000000000, 'middle_back': 8000000000, 'hidden_units': 16000000000}
BLOCKS = ((0, 1, 2, 3), (1, 0, 3, 2), (2, 3, 0, 1), (3, 2, 1, 0))


def dot(left, right):
    return jnp.dot(left, right, preferred_element_type=F32)


def dot_rt(left, right):
    return lax.dot_general(left, right, (((1,), (1,)), ((), ())), preferred_element_type=F32)


def dot_lt(left, right):
    return lax.dot_general(left, right, (((0,), (0,)), ((), ())), preferred_element_type=F32)


def norm_rows(values):
    centre = values - jnp.mean(values, axis=-1, keepdims=True)
    inverse = lax.rsqrt(jnp.mean(centre * centre, axis=-1, keepdims=True) + 1e-05)
    return (centre * inverse, inverse)


def norm_back(normed, inverse, upstream):
    return inverse * (
        upstream
        - jnp.mean(upstream, axis=-1, keepdims=True)
        - normed * jnp.mean(upstream * normed, axis=-1, keepdims=True)
    )


def across(value):
    return lax.ppermute(value, "rep", SWAP)


def sibling(value):
    return lax.ppermute(value, "core", SWAP)


def order_of(size):
    return list(range(0, size, 2)) + list(range(size - 1, 0, -2))


def scalar_table(size):
    order = order_of(size)
    place = np.argsort(order)
    table = np.zeros((2, size, 2, 2 * size + 5), np.int32)
    for rep in range(2):
        for g in range(size):
            for core in range(2):
                at = [order[(place[g] + k) % size] for k in range(size)]
                of = [(place[o] - place[g]) % size for o in range(size)]
                members = [2 * core + rep, 2 * (1 - core) + rep, 2 * core + 1 - rep, 2 * (1 - core) + 1 - rep]
                table[rep, g, core] = at + of + [core] + members
    return table


def upper_half(rows):
    return -(-(rows // 2) // PACK) * PACK


class Ring:
    def __init__(self, size):
        self.size = size
        self.half = size // 2
        order = order_of(size)
        self.right = [(order[i], order[(i + 1) % size]) for i in range(size)]
        self.left = [(b, a) for a, b in self.right]

    def exchange(self, pair):
        return lax.ppermute(pair[0], "ring", self.right), lax.ppermute(pair[1], "ring", self.left)


class Gather:
    def __init__(self, ring, chunk):
        self.ring = ring
        self.step = 0
        self.got = {0: chunk}
        self.cut = upper_half(chunk.shape[0])
        self.state = (chunk, chunk)

    def advance(self):
        if self.step == self.ring.half:
            return
        self.step += 1
        if self.step == self.ring.half:
            self.far = self.ring.exchange((self.state[0][: self.cut], self.state[1][self.cut :]))
            self.state = ()
            return
        self.state = self.ring.exchange(self.state)
        self.got[self.ring.size - self.step], self.got[self.step] = self.state

    def finish(self):
        while self.step < self.ring.half:
            self.advance()
        return [self.got[k] for k in range(self.ring.size) if k != self.ring.half] + list(self.far)


def ring_add(cut, right_term, left_term, right_got, left_got, right_ref, left_ref):
    if cut is None:
        right_ref[...] = (right_term[...].astype(F32) + right_got[...].astype(F32)).astype(BF)
        left_ref[...] = (left_term[...].astype(F32) + left_got[...].astype(F32)).astype(BF)
    else:
        right_ref[:cut] = (right_term[:cut].astype(F32) + right_got[...].astype(F32)).astype(BF)
        right_ref[cut:] = right_term[cut:]
        left_ref[:cut] = left_term[:cut]
        left_ref[cut:] = (left_term[cut:].astype(F32) + left_got[...].astype(F32)).astype(BF)


class Scatter:
    def __init__(self, ring, parts):
        self.ring = ring
        self.step = 0
        self.parts = parts
        self.cut = upper_half(parts[0].shape[0])
        far = parts[ring.half]
        self.state = (far[: self.cut], far[self.cut :])

    def send(self):
        self.got = self.ring.exchange(self.state)

    def add(self):
        ring = self.ring
        self.step += 1
        place = ring.half - self.step
        terms = (self.parts[place], self.parts[ring.size - place])
        body = functools.partial(ring_add, self.cut if self.step == 1 else None)
        self.state = tuple(call(body, [shape(t.shape, BF) for t in terms], [], 16000000000, *terms, *self.got, smem=0))

    def run(self):
        while self.step < self.ring.half - 1:
            self.add()
            self.send()
        return self.parts[0], *self.got


def sync(*values):
    return lax.optimization_barrier(values)


def call(body, outs, scratch, flops, *args, smem=1, still=0):
    nbytes = sum(a.size * a.dtype.itemsize for a in args) + sum(o.size * o.dtype.itemsize for o in outs)
    spaces = [pltpu.SMEM] * smem + [pl.ANY] * still + [pltpu.VMEM] * (len(args) - smem - still)
    return pl.pallas_call(
        body,
        name=body.func.__name__,
        out_shape=outs,
        in_specs=[pl.BlockSpec(memory_space=space) for space in spaces],
        out_specs=[pl.BlockSpec(memory_space=pltpu.VMEM)] * len(outs),
        scratch_shapes=scratch,
        compiler_params=pltpu.CompilerParams(vmem_limit_bytes=12 * MIB),
        cost_estimate=pl.CostEstimate(flops=WEIGHT.get(body.func.__name__, flops), bytes_accessed=nbytes, transcendentals=0),
    )(*args)


def shape(dims, dtype):
    return jax.ShapeDtypeStruct(dims, dtype)


def lanes(start, size):
    return pl.ds(pl.multiple_of(start, LANES), size)


def tiles_of(extent, tile=256):
    return [(at, min(tile, extent - at)) for at in range(0, extent, tile)]


def main_part(units):
    return units // LANES * LANES


def runs(size, stride, piece):
    units = size * stride
    main = main_part(units)
    rest = units - main
    for g in range(size):
        first = g * stride
        for low, high in ((first, min(first + piece, main)), (max(first, main), first + piece)):
            if low < high:
                columns = tuple(p * main + low if low < main else 2 * main + p * rest + low - main for p in range(2))
                yield g, low - first, high - low, columns


def pack_tokens(rows, prefix_ref, tokens_ref, own_ref):
    own_ref[:rows, :] = tokens_ref[...]
    for m in range(own_ref.shape[0] - rows):
        own_ref[rows + m : rows + m + 1, :] = jnp.broadcast_to(prefix_ref[m : m + 1, :].astype(F32), (1, own_ref.shape[1])).astype(BF)


def pack_first(size, width, scal, qkv_ref, out_ref, own_ref, sib_ref, sems):
    quarter = width // 4
    copies = []
    for ref, member in ((own_ref, scal[2 * size + 1]), (sib_ref, scal[2 * size + 2])):
        for j in range(4):
            source = qkv_ref.at[:, lanes(j * width + member * quarter, quarter)] if j < 3 else out_ref.at[:, lanes(member * quarter, quarter)]
            copies.append(pltpu.make_async_copy(source, ref.at[:, j * quarter : (j + 1) * quarter], sems.at[len(copies)]))
            copies[-1].start()
    for copy in copies:
        copy.wait()


def pack_in(size, units, piece, padded, scal, in_ref, down_ref, own_ref, sib_ref, rows_ref):
    rep = scal[2 * size + 1] - 2 * scal[2 * size]
    for r in range(2):

        @pl.when(rep == r)
        def _(r=r):
            rows_ref[...] = down_ref[r * piece : (r + 1) * piece, :]

    for ref, member in ((own_ref, scal[2 * size + 1]), (sib_ref, scal[2 * size + 2])):
        if padded > piece:
            ref[...] = jnp.zeros_like(ref)
        for q in range(4):

            @pl.when(member == q)
            def _(ref=ref, q=q):
                for g, offset, length, columns in runs(size, padded, piece):
                    for part in range(2):
                        start = part * units + (g * 4 + q) * piece + offset
                        ref[:, columns[part] : columns[part] + length] = in_ref[:, start : start + length]


def place_chunks(size, scal, chunk_refs, store):
    half = size // 2
    places = [k for k in range(size) if k != half]
    for k, ref in zip(places, chunk_refs, strict=False):
        store(scal[k], 0, ref[...])
    top, bottom = chunk_refs[-2:]
    store(scal[half], 0, top[...])
    store(scal[half], top.shape[0], bottom[...])


def place_rows(size, shard_rows, scal, chunk_refs, put):
    core = scal[2 * size]

    def store(chip, first, value):
        for lower in range(2):
            begin = lower * shard_rows - first
            if begin < 0 or begin >= value.shape[0]:
                continue
            row = chip * (2 * shard_rows) + (core if lower == 0 else 1 - core) * shard_rows
            put(pl.multiple_of(row, PACK), value[begin : begin + shard_rows])

    place_chunks(size, scal, chunk_refs, store)


def turned(values):
    lane = lax.broadcasted_iota(jnp.int32, values.shape, 1) % HD
    wide = values.shape[1]
    return jnp.where(lane < HALF, pltpu.roll(values, wide - HALF, 1), pltpu.roll(values, HALF, 1))


def visible(rows, length, limits):
    query = lax.broadcasted_iota(jnp.int32, (rows, rows), 0)
    key = lax.broadcasted_iota(jnp.int32, (rows, rows), 1)
    inside = (key % length).astype(F32)
    limit = jnp.zeros((rows, rows), F32)
    for s in range(rows // length):
        limit = jnp.where(key // length == s, limits[s : s + 1, :rows].astype(F32), limit)
    return (query // length == key // length) & ((key <= query) | (inside < limit))


def gather_out(size, shard_rows, quarter, scal, *refs):
    out_ref = refs[-1]

    def put(row, value):
        out_ref[pl.ds(row, shard_rows), :] = value[:, 3 * quarter :]

    place_rows(size, shard_rows, scal, refs[:-1], put)


def attention(size, shard_rows, rows, length, width, n_chunks, scal, *refs):
    blocks = refs[:4]
    chunks = refs[4 : 4 + n_chunks]
    cos_ref, sin_ref, o_ref, h1_ref, qkv_ref, p_ref, w_ref = refs[4 + n_chunks :]
    quarter = width // 4

    def put(row, value):
        w_ref[pl.ds(row, shard_rows), :] = value[:, : 3 * quarter]

    place_rows(size, shard_rows, scal, chunks, put)
    for b in range(4):
        normed, _ = norm_rows(blocks[b][:rows, :].astype(F32))
        h1_ref[b * rows : (b + 1) * rows, :] = normed.astype(BF)
    for j in range(3):
        mixed = dot(h1_ref[...], w_ref[:, j * quarter : (j + 1) * quarter])
        for b in range(4):
            piece = mixed[b * rows : (b + 1) * rows, :]
            if j < 2:
                piece = piece * cos_ref[...] + turned(piece) * sin_ref[...]
            qkv_ref[b * rows : (b + 1) * rows, j * quarter : (j + 1) * quarter] = piece.astype(BF)
    for b in range(4):
        allowed = visible(rows, length, blocks[b][rows:, :])
        block = slice(b * rows, (b + 1) * rows)
        for h in range(quarter // HD):
            query = qkv_ref[block, h * HD : (h + 1) * HD]
            keys = qkv_ref[block, quarter + h * HD : quarter + (h + 1) * HD]
            values = qkv_ref[block, 2 * quarter + h * HD : 2 * quarter + (h + 1) * HD]
            scores = jnp.where(allowed, dot_rt(query, keys) * HD ** (-0.5), -1e30)
            expo = jnp.exp(scores - jnp.max(scores, axis=-1, keepdims=True))
            probs = expo / jnp.sum(expo, axis=-1, keepdims=True)
            p_ref[b * (quarter // HD) + h] = probs
            o_ref[b, :, h * HD : (h + 1) * HD] = dot(probs.astype(BF), values).astype(BF)


def middle(size, rows, width, scal, *refs):
    blocks = refs[:4]
    o_own, o_far, w_own, w_far, near_ref = refs[4:9]
    full = 4 * rows
    outputs = (
        lambda b: o_own[b],
        lambda b: near_ref[b * rows : (b + 1) * rows],
        lambda b: o_far[b],
        lambda b: near_ref[full + b * rows : full + (b + 1) * rows],
    )
    weights = (w_own, near_ref.at[2 * full : 2 * full + width], w_far, near_ref.at[2 * full + width :])
    x2_ref, h2_ref, o_ref, rows_ref, w_full = refs[9:]
    quarter = width // 4
    members = [scal[2 * size + 1 + m] for m in range(4)]
    for m in range(4):
        w_full[:, lanes(members[m] * quarter, quarter)] = weights[m][...]
        for b in range(4):
            o_ref[b * rows : (b + 1) * rows, lanes(members[m] * quarter, quarter)] = outputs[m](BLOCKS[m][b])
    rows_ref[...] = w_full[pl.ds(pl.multiple_of(members[0] * quarter, quarter), quarter), :]
    for j in range(4):
        columns = slice(j * quarter, (j + 1) * quarter)
        added = dot(o_ref[...], w_full[:, columns])
        for b in range(4):
            x2_ref[b * rows : (b + 1) * rows, columns] = blocks[b][:rows, columns].astype(F32) + added[b * rows : (b + 1) * rows, :]
    for b in range(4):
        block = slice(b * rows, (b + 1) * rows)
        normed, _ = norm_rows(x2_ref[block, :])
        h2_ref[block, :] = normed.astype(BF)


def hidden_units(size, shard_rows, members_units, n_chunks, scal, h2_ref, *refs):
    chunks = refs[:n_chunks]
    up_ref, gate_ref, hid_ref, w_ref = refs[n_chunks:]

    def put(row, value):
        w_ref[pl.ds(row, shard_rows), :] = value

    place_rows(size, shard_rows, scal, chunks, put)
    main = main_part(members_units)
    rest = members_units - main

    def put_units(columns, up, gate):
        up_ref[:, columns] = up
        gate_ref[:, columns] = gate
        hid_ref[:, columns] = (gate * jax.nn.sigmoid(gate) * up).astype(BF)

    for at, tile in tiles_of(main):
        up = dot(h2_ref[...], w_ref[:, at : at + tile])
        put_units(slice(at, at + tile), up, dot(h2_ref[...], w_ref[:, main + at : main + at + tile]))
    if rest:
        both = dot(h2_ref[...], w_ref[:, 2 * main :])
        put_units(slice(main, members_units), both[:, :rest], both[:, rest:])


def hidden_back(size, rows, padded, piece, n_chunks, scal, *refs):
    gm_ref = refs[0]
    chunks = refs[1 : 1 + n_chunks]
    up_ref, gate_ref, w_in, ggu_ref, keep_ref, give_ref, down_ref = refs[1 + n_chunks :]
    units = up_ref.shape[1]
    width = gm_ref.shape[1]
    if padded > piece:
        down_ref[...] = jnp.zeros_like(down_ref)

    def store(chip, first, value):
        down_ref[pl.ds(pl.multiple_of(chip * padded + first, ROWS), value.shape[0]), :] = value

    place_chunks(size, scal, chunks, store)
    tile = 256

    main = main_part(units)
    rest = units - main
    pieces = [(at, size_, at, main + at) for at, size_ in tiles_of(main)]
    if rest:
        pieces.append((main, rest, 2 * main, 2 * main + rest))
    for at, count, up_at, gate_at in pieces:
        grad = dot_rt(gm_ref[...], down_ref[at : at + count, :])
        up = up_ref[:, at : at + count]
        gate = gate_ref[:, at : at + count]
        sig = jax.nn.sigmoid(gate)
        ggu_ref[:, up_at : up_at + count] = (grad * (gate * sig)).astype(BF)
        ggu_ref[:, gate_at : gate_at + count] = (grad * up * (sig * (1.0 + gate * (1.0 - sig)))).astype(BF)

    @pl.loop(0, width // tile)
    def _(i):
        at = pl.multiple_of(i * tile, tile)
        back = dot_rt(ggu_ref[...], w_in[pl.ds(at, tile), :])
        share(back, rows, keep_ref, give_ref, pl.ds(at, tile))


def share(partial, rows, keep_ref, give_ref, columns):
    keep_ref[0, :, columns] = partial[:rows]
    give_ref[0, :, columns] = partial[rows : 2 * rows].astype(BF)
    keep_ref[1, :, columns] = partial[2 * rows : 3 * rows]
    give_ref[1, :, columns] = partial[3 * rows :].astype(BF)


def last_projection(rows, scal, hid_ref, down_ref, keep_ref, give_ref):
    tile = 256

    @pl.loop(0, down_ref.shape[1] // tile)
    def _(i):
        columns = pl.ds(pl.multiple_of(i * tile, tile), tile)
        share(dot(hid_ref[...], down_ref[:, columns]), rows, keep_ref, give_ref, columns)


def write_parts(size, stride, scal, total, refs):
    for k, ref in enumerate(refs):
        ref[...] = total[pl.ds(pl.multiple_of(scal[k] * stride, ROWS), ref.shape[0]), :].astype(BF)


def grad_down_parts(size, rows, padded, scal, hid_ref, *refs):
    gm_ref, total = refs[-2:]
    for b in range(4):
        gm_ref[b * rows : (b + 1) * rows, :] = refs[b][...]
    tile = 256

    @pl.loop(0, gm_ref.shape[1] // tile)
    def _(i):
        columns = pl.ds(pl.multiple_of(i * tile, tile), tile)
        total[:, columns] = dot_lt(hid_ref[...], gm_ref[:, columns])

    write_parts(size, padded, scal, total, refs[4:-2])


def grad_in_parts(size, double, scal, h2_ref, ggu_ref, *refs):
    total = refs[-1]
    for at, tile in tiles_of(ggu_ref.shape[1]):
        total[:, at : at + tile] = dot_lt(h2_ref[...], ggu_ref[:, at : at + tile])
    write_parts(size, double, scal, total, refs[:-1])


def middle_back(rows, scal, keep_ref, got_ref, far_first, far_second, x2_ref, cot_own, cot_far, gx2_ref, ga_ref):
    for i, cot in ((0, cot_own), (1, cot_far)):
        upstream = keep_ref[i] + got_ref[i].astype(F32) + (far_second, far_first)[i][...].astype(F32)
        normed, inverse = norm_rows(x2_ref[2 * i * rows : (2 * i + 1) * rows, :])
        total = cot[...].astype(F32) + norm_back(normed, inverse, upstream)
        if i == 0:
            gx2_ref[...] = total
        ga_ref[i] = total.astype(BF)


def attention_back(rows, width, scal, ga_own, ga_near, out_rows, qkv_ref, p_ref, w_ref, cos_ref, sin_ref, gqkv_ref, ga_ref, keep_ref, give_ref, go_ref, grad_ref):
    quarter = width // 4
    for b, value in enumerate((ga_own[0], ga_near[0], ga_own[1], ga_near[1])):
        ga_ref[b * rows : (b + 1) * rows, :] = value
    go_ref[...] = dot_rt(ga_ref[...], out_rows[...]).astype(BF)
    for b in range(4):
        block = slice(b * rows, (b + 1) * rows)
        for h in range(quarter // HD):
            head = slice(h * HD, (h + 1) * HD)
            query = qkv_ref[block, h * HD : (h + 1) * HD]
            keys = qkv_ref[block, quarter + h * HD : quarter + (h + 1) * HD]
            values = qkv_ref[block, 2 * quarter + h * HD : 2 * quarter + (h + 1) * HD]
            probs = p_ref[b * (quarter // HD) + h]
            go = go_ref[block, head]
            dprob = dot_rt(go, values)
            centre = jnp.sum(probs * dprob, axis=-1, keepdims=True)
            dscore = (probs * (dprob - centre)).astype(BF)
            grad_ref[0, :, head] = dot(dscore, keys) * HD ** (-0.5)
            grad_ref[1, :, head] = dot_lt(dscore, query) * HD ** (-0.5)
            grad_ref[2, :, head] = dot_lt(probs.astype(BF), go)
        for j in range(3):
            grad = grad_ref[j]
            if j < 2:
                grad = grad * cos_ref[...] - turned(grad) * sin_ref[...]
            gqkv_ref[block, j * quarter : (j + 1) * quarter] = grad.astype(BF)
    for j in range(4):
        columns = slice(j * quarter, (j + 1) * quarter)
        share(dot_rt(gqkv_ref[...], w_ref[columns, :]), rows, keep_ref, give_ref, columns)


def grad_first_parts(size, double, width, scal, h1_ref, gqkv_ref, o_ref, ga_ref, *refs):
    total = refs[-1]
    quarter = width // 4
    for j in range(3):
        columns = slice(j * quarter, (j + 1) * quarter)
        total[:, columns] = dot_lt(h1_ref[...], gqkv_ref[:, columns])
    total[:, 3 * quarter :] = dot_lt(o_ref[...], ga_ref[:, lanes(scal[2 * size + 1] * quarter, quarter)])
    write_parts(size, double, scal, total, refs[:-1])


def split_rows(size, scal, own_ref, right_ref, left_ref, keep_ref, give_ref):
    core = scal[2 * size]
    rows = keep_ref.shape[0]
    for ref, first in ((keep_ref, core), (give_ref, 1 - core)):
        here = pl.ds(pl.multiple_of(first * rows, PACK), rows)
        ref[...] = (own_ref[here, :].astype(F32) + right_ref[here, :].astype(F32) + left_ref[here, :].astype(F32)).astype(BF)


def finish_tokens(rows, scal, keep_ref, got_ref, far_ref, block_ref, gx2_ref, out_ref):
    upstream = keep_ref[0] + got_ref[0].astype(F32) + far_ref[...].astype(F32)
    normed, inverse = norm_rows(block_ref[:rows, :].astype(F32))
    out_ref[...] = gx2_ref[...] + norm_back(normed, inverse, upstream)


def unpack_down(size, piece, scal, low_ref, other_ref, out_ref):
    rep = scal[2 * size + 1] - 2 * scal[2 * size]
    for r in range(2):

        @pl.when(rep == r)
        def _(r=r):
            out_ref[r * piece : (r + 1) * piece, :] = low_ref[...].astype(F32)
            out_ref[(1 - r) * piece : (2 - r) * piece, :] = other_ref[...].astype(F32)


def unpack_first(size, width, scal, own_ref, near_ref, far_ref, diagonal_ref, qkv_ref, out_ref):
    quarter = width // 4
    for m, ref in enumerate((own_ref, near_ref, far_ref, diagonal_ref)):
        value = ref[...].astype(F32)
        at = scal[2 * size + 1 + m] * quarter
        for j in range(3):
            qkv_ref[:, lanes(j * width + at, quarter)] = value[:, j * quarter : (j + 1) * quarter]
        out_ref[:, lanes(at, quarter)] = value[:, 3 * quarter :]


def unpack_in(size, units, piece, padded, scal, own_ref, near_ref, far_ref, diagonal_ref, in_ref, held):
    for m, ref in enumerate((own_ref, near_ref, far_ref, diagonal_ref)):
        held[scal[2 * size + 1 + m]] = ref[...].astype(F32)
    for q in range(4):
        for g, offset, length, columns in runs(size, padded, piece):
            for part in range(2):
                start = part * units + (g * 4 + q) * piece + offset
                in_ref[:, start : start + length] = held[q, :, columns[part] : columns[part] + length]


def local(tokens, prefix, qkv_weight, out_weight, in_weight, down_weight, cotangent):
    micro, _, length, width = tokens.shape
    rows = micro * length
    size = lax.axis_size("ring")
    ring = Ring(size)
    rep = lax.axis_index("rep")
    core = lax.axis_index("core")
    shard_rows = qkv_weight.shape[0]
    double = 2 * shard_rows
    units = in_weight.shape[1] // 2
    quarter = width // 4
    heads = quarter // HD
    piece = units // (4 * size)
    padded = -(-piece // ROWS) * ROWS
    while 2 * size * padded % LANES:
        padded += ROWS
    member_units = size * padded
    chunks = size + 1
    table = scalar_table(size)
    scal = lax.dynamic_slice(
        jnp.asarray(table.reshape(-1, table.shape[-1])), ((rep * size + lax.axis_index("ring")) * 2 + core, 0), (1, table.shape[-1])
    )[0]

    position = np.arange(length, dtype=np.float32)[:, None]
    frequency = np.float32(10000.0) ** (-np.arange(0, HD, 2, dtype=np.float32) / np.float32(HD))
    angles = (position * frequency[None, :]).astype(np.float32)
    angles = np.concatenate([angles, angles], axis=-1)
    sign = np.where(np.arange(HD) < HALF, -1.0, 1.0).astype(np.float32)
    cosine = jnp.asarray(np.tile(np.cos(angles), (micro, heads)).astype(np.float32))
    sine = jnp.asarray(np.tile(np.sin(angles) * sign, (micro, heads)).astype(np.float32))

    full_rows = 4 * rows
    pair_low = shape((2, rows, width), BF)
    pair_full = shape((2, rows, width), F32)
    project = 2 * full_rows * width * quarter

    tokens = tokens.reshape(rows, width)
    cot_own = cotangent.reshape(rows, width)
    a_own, a_sib = call(
        functools.partial(pack_first, size, width),
        [shape((shard_rows, width), BF)] * 2,
        [pltpu.SemaphoreType.DMA((8,))],
        0,
        scal,
        qkv_weight,
        out_weight,
        still=2,
    )
    a = Gather(ring, jnp.concatenate([a_own, sibling(a_sib)], axis=0))

    a.state, in_weight, tokens, cot_own = sync(a.state, in_weight, tokens, cot_own)
    a.advance()
    b_own, b_sib, down_rows = call(
        functools.partial(pack_in, size, units, piece, padded),
        [shape((shard_rows, 2 * member_units), BF)] * 2 + [shape((piece, width), BF)],
        [],
        0,
        scal,
        in_weight,
        down_weight,
    )
    c = Gather(ring, down_rows)
    c.advance()
    b_got = sibling(b_sib)
    (own,) = call(functools.partial(pack_tokens, rows), [shape((rows + micro, width), BF)], [], 0, prefix, tokens, smem=0)
    near = sibling(own)
    cot_near = sibling(cot_own)

    a.state, own, b_own, b_got, near, cot_near = sync(a.state, own, b_own, b_got, near, cot_near)
    a.advance()
    far = across(own)
    b = Gather(ring, jnp.concatenate([b_own, b_got], axis=0))

    (a.state,) = sync(a.state)
    a.advance()
    far, cot_own, b.state, c.state = sync(far, cot_own, b.state, c.state)
    cot_far = across(cot_own)
    b.advance()

    while a.step < ring.half - 1:
        (a.state,) = sync(a.state)
        a.advance()
    a.state, far, cot_far = sync(a.state, far, cot_far)
    a_chunks = a.finish()
    diagonal = sibling(far)

    a_chunks, b.state, c.state, diagonal = sync(a_chunks, b.state, c.state, diagonal)
    blocks = [own, near, far, diagonal]
    b.advance()
    c.advance()
    (out_mine,) = call(functools.partial(gather_out, size, shard_rows, quarter), [shape((width, quarter), BF)], [], 0, scal, *a_chunks)
    out_far = across(out_mine)
    o_own, h1, qkv, probs, qkv_mine = call(
        functools.partial(attention, size, shard_rows, rows, length, width, chunks),
        [
            shape((4, rows, quarter), BF),
            shape((full_rows, width), BF),
            shape((full_rows, 3 * quarter), BF),
            shape((4 * heads, rows, rows), F32),
            shape((width, 3 * quarter), BF),
        ],
        [],
        3 * project,
        scal,
        *blocks,
        *a_chunks,
        cosine,
        sine,
    )

    o_own, out_mine, b.state, c.state = sync(o_own, out_mine, b.state, c.state)
    o_far = across(o_own)
    b.advance()
    c.advance()

    o_far, out_far, b.state, c.state = sync(o_far, out_far, b.state, c.state)
    kept = [o_own.reshape(full_rows, quarter), o_far.reshape(full_rows, quarter), out_mine, out_far]
    near_all = sibling(jnp.concatenate(kept, axis=0))
    b_chunks = b.finish()
    c_chunks = c.finish()
    x2, h2, o_all, out_rows = call(
        functools.partial(middle, size, rows, width),
        [
            shape((full_rows, width), F32),
            shape((full_rows, width), BF),
            shape((full_rows, width), BF),
            shape((quarter, width), BF),
        ],
        [pltpu.VMEM((width, width), BF)],
        4 * project,
        scal,
        *blocks,
        o_own,
        o_far,
        out_mine,
        out_far,
        near_all,
    )

    h2, b_chunks, c_chunks, cot_far = sync(h2, b_chunks, c_chunks, cot_far)
    cot_diagonal = sibling(cot_far)
    up, gate, hid, in_mine = call(
        functools.partial(hidden_units, size, shard_rows, member_units, chunks),
        [
            shape((full_rows, member_units), F32),
            shape((full_rows, member_units), F32),
            shape((full_rows, member_units), BF),
            shape((width, 2 * member_units), BF),
        ],
        [],
        6 * project,
        scal,
        h2,
        *b_chunks,
    )
    hid, cot_diagonal = sync(hid, cot_diagonal)
    *down_parts, gm = call(
        functools.partial(grad_down_parts, size, rows, padded),
        [shape((piece, width), BF)] * size + [shape((full_rows, width), BF)],
        [pltpu.VMEM((member_units, width), F32)],
        3 * project,
        scal,
        hid,
        cot_own,
        cot_near,
        cot_far,
        cot_diagonal,
    )

    c = Scatter(ring, down_parts)
    c.state, gm, up, c_chunks = sync(c.state, gm, up, c_chunks)
    c.send()
    ggu, u2_keep, u2_give, down_mine = call(
        functools.partial(hidden_back, size, rows, padded, piece, chunks),
        [shape((full_rows, 2 * member_units), BF), pair_full, pair_low, shape((member_units, width), BF)],
        [],
        9 * project,
        scal,
        gm,
        *c_chunks,
        up,
        gate,
        in_mine,
    )

    u2_give, c.got = sync(u2_give, c.got)
    u2_got = sibling(u2_give)
    c.add()
    c.send()
    u2_low = (u2_keep + u2_got.astype(F32)).astype(BF)

    u2_low, ggu = sync(u2_low, ggu)
    u2_first = across(u2_low[0])
    in_parts = call(
        functools.partial(grad_in_parts, size, double),
        [shape((double, 2 * member_units), BF)] * size,
        [pltpu.VMEM((width, 2 * member_units), F32)],
        6 * project,
        scal,
        h2,
        ggu,
    )

    b = Scatter(ring, in_parts)
    b.state, c.got, u2_first, u2_low, hid = sync(b.state, c.got, u2_first, u2_low, hid)
    b.send()
    c.add()
    c.send()
    u2_second = across(u2_low[1])
    y_keep, y_give = call(functools.partial(last_projection, rows), [pair_full, pair_low], [], 3 * project, scal, hid, down_mine)

    y_give, c.got, b.got, u2_second = sync(y_give, c.got, b.got, u2_second)
    b.add()
    b.send()
    c.add()
    c.send()
    gx2, ga = call(
        functools.partial(middle_back, rows),
        [shape((rows, width), F32), pair_low],
        [],
        0,
        scal,
        u2_keep,
        u2_got,
        u2_first,
        u2_second,
        x2,
        cot_own,
        cot_far,
    )
    ga_near = sibling(ga)
    gqkv, ga_all, u1_keep, u1_give = call(
        functools.partial(attention_back, rows, width),
        [shape((full_rows, 3 * quarter), BF), shape((full_rows, width), BF), pair_full, pair_low],
        [pltpu.VMEM((full_rows, quarter), BF), pltpu.VMEM((3, rows, quarter), F32)],
        7 * project,
        scal,
        ga,
        ga_near,
        out_rows,
        qkv,
        probs,
        qkv_mine,
        cosine,
        sine,
    )

    gqkv, u1_give, b.got, c.got = sync(gqkv, u1_give, b.got, c.got)
    b.add()
    b.send()
    u1_got = sibling(u1_give)
    first_parts = call(
        functools.partial(grad_first_parts, size, double, width),
        [shape((double, width), BF)] * size,
        [pltpu.VMEM((width, width), F32)],
        4 * project,
        scal,
        h1,
        gqkv,
        o_all,
        ga_all,
    )
    down_low = sum(v.astype(F32) for v in c.run()).astype(BF)

    a = Scatter(ring, first_parts)
    a.state, u1_got, down_low = sync(a.state, u1_got, down_low)
    a.send()
    u1_low = (u1_keep[1] + u1_got[1].astype(F32)).astype(BF)
    u1_far = across(u1_low)

    a.got, b.got, u1_far, y_give = sync(a.got, b.got, u1_far, y_give)
    a.add()
    a.send()
    b.add()
    b.send()
    down_other = across(down_low)
    y_got = sibling(y_give)

    (grad_tokens,) = call(
        functools.partial(finish_tokens, rows), [shape((rows, width), F32)], [], 0, scal, u1_keep, u1_got, u1_far, own, gx2
    )
    while a.step < ring.half - 2:
        a.got, down_other, grad_tokens = sync(a.got, down_other, grad_tokens)
        a.add()
        a.send()
    y_low = (y_keep[1] + y_got[1].astype(F32)).astype(BF)
    y_far = across(y_low)

    def halves(summed):
        columns = summed[0].shape[1]
        return call(functools.partial(split_rows, size), [shape((shard_rows, columns), BF)] * 2, [], 0, scal, *summed)

    in_keep, in_give = halves(b.run())
    in_near = sibling(in_give)
    a.got, in_keep, in_near, y_far = sync(a.got, in_keep, in_near, y_far)
    a.add()
    a.send()
    in_far = across(in_keep)
    in_diagonal = across(in_near)
    first_keep, first_give = halves(a.run())
    first_keep, first_give, in_far = sync(first_keep, first_give, in_far)
    first_far = across(first_keep)
    first_near = sibling(first_give)
    first_diagonal = across(first_near)
    y_far, down_other, in_keep, first_near = sync(y_far, down_other, in_keep, first_near)
    result = (x2[:rows] + (y_keep[0] + y_got[0].astype(F32) + y_far.astype(F32))).astype(BF)
    (grad_down,) = call(functools.partial(unpack_down, size, piece), [shape((2 * piece, width), F32)], [], 0, scal, down_low, down_other)
    (grad_in,) = call(
        functools.partial(unpack_in, size, units, piece, padded),
        [shape((shard_rows, 2 * units), F32)],
        [pltpu.VMEM((4, shard_rows, 2 * member_units), F32)],
        0,
        scal,
        in_keep,
        in_near,
        in_far,
        in_diagonal,
    )
    grad_qkv, grad_out = call(
        functools.partial(unpack_first, size, width),
        [shape((shard_rows, 3 * width), F32), shape((shard_rows, width), F32)],
        [],
        0,
        scal,
        first_keep,
        first_near,
        first_far,
        first_diagonal,
    )
    return (
        result.reshape(micro, 1, length, width),
        grad_tokens.reshape(micro, 1, length, width),
        grad_qkv,
        grad_out,
        grad_in,
        grad_down,
    )


def solution(mesh):
    inner = Mesh(mesh.devices.reshape(mesh.shape["rep"], mesh.shape["shard"] // 2, 2), ("rep", "ring", "core"))
    everyone = ("rep", "ring", "core")
    group = ("ring", "core")
    sequences = P(None, everyone, None, None)
    weights = P(group, None)
    return jax.shard_map(
        local,
        mesh=inner,
        in_specs=(sequences, P(None, everyone), weights, weights, weights, weights, sequences),
        out_specs=(sequences, sequences, weights, weights, weights, weights),
        check_vma=False,
    )
```

```python
import functools

import jax
import jax.numpy as jnp
import numpy as np
from jax import lax
from jax.experimental import pallas as pl
from jax.experimental.pallas import tpu as pltpu
from jax.sharding import Mesh, PartitionSpec as P

H = 16
HD = 64
HALF = HD // 2
LANES = 128
PACK = 16
ROWS = 8
BF = jnp.bfloat16
F32 = jnp.float32
SWAP = ((0, 1), (1, 0))
MIB = 1 << 20
WEIGHT = {'ring_add': 16000000000, 'unpack_in': 4000000000, 'pack_in': 1000000000, 'hidden_back': 32000000000, 'grad_first_parts': 32000000000, 'middle_back': 4000000000, 'hidden_units': 16000000000, 'last_projection': 4000000000}
BLOCKS = ((0, 1, 2, 3), (1, 0, 3, 2), (2, 3, 0, 1), (3, 2, 1, 0))


def dot(left, right):
    return jnp.dot(left, right, preferred_element_type=F32)


def dot_rt(left, right):
    return lax.dot_general(left, right, (((1,), (1,)), ((), ())), preferred_element_type=F32)


def dot_lt(left, right):
    return lax.dot_general(left, right, (((0,), (0,)), ((), ())), preferred_element_type=F32)


def norm_rows(values):
    centre = values - jnp.mean(values, axis=-1, keepdims=True)
    inverse = lax.rsqrt(jnp.mean(centre * centre, axis=-1, keepdims=True) + 1e-05)
    return (centre * inverse, inverse)


def norm_back(normed, inverse, upstream):
    return inverse * (
        upstream
        - jnp.mean(upstream, axis=-1, keepdims=True)
        - normed * jnp.mean(upstream * normed, axis=-1, keepdims=True)
    )


def across(value):
    return lax.ppermute(value, "rep", SWAP)


def sibling(value):
    return lax.ppermute(value, "core", SWAP)


def order_of(size):
    return list(range(0, size, 2)) + list(range(size - 1, 0, -2))


def scalar_table(size):
    order = order_of(size)
    place = np.argsort(order)
    table = np.zeros((2, size, 2, 2 * size + 5), np.int32)
    for rep in range(2):
        for g in range(size):
            for core in range(2):
                at = [order[(place[g] + k) % size] for k in range(size)]
                of = [(place[o] - place[g]) % size for o in range(size)]
                members = [2 * core + rep, 2 * (1 - core) + rep, 2 * core + 1 - rep, 2 * (1 - core) + 1 - rep]
                table[rep, g, core] = at + of + [core] + members
    return table


def upper_half(rows):
    return -(-(rows // 2) // PACK) * PACK


class Ring:
    def __init__(self, size):
        self.size = size
        self.half = size // 2
        order = order_of(size)
        self.right = [(order[i], order[(i + 1) % size]) for i in range(size)]
        self.left = [(b, a) for a, b in self.right]

    def exchange(self, pair):
        return lax.ppermute(pair[0], "ring", self.right), lax.ppermute(pair[1], "ring", self.left)


class Gather:
    def __init__(self, ring, chunk):
        self.ring = ring
        self.step = 0
        self.got = {0: chunk}
        self.cut = upper_half(chunk.shape[0])
        self.state = (chunk, chunk)

    def advance(self):
        if self.step == self.ring.half:
            return
        self.step += 1
        if self.step == self.ring.half:
            self.far = self.ring.exchange((self.state[0][: self.cut], self.state[1][self.cut :]))
            self.state = ()
            return
        self.state = self.ring.exchange(self.state)
        self.got[self.ring.size - self.step], self.got[self.step] = self.state

    def finish(self):
        while self.step < self.ring.half:
            self.advance()
        return [self.got[k] for k in range(self.ring.size) if k != self.ring.half] + list(self.far)


def ring_add(cut, right_term, left_term, right_got, left_got, right_ref, left_ref):
    if cut is None:
        right_ref[...] = (right_term[...].astype(F32) + right_got[...].astype(F32)).astype(BF)
        left_ref[...] = (left_term[...].astype(F32) + left_got[...].astype(F32)).astype(BF)
    else:
        right_ref[:cut] = (right_term[:cut].astype(F32) + right_got[...].astype(F32)).astype(BF)
        right_ref[cut:] = right_term[cut:]
        left_ref[:cut] = left_term[:cut]
        left_ref[cut:] = (left_term[cut:].astype(F32) + left_got[...].astype(F32)).astype(BF)


class Scatter:
    def __init__(self, ring, parts):
        self.ring = ring
        self.step = 0
        self.parts = parts
        self.cut = upper_half(parts[0].shape[0])
        far = parts[ring.half]
        self.state = (far[: self.cut], far[self.cut :])

    def send(self):
        self.got = self.ring.exchange(self.state)

    def add(self):
        ring = self.ring
        self.step += 1
        place = ring.half - self.step
        terms = (self.parts[place], self.parts[ring.size - place])
        body = functools.partial(ring_add, self.cut if self.step == 1 else None)
        self.state = tuple(call(body, [shape(t.shape, BF) for t in terms], [], 16000000000, *terms, *self.got, smem=0))

    def run(self):
        while self.step < self.ring.half - 1:
            self.add()
            self.send()
        return self.parts[0], *self.got


def sync(*values):
    return lax.optimization_barrier(values)


def call(body, outs, scratch, flops, *args, smem=1, still=0):
    nbytes = sum(a.size * a.dtype.itemsize for a in args) + sum(o.size * o.dtype.itemsize for o in outs)
    spaces = [pltpu.SMEM] * smem + [pl.ANY] * still + [pltpu.VMEM] * (len(args) - smem - still)
    return pl.pallas_call(
        body,
        name=body.func.__name__,
        out_shape=outs,
        in_specs=[pl.BlockSpec(memory_space=space) for space in spaces],
        out_specs=[pl.BlockSpec(memory_space=pltpu.VMEM)] * len(outs),
        scratch_shapes=scratch,
        compiler_params=pltpu.CompilerParams(vmem_limit_bytes=12 * MIB),
        cost_estimate=pl.CostEstimate(flops=WEIGHT.get(body.func.__name__, flops), bytes_accessed=nbytes, transcendentals=0),
    )(*args)


def shape(dims, dtype):
    return jax.ShapeDtypeStruct(dims, dtype)


def lanes(start, size):
    return pl.ds(pl.multiple_of(start, LANES), size)


def tiles_of(extent, tile=256):
    return [(at, min(tile, extent - at)) for at in range(0, extent, tile)]


def main_part(units):
    return units // LANES * LANES


def runs(size, stride, piece):
    units = size * stride
    main = main_part(units)
    rest = units - main
    for g in range(size):
        first = g * stride
        for low, high in ((first, min(first + piece, main)), (max(first, main), first + piece)):
            if low < high:
                columns = tuple(p * main + low if low < main else 2 * main + p * rest + low - main for p in range(2))
                yield g, low - first, high - low, columns


def pack_tokens(rows, prefix_ref, tokens_ref, own_ref):
    own_ref[:rows, :] = tokens_ref[...]
    for m in range(own_ref.shape[0] - rows):
        own_ref[rows + m : rows + m + 1, :] = jnp.broadcast_to(prefix_ref[m : m + 1, :].astype(F32), (1, own_ref.shape[1])).astype(BF)


def pack_first(size, width, scal, qkv_ref, out_ref, own_ref, sib_ref, sems):
    quarter = width // 4
    copies = []
    for ref, member in ((own_ref, scal[2 * size + 1]), (sib_ref, scal[2 * size + 2])):
        for j in range(4):
            source = qkv_ref.at[:, lanes(j * width + member * quarter, quarter)] if j < 3 else out_ref.at[:, lanes(member * quarter, quarter)]
            copies.append(pltpu.make_async_copy(source, ref.at[:, j * quarter : (j + 1) * quarter], sems.at[len(copies)]))
            copies[-1].start()
    for copy in copies:
        copy.wait()


def pack_in(size, units, piece, padded, scal, in_ref, down_ref, own_ref, sib_ref, rows_ref):
    rep = scal[2 * size + 1] - 2 * scal[2 * size]
    for r in range(2):

        @pl.when(rep == r)
        def _(r=r):
            rows_ref[...] = down_ref[r * piece : (r + 1) * piece, :]

    for ref, member in ((own_ref, scal[2 * size + 1]), (sib_ref, scal[2 * size + 2])):
        if padded > piece:
            ref[...] = jnp.zeros_like(ref)
        for q in range(4):

            @pl.when(member == q)
            def _(ref=ref, q=q):
                for g, offset, length, columns in runs(size, padded, piece):
                    for part in range(2):
                        start = part * units + (g * 4 + q) * piece + offset
                        ref[:, columns[part] : columns[part] + length] = in_ref[:, start : start + length]


def place_chunks(size, scal, chunk_refs, store):
    half = size // 2
    places = [k for k in range(size) if k != half]
    for k, ref in zip(places, chunk_refs, strict=False):
        store(scal[k], 0, ref[...])
    top, bottom = chunk_refs[-2:]
    store(scal[half], 0, top[...])
    store(scal[half], top.shape[0], bottom[...])


def place_rows(size, shard_rows, scal, chunk_refs, put):
    core = scal[2 * size]

    def store(chip, first, value):
        for lower in range(2):
            begin = lower * shard_rows - first
            if begin < 0 or begin >= value.shape[0]:
                continue
            row = chip * (2 * shard_rows) + (core if lower == 0 else 1 - core) * shard_rows
            put(pl.multiple_of(row, PACK), value[begin : begin + shard_rows])

    place_chunks(size, scal, chunk_refs, store)


def turned(values):
    lane = lax.broadcasted_iota(jnp.int32, values.shape, 1) % HD
    wide = values.shape[1]
    return jnp.where(lane < HALF, pltpu.roll(values, wide - HALF, 1), pltpu.roll(values, HALF, 1))


def visible(rows, length, limits):
    query = lax.broadcasted_iota(jnp.int32, (rows, rows), 0)
    key = lax.broadcasted_iota(jnp.int32, (rows, rows), 1)
    inside = (key % length).astype(F32)
    limit = jnp.zeros((rows, rows), F32)
    for s in range(rows // length):
        limit = jnp.where(key // length == s, limits[s : s + 1, :rows].astype(F32), limit)
    return (query // length == key // length) & ((key <= query) | (inside < limit))


def gather_out(size, shard_rows, quarter, scal, *refs):
    out_ref = refs[-1]

    def put(row, value):
        out_ref[pl.ds(row, shard_rows), :] = value[:, 3 * quarter :]

    place_rows(size, shard_rows, scal, refs[:-1], put)


def attention(size, shard_rows, rows, length, width, n_chunks, scal, *refs):
    blocks = refs[:4]
    chunks = refs[4 : 4 + n_chunks]
    cos_ref, sin_ref, o_ref, h1_ref, qkv_ref, p_ref, w_ref = refs[4 + n_chunks :]
    quarter = width // 4

    def put(row, value):
        w_ref[pl.ds(row, shard_rows), :] = value[:, : 3 * quarter]

    place_rows(size, shard_rows, scal, chunks, put)
    for b in range(4):
        normed, _ = norm_rows(blocks[b][:rows, :].astype(F32))
        h1_ref[b * rows : (b + 1) * rows, :] = normed.astype(BF)
    for j in range(3):
        mixed = dot(h1_ref[...], w_ref[:, j * quarter : (j + 1) * quarter])
        for b in range(4):
            piece = mixed[b * rows : (b + 1) * rows, :]
            if j < 2:
                piece = piece * cos_ref[...] + turned(piece) * sin_ref[...]
            qkv_ref[b * rows : (b + 1) * rows, j * quarter : (j + 1) * quarter] = piece.astype(BF)
    for b in range(4):
        allowed = visible(rows, length, blocks[b][rows:, :])
        block = slice(b * rows, (b + 1) * rows)
        for h in range(quarter // HD):
            query = qkv_ref[block, h * HD : (h + 1) * HD]
            keys = qkv_ref[block, quarter + h * HD : quarter + (h + 1) * HD]
            values = qkv_ref[block, 2 * quarter + h * HD : 2 * quarter + (h + 1) * HD]
            scores = jnp.where(allowed, dot_rt(query, keys) * HD ** (-0.5), -1e30)
            expo = jnp.exp(scores - jnp.max(scores, axis=-1, keepdims=True))
            probs = expo / jnp.sum(expo, axis=-1, keepdims=True)
            p_ref[b * (quarter // HD) + h] = probs
            o_ref[b, :, h * HD : (h + 1) * HD] = dot(probs.astype(BF), values).astype(BF)


def middle(size, rows, width, scal, *refs):
    blocks = refs[:4]
    o_own, o_far, w_own, w_far, near_ref = refs[4:9]
    full = 4 * rows
    outputs = (
        lambda b: o_own[b],
        lambda b: near_ref[b * rows : (b + 1) * rows],
        lambda b: o_far[b],
        lambda b: near_ref[full + b * rows : full + (b + 1) * rows],
    )
    weights = (w_own, near_ref.at[2 * full : 2 * full + width], w_far, near_ref.at[2 * full + width :])
    x2_ref, h2_ref, o_ref, rows_ref, w_full = refs[9:]
    quarter = width // 4
    members = [scal[2 * size + 1 + m] for m in range(4)]
    for m in range(4):
        w_full[:, lanes(members[m] * quarter, quarter)] = weights[m][...]
        for b in range(4):
            o_ref[b * rows : (b + 1) * rows, lanes(members[m] * quarter, quarter)] = outputs[m](BLOCKS[m][b])
    rows_ref[...] = w_full[pl.ds(pl.multiple_of(members[0] * quarter, quarter), quarter), :]
    for j in range(4):
        columns = slice(j * quarter, (j + 1) * quarter)
        added = dot(o_ref[...], w_full[:, columns])
        for b in range(4):
            x2_ref[b * rows : (b + 1) * rows, columns] = blocks[b][:rows, columns].astype(F32) + added[b * rows : (b + 1) * rows, :]
    for b in range(4):
        block = slice(b * rows, (b + 1) * rows)
        normed, _ = norm_rows(x2_ref[block, :])
        h2_ref[block, :] = normed.astype(BF)


def hidden_units(size, shard_rows, members_units, n_chunks, scal, h2_ref, *refs):
    chunks = refs[:n_chunks]
    up_ref, gate_ref, hid_ref, w_ref = refs[n_chunks:]

    def put(row, value):
        w_ref[pl.ds(row, shard_rows), :] = value

    place_rows(size, shard_rows, scal, chunks, put)
    main = main_part(members_units)
    rest = members_units - main

    def put_units(columns, up, gate):
        up_ref[:, columns] = up
        gate_ref[:, columns] = gate
        hid_ref[:, columns] = (gate * jax.nn.sigmoid(gate) * up).astype(BF)

    for at, tile in tiles_of(main):
        up = dot(h2_ref[...], w_ref[:, at : at + tile])
        put_units(slice(at, at + tile), up, dot(h2_ref[...], w_ref[:, main + at : main + at + tile]))
    if rest:
        both = dot(h2_ref[...], w_ref[:, 2 * main :])
        put_units(slice(main, members_units), both[:, :rest], both[:, rest:])


def hidden_back(size, rows, padded, piece, n_chunks, scal, *refs):
    gm_ref = refs[0]
    chunks = refs[1 : 1 + n_chunks]
    up_ref, gate_ref, w_in, ggu_ref, keep_ref, give_ref, down_ref = refs[1 + n_chunks :]
    units = up_ref.shape[1]
    width = gm_ref.shape[1]
    if padded > piece:
        down_ref[...] = jnp.zeros_like(down_ref)

    def store(chip, first, value):
        down_ref[pl.ds(pl.multiple_of(chip * padded + first, ROWS), value.shape[0]), :] = value

    place_chunks(size, scal, chunks, store)
    tile = 256

    main = main_part(units)
    rest = units - main
    pieces = [(at, size_, at, main + at) for at, size_ in tiles_of(main)]
    if rest:
        pieces.append((main, rest, 2 * main, 2 * main + rest))
    for at, count, up_at, gate_at in pieces:
        grad = dot_rt(gm_ref[...], down_ref[at : at + count, :])
        up = up_ref[:, at : at + count]
        gate = gate_ref[:, at : at + count]
        sig = jax.nn.sigmoid(gate)
        ggu_ref[:, up_at : up_at + count] = (grad * (gate * sig)).astype(BF)
        ggu_ref[:, gate_at : gate_at + count] = (grad * up * (sig * (1.0 + gate * (1.0 - sig)))).astype(BF)

    @pl.loop(0, width // tile)
    def _(i):
        at = pl.multiple_of(i * tile, tile)
        back = dot_rt(ggu_ref[...], w_in[pl.ds(at, tile), :])
        share(back, rows, keep_ref, give_ref, pl.ds(at, tile))


def share(partial, rows, keep_ref, give_ref, columns):
    keep_ref[0, :, columns] = partial[:rows]
    give_ref[0, :, columns] = partial[rows : 2 * rows].astype(BF)
    keep_ref[1, :, columns] = partial[2 * rows : 3 * rows]
    give_ref[1, :, columns] = partial[3 * rows :].astype(BF)


def last_projection(rows, scal, hid_ref, down_ref, keep_ref, give_ref):
    tile = 256

    @pl.loop(0, down_ref.shape[1] // tile)
    def _(i):
        columns = pl.ds(pl.multiple_of(i * tile, tile), tile)
        share(dot(hid_ref[...], down_ref[:, columns]), rows, keep_ref, give_ref, columns)


def write_parts(size, stride, scal, total, refs):
    for k, ref in enumerate(refs):
        ref[...] = total[pl.ds(pl.multiple_of(scal[k] * stride, ROWS), ref.shape[0]), :].astype(BF)


def grad_down_parts(size, rows, padded, scal, hid_ref, *refs):
    gm_ref, total = refs[-2:]
    for b in range(4):
        gm_ref[b * rows : (b + 1) * rows, :] = refs[b][...]
    tile = 256

    @pl.loop(0, gm_ref.shape[1] // tile)
    def _(i):
        columns = pl.ds(pl.multiple_of(i * tile, tile), tile)
        total[:, columns] = dot_lt(hid_ref[...], gm_ref[:, columns])

    write_parts(size, padded, scal, total, refs[4:-2])


def grad_in_parts(size, double, scal, h2_ref, ggu_ref, *refs):
    total = refs[-1]
    for at, tile in tiles_of(ggu_ref.shape[1]):
        total[:, at : at + tile] = dot_lt(h2_ref[...], ggu_ref[:, at : at + tile])
    write_parts(size, double, scal, total, refs[:-1])


def middle_back(rows, scal, keep_ref, got_ref, far_first, far_second, x2_ref, cot_own, cot_far, gx2_ref, ga_ref):
    for i, cot in ((0, cot_own), (1, cot_far)):
        upstream = keep_ref[i] + got_ref[i].astype(F32) + (far_second, far_first)[i][...].astype(F32)
        normed, inverse = norm_rows(x2_ref[2 * i * rows : (2 * i + 1) * rows, :])
        total = cot[...].astype(F32) + norm_back(normed, inverse, upstream)
        if i == 0:
            gx2_ref[...] = total
        ga_ref[i] = total.astype(BF)


def attention_back(rows, width, scal, ga_own, ga_near, out_rows, qkv_ref, p_ref, w_ref, cos_ref, sin_ref, gqkv_ref, ga_ref, keep_ref, give_ref, go_ref, grad_ref):
    quarter = width // 4
    for b, value in enumerate((ga_own[0], ga_near[0], ga_own[1], ga_near[1])):
        ga_ref[b * rows : (b + 1) * rows, :] = value
    go_ref[...] = dot_rt(ga_ref[...], out_rows[...]).astype(BF)
    for b in range(4):
        block = slice(b * rows, (b + 1) * rows)
        for h in range(quarter // HD):
            head = slice(h * HD, (h + 1) * HD)
            query = qkv_ref[block, h * HD : (h + 1) * HD]
            keys = qkv_ref[block, quarter + h * HD : quarter + (h + 1) * HD]
            values = qkv_ref[block, 2 * quarter + h * HD : 2 * quarter + (h + 1) * HD]
            probs = p_ref[b * (quarter // HD) + h]
            go = go_ref[block, head]
            dprob = dot_rt(go, values)
            centre = jnp.sum(probs * dprob, axis=-1, keepdims=True)
            dscore = (probs * (dprob - centre)).astype(BF)
            grad_ref[0, :, head] = dot(dscore, keys) * HD ** (-0.5)
            grad_ref[1, :, head] = dot_lt(dscore, query) * HD ** (-0.5)
            grad_ref[2, :, head] = dot_lt(probs.astype(BF), go)
        for j in range(3):
            grad = grad_ref[j]
            if j < 2:
                grad = grad * cos_ref[...] - turned(grad) * sin_ref[...]
            gqkv_ref[block, j * quarter : (j + 1) * quarter] = grad.astype(BF)
    for j in range(4):
        columns = slice(j * quarter, (j + 1) * quarter)
        share(dot_rt(gqkv_ref[...], w_ref[columns, :]), rows, keep_ref, give_ref, columns)


def grad_first_parts(size, double, width, scal, h1_ref, gqkv_ref, o_ref, ga_ref, *refs):
    total = refs[-1]
    quarter = width // 4
    for j in range(3):
        columns = slice(j * quarter, (j + 1) * quarter)
        total[:, columns] = dot_lt(h1_ref[...], gqkv_ref[:, columns])
    total[:, 3 * quarter :] = dot_lt(o_ref[...], ga_ref[:, lanes(scal[2 * size + 1] * quarter, quarter)])
    write_parts(size, double, scal, total, refs[:-1])


def split_rows(size, scal, own_ref, right_ref, left_ref, keep_ref, give_ref):
    core = scal[2 * size]
    rows = keep_ref.shape[0]
    for ref, first in ((keep_ref, core), (give_ref, 1 - core)):
        here = pl.ds(pl.multiple_of(first * rows, PACK), rows)
        ref[...] = (own_ref[here, :].astype(F32) + right_ref[here, :].astype(F32) + left_ref[here, :].astype(F32)).astype(BF)


def finish_tokens(rows, scal, keep_ref, got_ref, far_ref, block_ref, gx2_ref, out_ref):
    upstream = keep_ref[0] + got_ref[0].astype(F32) + far_ref[...].astype(F32)
    normed, inverse = norm_rows(block_ref[:rows, :].astype(F32))
    out_ref[...] = gx2_ref[...] + norm_back(normed, inverse, upstream)


def unpack_down(size, piece, scal, low_ref, other_ref, out_ref):
    rep = scal[2 * size + 1] - 2 * scal[2 * size]
    for r in range(2):

        @pl.when(rep == r)
        def _(r=r):
            out_ref[r * piece : (r + 1) * piece, :] = low_ref[...].astype(F32)
            out_ref[(1 - r) * piece : (2 - r) * piece, :] = other_ref[...].astype(F32)


def unpack_first(size, width, scal, own_ref, near_ref, far_ref, diagonal_ref, qkv_ref, out_ref):
    quarter = width // 4
    for m, ref in enumerate((own_ref, near_ref, far_ref, diagonal_ref)):
        value = ref[...].astype(F32)
        at = scal[2 * size + 1 + m] * quarter
        for j in range(3):
            qkv_ref[:, lanes(j * width + at, quarter)] = value[:, j * quarter : (j + 1) * quarter]
        out_ref[:, lanes(at, quarter)] = value[:, 3 * quarter :]


def unpack_in(size, units, piece, padded, scal, own_ref, near_ref, far_ref, diagonal_ref, in_ref, held):
    for m, ref in enumerate((own_ref, near_ref, far_ref, diagonal_ref)):
        held[scal[2 * size + 1 + m]] = ref[...].astype(F32)
    for q in range(4):
        for g, offset, length, columns in runs(size, padded, piece):
            for part in range(2):
                start = part * units + (g * 4 + q) * piece + offset
                in_ref[:, start : start + length] = held[q, :, columns[part] : columns[part] + length]


def local(tokens, prefix, qkv_weight, out_weight, in_weight, down_weight, cotangent):
    micro, _, length, width = tokens.shape
    rows = micro * length
    size = lax.axis_size("ring")
    ring = Ring(size)
    rep = lax.axis_index("rep")
    core = lax.axis_index("core")
    shard_rows = qkv_weight.shape[0]
    double = 2 * shard_rows
    units = in_weight.shape[1] // 2
    quarter = width // 4
    heads = quarter // HD
    piece = units // (4 * size)
    padded = -(-piece // ROWS) * ROWS
    while 2 * size * padded % LANES:
        padded += ROWS
    member_units = size * padded
    chunks = size + 1
    table = scalar_table(size)
    scal = lax.dynamic_slice(
        jnp.asarray(table.reshape(-1, table.shape[-1])), ((rep * size + lax.axis_index("ring")) * 2 + core, 0), (1, table.shape[-1])
    )[0]

    position = np.arange(length, dtype=np.float32)[:, None]
    frequency = np.float32(10000.0) ** (-np.arange(0, HD, 2, dtype=np.float32) / np.float32(HD))
    angles = (position * frequency[None, :]).astype(np.float32)
    angles = np.concatenate([angles, angles], axis=-1)
    sign = np.where(np.arange(HD) < HALF, -1.0, 1.0).astype(np.float32)
    cosine = jnp.asarray(np.tile(np.cos(angles), (micro, heads)).astype(np.float32))
    sine = jnp.asarray(np.tile(np.sin(angles) * sign, (micro, heads)).astype(np.float32))

    full_rows = 4 * rows
    pair_low = shape((2, rows, width), BF)
    pair_full = shape((2, rows, width), F32)
    project = 2 * full_rows * width * quarter

    tokens = tokens.reshape(rows, width)
    cot_own = cotangent.reshape(rows, width)
    a_own, a_sib = call(
        functools.partial(pack_first, size, width),
        [shape((shard_rows, width), BF)] * 2,
        [pltpu.SemaphoreType.DMA((8,))],
        0,
        scal,
        qkv_weight,
        out_weight,
        still=2,
    )
    a = Gather(ring, jnp.concatenate([a_own, sibling(a_sib)], axis=0))

    a.state, in_weight, tokens = sync(a.state, in_weight, tokens)
    a.advance()
    b_own, b_sib, down_rows = call(
        functools.partial(pack_in, size, units, piece, padded),
        [shape((shard_rows, 2 * member_units), BF)] * 2 + [shape((piece, width), BF)],
        [],
        0,
        scal,
        in_weight,
        down_weight,
    )
    c = Gather(ring, down_rows)
    c.advance()
    b_got = sibling(b_sib)
    (own,) = call(functools.partial(pack_tokens, rows), [shape((rows + micro, width), BF)], [], 0, prefix, tokens, smem=0)
    near = sibling(own)

    a.state, own, b_own, b_got, near = sync(a.state, own, b_own, b_got, near)
    a.advance()
    far = across(own)
    b = Gather(ring, jnp.concatenate([b_own, b_got], axis=0))

    (a.state,) = sync(a.state)
    a.advance()
    far, cot_own, b.state, c.state = sync(far, cot_own, b.state, c.state)
    cot_far = across(cot_own)
    b.advance()

    while a.step < ring.half - 1:
        (a.state,) = sync(a.state)
        a.advance()
    a.state, far, cot_far = sync(a.state, far, cot_far)
    a_chunks = a.finish()
    diagonal = sibling(far)

    a_chunks, b.state, c.state, diagonal = sync(a_chunks, b.state, c.state, diagonal)
    blocks = [own, near, far, diagonal]
    b.advance()
    c.advance()
    (out_mine,) = call(functools.partial(gather_out, size, shard_rows, quarter), [shape((width, quarter), BF)], [], 0, scal, *a_chunks)
    out_far = across(out_mine)
    o_own, h1, qkv, probs, qkv_mine = call(
        functools.partial(attention, size, shard_rows, rows, length, width, chunks),
        [
            shape((4, rows, quarter), BF),
            shape((full_rows, width), BF),
            shape((full_rows, 3 * quarter), BF),
            shape((4 * heads, rows, rows), F32),
            shape((width, 3 * quarter), BF),
        ],
        [],
        3 * project,
        scal,
        *blocks,
        *a_chunks,
        cosine,
        sine,
    )

    o_own, out_mine, b.state, c.state = sync(o_own, out_mine, b.state, c.state)
    o_far = across(o_own)
    b.advance()
    c.advance()

    o_far, out_far, b.state, c.state = sync(o_far, out_far, b.state, c.state)
    kept = [o_own.reshape(full_rows, quarter), o_far.reshape(full_rows, quarter), out_mine, out_far]
    near_all = sibling(jnp.concatenate(kept, axis=0))
    b_chunks = b.finish()
    c_chunks = c.finish()
    x2, h2, o_all, out_rows = call(
        functools.partial(middle, size, rows, width),
        [
            shape((full_rows, width), F32),
            shape((full_rows, width), BF),
            shape((full_rows, width), BF),
            shape((quarter, width), BF),
        ],
        [pltpu.VMEM((width, width), BF)],
        4 * project,
        scal,
        *blocks,
        o_own,
        o_far,
        out_mine,
        out_far,
        near_all,
    )

    h2, b_chunks, c_chunks, cot_own, cot_far = sync(h2, b_chunks, c_chunks, cot_own, cot_far)
    cot_near = sibling(cot_own)
    cot_diagonal = sibling(cot_far)
    up, gate, hid, in_mine = call(
        functools.partial(hidden_units, size, shard_rows, member_units, chunks),
        [
            shape((full_rows, member_units), F32),
            shape((full_rows, member_units), F32),
            shape((full_rows, member_units), BF),
            shape((width, 2 * member_units), BF),
        ],
        [],
        6 * project,
        scal,
        h2,
        *b_chunks,
    )
    hid, cot_near, cot_diagonal = sync(hid, cot_near, cot_diagonal)
    *down_parts, gm = call(
        functools.partial(grad_down_parts, size, rows, padded),
        [shape((piece, width), BF)] * size + [shape((full_rows, width), BF)],
        [pltpu.VMEM((member_units, width), F32)],
        3 * project,
        scal,
        hid,
        cot_own,
        cot_near,
        cot_far,
        cot_diagonal,
    )

    c = Scatter(ring, down_parts)
    c.state, gm, up, c_chunks = sync(c.state, gm, up, c_chunks)
    c.send()
    ggu, u2_keep, u2_give, down_mine = call(
        functools.partial(hidden_back, size, rows, padded, piece, chunks),
        [shape((full_rows, 2 * member_units), BF), pair_full, pair_low, shape((member_units, width), BF)],
        [],
        9 * project,
        scal,
        gm,
        *c_chunks,
        up,
        gate,
        in_mine,
    )

    u2_give, c.got = sync(u2_give, c.got)
    u2_got = sibling(u2_give)
    c.add()
    c.send()
    u2_low = (u2_keep + u2_got.astype(F32)).astype(BF)

    u2_low, ggu = sync(u2_low, ggu)
    u2_first = across(u2_low[0])
    in_parts = call(
        functools.partial(grad_in_parts, size, double),
        [shape((double, 2 * member_units), BF)] * size,
        [pltpu.VMEM((width, 2 * member_units), F32)],
        6 * project,
        scal,
        h2,
        ggu,
    )

    b = Scatter(ring, in_parts)
    b.state, c.got = sync(b.state, c.got)
    b.send()
    c.add()
    c.state, u2_first, u2_low, hid = sync(c.state, u2_first, u2_low, hid)
    c.send()
    u2_second = across(u2_low[1])
    y_keep, y_give = call(functools.partial(last_projection, rows), [pair_full, pair_low], [], 3 * project, scal, hid, down_mine)

    y_give, c.got, b.got, u2_second = sync(y_give, c.got, b.got, u2_second)
    b.add()
    b.send()
    c.add()
    c.send()
    gx2, ga = call(
        functools.partial(middle_back, rows),
        [shape((rows, width), F32), pair_low],
        [],
        0,
        scal,
        u2_keep,
        u2_got,
        u2_first,
        u2_second,
        x2,
        cot_own,
        cot_far,
    )
    ga_near = sibling(ga)
    gqkv, ga_all, u1_keep, u1_give = call(
        functools.partial(attention_back, rows, width),
        [shape((full_rows, 3 * quarter), BF), shape((full_rows, width), BF), pair_full, pair_low],
        [pltpu.VMEM((full_rows, quarter), BF), pltpu.VMEM((3, rows, quarter), F32)],
        7 * project,
        scal,
        ga,
        ga_near,
        out_rows,
        qkv,
        probs,
        qkv_mine,
        cosine,
        sine,
    )

    gqkv, u1_give, b.got = sync(gqkv, u1_give, b.got)
    b.add()
    b.send()
    u1_got = sibling(u1_give)
    first_parts = call(
        functools.partial(grad_first_parts, size, double, width),
        [shape((double, width), BF)] * size,
        [pltpu.VMEM((width, width), F32)],
        4 * project,
        scal,
        h1,
        gqkv,
        o_all,
        ga_all,
    )
    down_low = sum(v.astype(F32) for v in c.run()).astype(BF)

    a = Scatter(ring, first_parts)
    a.state, u1_got, down_low = sync(a.state, u1_got, down_low)
    a.send()
    u1_low = (u1_keep[1] + u1_got[1].astype(F32)).astype(BF)
    u1_far = across(u1_low)

    a.got, b.got, u1_far, y_give = sync(a.got, b.got, u1_far, y_give)
    a.add()
    a.send()
    b.add()
    b.send()
    down_other = across(down_low)
    y_got = sibling(y_give)

    (grad_tokens,) = call(
        functools.partial(finish_tokens, rows), [shape((rows, width), F32)], [], 0, scal, u1_keep, u1_got, u1_far, own, gx2
    )
    while a.step < ring.half - 2:
        a.got, down_other, grad_tokens = sync(a.got, down_other, grad_tokens)
        a.add()
        a.send()
    y_low = (y_keep[1] + y_got[1].astype(F32)).astype(BF)
    y_far = across(y_low)

    def halves(summed):
        columns = summed[0].shape[1]
        return call(functools.partial(split_rows, size), [shape((shard_rows, columns), BF)] * 2, [], 0, scal, *summed)

    in_keep, in_give = halves(b.run())
    in_near = sibling(in_give)
    a.got, in_keep, in_near, y_far = sync(a.got, in_keep, in_near, y_far)
    a.add()
    a.send()
    in_far = across(in_keep)
    in_diagonal = across(in_near)
    first_keep, first_give = halves(a.run())
    first_keep, first_give, in_far = sync(first_keep, first_give, in_far)
    first_far = across(first_keep)
    first_near = sibling(first_give)
    first_diagonal = across(first_near)
    y_far, down_other, in_keep, first_near = sync(y_far, down_other, in_keep, first_near)
    result = (x2[:rows] + (y_keep[0] + y_got[0].astype(F32) + y_far.astype(F32))).astype(BF)
    (grad_down,) = call(functools.partial(unpack_down, size, piece), [shape((2 * piece, width), F32)], [], 0, scal, down_low, down_other)
    (grad_in,) = call(
        functools.partial(unpack_in, size, units, piece, padded),
        [shape((shard_rows, 2 * units), F32)],
        [pltpu.VMEM((4, shard_rows, 2 * member_units), F32)],
        0,
        scal,
        in_keep,
        in_near,
        in_far,
        in_diagonal,
    )
    grad_qkv, grad_out = call(
        functools.partial(unpack_first, size, width),
        [shape((shard_rows, 3 * width), F32), shape((shard_rows, width), F32)],
        [],
        0,
        scal,
        first_keep,
        first_near,
        first_far,
        first_diagonal,
    )
    return (
        result.reshape(micro, 1, length, width),
        grad_tokens.reshape(micro, 1, length, width),
        grad_qkv,
        grad_out,
        grad_in,
        grad_down,
    )


def solution(mesh):
    inner = Mesh(mesh.devices.reshape(mesh.shape["rep"], mesh.shape["shard"] // 2, 2), ("rep", "ring", "core"))
    everyone = ("rep", "ring", "core")
    group = ("ring", "core")
    sequences = P(None, everyone, None, None)
    weights = P(group, None)
    return jax.shard_map(
        local,
        mesh=inner,
        in_specs=(sequences, P(None, everyone), weights, weights, weights, weights, sequences),
        out_specs=(sequences, sequences, weights, weights, weights, weights),
        check_vma=False,
    )
```

```python
import functools

import jax
import jax.numpy as jnp
import numpy as np
from jax import lax
from jax.experimental import pallas as pl
from jax.experimental.pallas import tpu as pltpu
from jax.sharding import Mesh, PartitionSpec as P

H = 16
HD = 64
HALF = HD // 2
LANES = 128
PACK = 16
ROWS = 8
BF = jnp.bfloat16
F32 = jnp.float32
SWAP = ((0, 1), (1, 0))
MIB = 1 << 20
WEIGHT = {'ring_add': 16000000000, 'unpack_in': 4000000000, 'pack_in': 1000000000, 'hidden_back': 32000000000, 'grad_first_parts': 32000000000, 'middle_back': 4000000000, 'hidden_units': 16000000000, 'last_projection': 4000000000}
BLOCKS = ((0, 1, 2, 3), (1, 0, 3, 2), (2, 3, 0, 1), (3, 2, 1, 0))


def dot(left, right):
    return jnp.dot(left, right, preferred_element_type=F32)


def dot_rt(left, right):
    return lax.dot_general(left, right, (((1,), (1,)), ((), ())), preferred_element_type=F32)


def dot_lt(left, right):
    return lax.dot_general(left, right, (((0,), (0,)), ((), ())), preferred_element_type=F32)


def norm_rows(values):
    centre = values - jnp.mean(values, axis=-1, keepdims=True)
    inverse = lax.rsqrt(jnp.mean(centre * centre, axis=-1, keepdims=True) + 1e-05)
    return (centre * inverse, inverse)


def norm_back(normed, inverse, upstream):
    return inverse * (
        upstream
        - jnp.mean(upstream, axis=-1, keepdims=True)
        - normed * jnp.mean(upstream * normed, axis=-1, keepdims=True)
    )


def across(value):
    return lax.ppermute(value, "rep", SWAP)


def sibling(value):
    return lax.ppermute(value, "core", SWAP)


def order_of(size):
    return list(range(0, size, 2)) + list(range(size - 1, 0, -2))


def scalar_table(size):
    order = order_of(size)
    place = np.argsort(order)
    table = np.zeros((2, size, 2, 2 * size + 5), np.int32)
    for rep in range(2):
        for g in range(size):
            for core in range(2):
                at = [order[(place[g] + k) % size] for k in range(size)]
                of = [(place[o] - place[g]) % size for o in range(size)]
                members = [2 * core + rep, 2 * (1 - core) + rep, 2 * core + 1 - rep, 2 * (1 - core) + 1 - rep]
                table[rep, g, core] = at + of + [core] + members
    return table


def upper_half(rows):
    return -(-(rows // 2) // PACK) * PACK


class Ring:
    def __init__(self, size):
        self.size = size
        self.half = size // 2
        order = order_of(size)
        self.right = [(order[i], order[(i + 1) % size]) for i in range(size)]
        self.left = [(b, a) for a, b in self.right]

    def exchange(self, pair):
        return lax.ppermute(pair[0], "ring", self.right), lax.ppermute(pair[1], "ring", self.left)


class Gather:
    def __init__(self, ring, chunk):
        self.ring = ring
        self.step = 0
        self.got = {0: chunk}
        self.cut = upper_half(chunk.shape[0])
        self.state = (chunk, chunk)

    def advance(self):
        if self.step == self.ring.half:
            return
        self.step += 1
        if self.step == self.ring.half:
            self.far = self.ring.exchange((self.state[0][: self.cut], self.state[1][self.cut :]))
            self.state = ()
            return
        self.state = self.ring.exchange(self.state)
        self.got[self.ring.size - self.step], self.got[self.step] = self.state

    def finish(self):
        while self.step < self.ring.half:
            self.advance()
        return [self.got[k] for k in range(self.ring.size) if k != self.ring.half] + list(self.far)


def ring_add(cut, right_term, left_term, right_got, left_got, right_ref, left_ref):
    if cut is None:
        right_ref[...] = (right_term[...].astype(F32) + right_got[...].astype(F32)).astype(BF)
        left_ref[...] = (left_term[...].astype(F32) + left_got[...].astype(F32)).astype(BF)
    else:
        right_ref[:cut] = (right_term[:cut].astype(F32) + right_got[...].astype(F32)).astype(BF)
        right_ref[cut:] = right_term[cut:]
        left_ref[:cut] = left_term[:cut]
        left_ref[cut:] = (left_term[cut:].astype(F32) + left_got[...].astype(F32)).astype(BF)


class Scatter:
    def __init__(self, ring, parts):
        self.ring = ring
        self.step = 0
        self.parts = parts
        self.cut = upper_half(parts[0].shape[0])
        far = parts[ring.half]
        self.state = (far[: self.cut], far[self.cut :])

    def send(self):
        self.got = self.ring.exchange(self.state)

    def add(self):
        ring = self.ring
        self.step += 1
        place = ring.half - self.step
        terms = (self.parts[place], self.parts[ring.size - place])
        body = functools.partial(ring_add, self.cut if self.step == 1 else None)
        self.state = tuple(call(body, [shape(t.shape, BF) for t in terms], [], 16000000000, *terms, *self.got, smem=0))

    def run(self):
        while self.step < self.ring.half - 1:
            self.add()
            self.send()
        return self.parts[0], *self.got


def sync(*values):
    return lax.optimization_barrier(values)


def call(body, outs, scratch, flops, *args, smem=1, still=0):
    nbytes = sum(a.size * a.dtype.itemsize for a in args) + sum(o.size * o.dtype.itemsize for o in outs)
    spaces = [pltpu.SMEM] * smem + [pl.ANY] * still + [pltpu.VMEM] * (len(args) - smem - still)
    return pl.pallas_call(
        body,
        name=body.func.__name__,
        out_shape=outs,
        in_specs=[pl.BlockSpec(memory_space=space) for space in spaces],
        out_specs=[pl.BlockSpec(memory_space=pltpu.VMEM)] * len(outs),
        scratch_shapes=scratch,
        compiler_params=pltpu.CompilerParams(vmem_limit_bytes=12 * MIB),
        cost_estimate=pl.CostEstimate(flops=WEIGHT.get(body.func.__name__, flops), bytes_accessed=nbytes, transcendentals=0),
    )(*args)


def shape(dims, dtype):
    return jax.ShapeDtypeStruct(dims, dtype)


def lanes(start, size):
    return pl.ds(pl.multiple_of(start, LANES), size)


def tiles_of(extent, tile=256):
    return [(at, min(tile, extent - at)) for at in range(0, extent, tile)]


def main_part(units):
    return units // LANES * LANES


def runs(size, stride, piece):
    units = size * stride
    main = main_part(units)
    rest = units - main
    for g in range(size):
        first = g * stride
        for low, high in ((first, min(first + piece, main)), (max(first, main), first + piece)):
            if low < high:
                columns = tuple(p * main + low if low < main else 2 * main + p * rest + low - main for p in range(2))
                yield g, low - first, high - low, columns


def pack_tokens(rows, prefix_ref, tokens_ref, own_ref):
    own_ref[:rows, :] = tokens_ref[...]
    for m in range(own_ref.shape[0] - rows):
        own_ref[rows + m : rows + m + 1, :] = jnp.broadcast_to(prefix_ref[m : m + 1, :].astype(F32), (1, own_ref.shape[1])).astype(BF)


def pack_first(size, width, scal, qkv_ref, out_ref, own_ref, sib_ref, sems):
    quarter = width // 4
    copies = []
    for ref, member in ((own_ref, scal[2 * size + 1]), (sib_ref, scal[2 * size + 2])):
        for j in range(4):
            source = qkv_ref.at[:, lanes(j * width + member * quarter, quarter)] if j < 3 else out_ref.at[:, lanes(member * quarter, quarter)]
            copies.append(pltpu.make_async_copy(source, ref.at[:, j * quarter : (j + 1) * quarter], sems.at[len(copies)]))
            copies[-1].start()
    for copy in copies:
        copy.wait()


def pack_in(size, units, piece, padded, scal, in_ref, down_ref, own_ref, sib_ref, rows_ref):
    rep = scal[2 * size + 1] - 2 * scal[2 * size]
    for r in range(2):

        @pl.when(rep == r)
        def _(r=r):
            rows_ref[...] = down_ref[r * piece : (r + 1) * piece, :]

    for ref, member in ((own_ref, scal[2 * size + 1]), (sib_ref, scal[2 * size + 2])):
        if padded > piece:
            ref[...] = jnp.zeros_like(ref)
        for q in range(4):

            @pl.when(member == q)
            def _(ref=ref, q=q):
                for g, offset, length, columns in runs(size, padded, piece):
                    for part in range(2):
                        start = part * units + (g * 4 + q) * piece + offset
                        ref[:, columns[part] : columns[part] + length] = in_ref[:, start : start + length]


def place_chunks(size, scal, chunk_refs, store):
    half = size // 2
    places = [k for k in range(size) if k != half]
    for k, ref in zip(places, chunk_refs, strict=False):
        store(scal[k], 0, ref[...])
    top, bottom = chunk_refs[-2:]
    store(scal[half], 0, top[...])
    store(scal[half], top.shape[0], bottom[...])


def place_rows(size, shard_rows, scal, chunk_refs, put):
    core = scal[2 * size]

    def store(chip, first, value):
        for lower in range(2):
            begin = lower * shard_rows - first
            if begin < 0 or begin >= value.shape[0]:
                continue
            row = chip * (2 * shard_rows) + (core if lower == 0 else 1 - core) * shard_rows
            put(pl.multiple_of(row, PACK), value[begin : begin + shard_rows])

    place_chunks(size, scal, chunk_refs, store)


def turned(values):
    lane = lax.broadcasted_iota(jnp.int32, values.shape, 1) % HD
    wide = values.shape[1]
    return jnp.where(lane < HALF, pltpu.roll(values, wide - HALF, 1), pltpu.roll(values, HALF, 1))


def visible(rows, length, limits):
    query = lax.broadcasted_iota(jnp.int32, (rows, rows), 0)
    key = lax.broadcasted_iota(jnp.int32, (rows, rows), 1)
    inside = (key % length).astype(F32)
    limit = jnp.zeros((rows, rows), F32)
    for s in range(rows // length):
        limit = jnp.where(key // length == s, limits[s : s + 1, :rows].astype(F32), limit)
    return (query // length == key // length) & ((key <= query) | (inside < limit))


def gather_out(size, shard_rows, quarter, scal, *refs):
    out_ref = refs[-1]

    def put(row, value):
        out_ref[pl.ds(row, shard_rows), :] = value[:, 3 * quarter :]

    place_rows(size, shard_rows, scal, refs[:-1], put)


def attention(size, shard_rows, rows, length, width, n_chunks, scal, *refs):
    blocks = refs[:4]
    chunks = refs[4 : 4 + n_chunks]
    cos_ref, sin_ref, o_ref, h1_ref, qkv_ref, p_ref, w_ref = refs[4 + n_chunks :]
    quarter = width // 4

    def put(row, value):
        w_ref[pl.ds(row, shard_rows), :] = value[:, : 3 * quarter]

    place_rows(size, shard_rows, scal, chunks, put)
    for b in range(4):
        normed, _ = norm_rows(blocks[b][:rows, :].astype(F32))
        h1_ref[b * rows : (b + 1) * rows, :] = normed.astype(BF)
    for j in range(3):
        mixed = dot(h1_ref[...], w_ref[:, j * quarter : (j + 1) * quarter])
        for b in range(4):
            piece = mixed[b * rows : (b + 1) * rows, :]
            if j < 2:
                piece = piece * cos_ref[...] + turned(piece) * sin_ref[...]
            qkv_ref[b * rows : (b + 1) * rows, j * quarter : (j + 1) * quarter] = piece.astype(BF)
    for b in range(4):
        allowed = visible(rows, length, blocks[b][rows:, :])
        block = slice(b * rows, (b + 1) * rows)
        for h in range(quarter // HD):
            query = qkv_ref[block, h * HD : (h + 1) * HD]
            keys = qkv_ref[block, quarter + h * HD : quarter + (h + 1) * HD]
            values = qkv_ref[block, 2 * quarter + h * HD : 2 * quarter + (h + 1) * HD]
            scores = jnp.where(allowed, dot_rt(query, keys) * HD ** (-0.5), -1e30)
            expo = jnp.exp(scores - jnp.max(scores, axis=-1, keepdims=True))
            probs = expo / jnp.sum(expo, axis=-1, keepdims=True)
            p_ref[b * (quarter // HD) + h] = probs
            o_ref[b, :, h * HD : (h + 1) * HD] = dot(probs.astype(BF), values).astype(BF)


def middle(size, rows, width, scal, *refs):
    blocks = refs[:4]
    o_own, o_far, w_own, w_far, near_ref = refs[4:9]
    full = 4 * rows
    outputs = (
        lambda b: o_own[b],
        lambda b: near_ref[b * rows : (b + 1) * rows],
        lambda b: o_far[b],
        lambda b: near_ref[full + b * rows : full + (b + 1) * rows],
    )
    weights = (w_own, near_ref.at[2 * full : 2 * full + width], w_far, near_ref.at[2 * full + width :])
    x2_ref, h2_ref, o_ref, rows_ref, w_full = refs[9:]
    quarter = width // 4
    members = [scal[2 * size + 1 + m] for m in range(4)]
    for m in range(4):
        w_full[:, lanes(members[m] * quarter, quarter)] = weights[m][...]
        for b in range(4):
            o_ref[b * rows : (b + 1) * rows, lanes(members[m] * quarter, quarter)] = outputs[m](BLOCKS[m][b])
    rows_ref[...] = w_full[pl.ds(pl.multiple_of(members[0] * quarter, quarter), quarter), :]
    for j in range(4):
        columns = slice(j * quarter, (j + 1) * quarter)
        added = dot(o_ref[...], w_full[:, columns])
        for b in range(4):
            x2_ref[b * rows : (b + 1) * rows, columns] = blocks[b][:rows, columns].astype(F32) + added[b * rows : (b + 1) * rows, :]
    for b in range(4):
        block = slice(b * rows, (b + 1) * rows)
        normed, _ = norm_rows(x2_ref[block, :])
        h2_ref[block, :] = normed.astype(BF)


def hidden_units(size, shard_rows, members_units, n_chunks, scal, h2_ref, *refs):
    chunks = refs[:n_chunks]
    up_ref, gate_ref, hid_ref, w_ref = refs[n_chunks:]

    def put(row, value):
        w_ref[pl.ds(row, shard_rows), :] = value

    place_rows(size, shard_rows, scal, chunks, put)
    main = main_part(members_units)
    rest = members_units - main

    def put_units(columns, up, gate):
        up_ref[:, columns] = up
        gate_ref[:, columns] = gate
        hid_ref[:, columns] = (gate * jax.nn.sigmoid(gate) * up).astype(BF)

    for at, tile in tiles_of(main):
        up = dot(h2_ref[...], w_ref[:, at : at + tile])
        put_units(slice(at, at + tile), up, dot(h2_ref[...], w_ref[:, main + at : main + at + tile]))
    if rest:
        both = dot(h2_ref[...], w_ref[:, 2 * main :])
        put_units(slice(main, members_units), both[:, :rest], both[:, rest:])


def hidden_back(size, rows, padded, piece, n_chunks, scal, *refs):
    gm_ref = refs[0]
    chunks = refs[1 : 1 + n_chunks]
    up_ref, gate_ref, w_in, ggu_ref, keep_ref, give_ref, down_ref = refs[1 + n_chunks :]
    units = up_ref.shape[1]
    width = gm_ref.shape[1]
    if padded > piece:
        down_ref[...] = jnp.zeros_like(down_ref)

    def store(chip, first, value):
        down_ref[pl.ds(pl.multiple_of(chip * padded + first, ROWS), value.shape[0]), :] = value

    place_chunks(size, scal, chunks, store)

    main = main_part(units)
    rest = units - main
    pieces = [(at, size_, at, main + at) for at, size_ in tiles_of(main)]
    if rest:
        pieces.append((main, rest, 2 * main, 2 * main + rest))
    for at, count, up_at, gate_at in pieces:
        grad = dot_rt(gm_ref[...], down_ref[at : at + count, :])
        up = up_ref[:, at : at + count]
        gate = gate_ref[:, at : at + count]
        sig = jax.nn.sigmoid(gate)
        ggu_ref[:, up_at : up_at + count] = (grad * (gate * sig)).astype(BF)
        ggu_ref[:, gate_at : gate_at + count] = (grad * up * (sig * (1.0 + gate * (1.0 - sig)))).astype(BF)

    for at, count in tiles_of(width):
        back = dot_rt(ggu_ref[...], w_in[at : at + count, :])
        share(back, rows, keep_ref, give_ref, slice(at, at + count))


def share(partial, rows, keep_ref, give_ref, columns):
    keep_ref[0, :, columns] = partial[:rows]
    give_ref[0, :, columns] = partial[rows : 2 * rows].astype(BF)
    keep_ref[1, :, columns] = partial[2 * rows : 3 * rows]
    give_ref[1, :, columns] = partial[3 * rows :].astype(BF)


def last_projection(rows, scal, hid_ref, down_ref, keep_ref, give_ref):
    for at, count in tiles_of(down_ref.shape[1]):
        columns = slice(at, at + count)
        share(dot(hid_ref[...], down_ref[:, columns]), rows, keep_ref, give_ref, columns)


def write_parts(size, stride, scal, total, refs):
    for k, ref in enumerate(refs):
        ref[...] = total[pl.ds(pl.multiple_of(scal[k] * stride, ROWS), ref.shape[0]), :].astype(BF)


def grad_down_parts(size, rows, padded, scal, hid_ref, *refs):
    gm_ref, total = refs[-2:]
    for b in range(4):
        gm_ref[b * rows : (b + 1) * rows, :] = refs[b][...]
    for at, count in tiles_of(gm_ref.shape[1]):
        columns = slice(at, at + count)
        total[:, columns] = dot_lt(hid_ref[...], gm_ref[:, columns])

    write_parts(size, padded, scal, total, refs[4:-2])


def grad_in_parts(size, double, scal, h2_ref, ggu_ref, *refs):
    total = refs[-1]
    for at, tile in tiles_of(ggu_ref.shape[1]):
        total[:, at : at + tile] = dot_lt(h2_ref[...], ggu_ref[:, at : at + tile])
    write_parts(size, double, scal, total, refs[:-1])


def middle_back(rows, scal, keep_ref, got_ref, far_first, far_second, x2_ref, cot_own, cot_far, gx2_ref, ga_ref):
    for i, cot in ((0, cot_own), (1, cot_far)):
        upstream = keep_ref[i] + got_ref[i].astype(F32) + (far_second, far_first)[i][...].astype(F32)
        normed, inverse = norm_rows(x2_ref[2 * i * rows : (2 * i + 1) * rows, :])
        total = cot[...].astype(F32) + norm_back(normed, inverse, upstream)
        if i == 0:
            gx2_ref[...] = total
        ga_ref[i] = total.astype(BF)


def attention_back(rows, width, scal, ga_own, ga_near, out_rows, qkv_ref, p_ref, w_ref, cos_ref, sin_ref, gqkv_ref, ga_ref, keep_ref, give_ref, go_ref, grad_ref):
    quarter = width // 4
    for b, value in enumerate((ga_own[0], ga_near[0], ga_own[1], ga_near[1])):
        ga_ref[b * rows : (b + 1) * rows, :] = value
    go_ref[...] = dot_rt(ga_ref[...], out_rows[...]).astype(BF)
    for b in range(4):
        block = slice(b * rows, (b + 1) * rows)
        for h in range(quarter // HD):
            head = slice(h * HD, (h + 1) * HD)
            query = qkv_ref[block, h * HD : (h + 1) * HD]
            keys = qkv_ref[block, quarter + h * HD : quarter + (h + 1) * HD]
            values = qkv_ref[block, 2 * quarter + h * HD : 2 * quarter + (h + 1) * HD]
            probs = p_ref[b * (quarter // HD) + h]
            go = go_ref[block, head]
            dprob = dot_rt(go, values)
            centre = jnp.sum(probs * dprob, axis=-1, keepdims=True)
            dscore = (probs * (dprob - centre)).astype(BF)
            grad_ref[0, :, head] = dot(dscore, keys) * HD ** (-0.5)
            grad_ref[1, :, head] = dot_lt(dscore, query) * HD ** (-0.5)
            grad_ref[2, :, head] = dot_lt(probs.astype(BF), go)
        for j in range(3):
            grad = grad_ref[j]
            if j < 2:
                grad = grad * cos_ref[...] - turned(grad) * sin_ref[...]
            gqkv_ref[block, j * quarter : (j + 1) * quarter] = grad.astype(BF)
    for j in range(4):
        columns = slice(j * quarter, (j + 1) * quarter)
        share(dot_rt(gqkv_ref[...], w_ref[columns, :]), rows, keep_ref, give_ref, columns)


def grad_first_parts(size, double, width, scal, h1_ref, gqkv_ref, o_ref, ga_ref, *refs):
    total = refs[-1]
    quarter = width // 4
    for j in range(3):
        columns = slice(j * quarter, (j + 1) * quarter)
        total[:, columns] = dot_lt(h1_ref[...], gqkv_ref[:, columns])
    total[:, 3 * quarter :] = dot_lt(o_ref[...], ga_ref[:, lanes(scal[2 * size + 1] * quarter, quarter)])
    write_parts(size, double, scal, total, refs[:-1])


def split_rows(size, scal, own_ref, right_ref, left_ref, keep_ref, give_ref):
    core = scal[2 * size]
    rows = keep_ref.shape[0]
    for ref, first in ((keep_ref, core), (give_ref, 1 - core)):
        here = pl.ds(pl.multiple_of(first * rows, PACK), rows)
        ref[...] = (own_ref[here, :].astype(F32) + right_ref[here, :].astype(F32) + left_ref[here, :].astype(F32)).astype(BF)


def finish_tokens(rows, scal, keep_ref, got_ref, far_ref, block_ref, gx2_ref, out_ref):
    upstream = keep_ref[0] + got_ref[0].astype(F32) + far_ref[...].astype(F32)
    normed, inverse = norm_rows(block_ref[:rows, :].astype(F32))
    out_ref[...] = gx2_ref[...] + norm_back(normed, inverse, upstream)


def unpack_down(size, piece, scal, low_ref, other_ref, out_ref):
    rep = scal[2 * size + 1] - 2 * scal[2 * size]
    for r in range(2):

        @pl.when(rep == r)
        def _(r=r):
            out_ref[r * piece : (r + 1) * piece, :] = low_ref[...].astype(F32)
            out_ref[(1 - r) * piece : (2 - r) * piece, :] = other_ref[...].astype(F32)


def unpack_first(size, width, scal, own_ref, near_ref, far_ref, diagonal_ref, qkv_ref, out_ref):
    quarter = width // 4
    for m, ref in enumerate((own_ref, near_ref, far_ref, diagonal_ref)):
        value = ref[...].astype(F32)
        at = scal[2 * size + 1 + m] * quarter
        for j in range(3):
            qkv_ref[:, lanes(j * width + at, quarter)] = value[:, j * quarter : (j + 1) * quarter]
        out_ref[:, lanes(at, quarter)] = value[:, 3 * quarter :]


def unpack_in(size, units, piece, padded, scal, own_ref, near_ref, far_ref, diagonal_ref, in_ref, held):
    for m, ref in enumerate((own_ref, near_ref, far_ref, diagonal_ref)):
        held[scal[2 * size + 1 + m]] = ref[...].astype(F32)
    for q in range(4):
        for g, offset, length, columns in runs(size, padded, piece):
            for part in range(2):
                start = part * units + (g * 4 + q) * piece + offset
                in_ref[:, start : start + length] = held[q, :, columns[part] : columns[part] + length]


def local(tokens, prefix, qkv_weight, out_weight, in_weight, down_weight, cotangent):
    micro, _, length, width = tokens.shape
    rows = micro * length
    size = lax.axis_size("ring")
    ring = Ring(size)
    rep = lax.axis_index("rep")
    core = lax.axis_index("core")
    shard_rows = qkv_weight.shape[0]
    double = 2 * shard_rows
    units = in_weight.shape[1] // 2
    quarter = width // 4
    heads = quarter // HD
    piece = units // (4 * size)
    padded = -(-piece // ROWS) * ROWS
    while 2 * size * padded % LANES:
        padded += ROWS
    member_units = size * padded
    chunks = size + 1
    table = scalar_table(size)
    scal = lax.dynamic_slice(
        jnp.asarray(table.reshape(-1, table.shape[-1])), ((rep * size + lax.axis_index("ring")) * 2 + core, 0), (1, table.shape[-1])
    )[0]

    position = np.arange(length, dtype=np.float32)[:, None]
    frequency = np.float32(10000.0) ** (-np.arange(0, HD, 2, dtype=np.float32) / np.float32(HD))
    angles = (position * frequency[None, :]).astype(np.float32)
    angles = np.concatenate([angles, angles], axis=-1)
    sign = np.where(np.arange(HD) < HALF, -1.0, 1.0).astype(np.float32)
    cosine = jnp.asarray(np.tile(np.cos(angles), (micro, heads)).astype(np.float32))
    sine = jnp.asarray(np.tile(np.sin(angles) * sign, (micro, heads)).astype(np.float32))

    full_rows = 4 * rows
    pair_low = shape((2, rows, width), BF)
    pair_full = shape((2, rows, width), F32)
    project = 2 * full_rows * width * quarter

    tokens = tokens.reshape(rows, width)
    cot_own = cotangent.reshape(rows, width)
    a_own, a_sib = call(
        functools.partial(pack_first, size, width),
        [shape((shard_rows, width), BF)] * 2,
        [pltpu.SemaphoreType.DMA((8,))],
        0,
        scal,
        qkv_weight,
        out_weight,
        still=2,
    )
    a = Gather(ring, jnp.concatenate([a_own, sibling(a_sib)], axis=0))

    a.state, in_weight, tokens = sync(a.state, in_weight, tokens)
    a.advance()
    b_own, b_sib, down_rows = call(
        functools.partial(pack_in, size, units, piece, padded),
        [shape((shard_rows, 2 * member_units), BF)] * 2 + [shape((piece, width), BF)],
        [],
        0,
        scal,
        in_weight,
        down_weight,
    )
    c = Gather(ring, down_rows)
    c.advance()
    b_got = sibling(b_sib)
    (own,) = call(functools.partial(pack_tokens, rows), [shape((rows + micro, width), BF)], [], 0, prefix, tokens, smem=0)
    near = sibling(own)

    a.state, own, b_own, b_got, near = sync(a.state, own, b_own, b_got, near)
    a.advance()
    far = across(own)
    b = Gather(ring, jnp.concatenate([b_own, b_got], axis=0))

    (a.state,) = sync(a.state)
    a.advance()
    far, cot_own, b.state, c.state = sync(far, cot_own, b.state, c.state)
    cot_far = across(cot_own)
    b.advance()

    while a.step < ring.half - 1:
        (a.state,) = sync(a.state)
        a.advance()
    a.state, far, cot_far = sync(a.state, far, cot_far)
    a_chunks = a.finish()
    diagonal = sibling(far)

    a_chunks, b.state, c.state, diagonal = sync(a_chunks, b.state, c.state, diagonal)
    blocks = [own, near, far, diagonal]
    b.advance()
    c.advance()
    (out_mine,) = call(functools.partial(gather_out, size, shard_rows, quarter), [shape((width, quarter), BF)], [], 0, scal, *a_chunks)
    out_far = across(out_mine)
    o_own, h1, qkv, probs, qkv_mine = call(
        functools.partial(attention, size, shard_rows, rows, length, width, chunks),
        [
            shape((4, rows, quarter), BF),
            shape((full_rows, width), BF),
            shape((full_rows, 3 * quarter), BF),
            shape((4 * heads, rows, rows), F32),
            shape((width, 3 * quarter), BF),
        ],
        [],
        3 * project,
        scal,
        *blocks,
        *a_chunks,
        cosine,
        sine,
    )

    o_own, out_mine, b.state, c.state = sync(o_own, out_mine, b.state, c.state)
    o_far = across(o_own)
    b.advance()
    c.advance()

    o_far, out_far, b.state, c.state = sync(o_far, out_far, b.state, c.state)
    kept = [o_own.reshape(full_rows, quarter), o_far.reshape(full_rows, quarter), out_mine, out_far]
    near_all = sibling(jnp.concatenate(kept, axis=0))
    b_chunks = b.finish()
    c_chunks = c.finish()
    x2, h2, o_all, out_rows = call(
        functools.partial(middle, size, rows, width),
        [
            shape((full_rows, width), F32),
            shape((full_rows, width), BF),
            shape((full_rows, width), BF),
            shape((quarter, width), BF),
        ],
        [pltpu.VMEM((width, width), BF)],
        4 * project,
        scal,
        *blocks,
        o_own,
        o_far,
        out_mine,
        out_far,
        near_all,
    )

    h2, b_chunks, c_chunks, cot_own, cot_far = sync(h2, b_chunks, c_chunks, cot_own, cot_far)
    cot_near = sibling(cot_own)
    cot_diagonal = sibling(cot_far)
    up, gate, hid, in_mine = call(
        functools.partial(hidden_units, size, shard_rows, member_units, chunks),
        [
            shape((full_rows, member_units), F32),
            shape((full_rows, member_units), F32),
            shape((full_rows, member_units), BF),
            shape((width, 2 * member_units), BF),
        ],
        [],
        6 * project,
        scal,
        h2,
        *b_chunks,
    )
    hid, cot_near, cot_diagonal = sync(hid, cot_near, cot_diagonal)
    *down_parts, gm = call(
        functools.partial(grad_down_parts, size, rows, padded),
        [shape((piece, width), BF)] * size + [shape((full_rows, width), BF)],
        [pltpu.VMEM((member_units, width), F32)],
        3 * project,
        scal,
        hid,
        cot_own,
        cot_near,
        cot_far,
        cot_diagonal,
    )

    c = Scatter(ring, down_parts)
    c.state, gm, up, c_chunks = sync(c.state, gm, up, c_chunks)
    c.send()
    ggu, u2_keep, u2_give, down_mine = call(
        functools.partial(hidden_back, size, rows, padded, piece, chunks),
        [shape((full_rows, 2 * member_units), BF), pair_full, pair_low, shape((member_units, width), BF)],
        [],
        9 * project,
        scal,
        gm,
        *c_chunks,
        up,
        gate,
        in_mine,
    )

    u2_give, c.got = sync(u2_give, c.got)
    u2_got = sibling(u2_give)
    c.add()
    c.send()
    u2_low = (u2_keep + u2_got.astype(F32)).astype(BF)

    u2_low, ggu = sync(u2_low, ggu)
    u2_first = across(u2_low[0])
    in_parts = call(
        functools.partial(grad_in_parts, size, double),
        [shape((double, 2 * member_units), BF)] * size,
        [pltpu.VMEM((width, 2 * member_units), F32)],
        6 * project,
        scal,
        h2,
        ggu,
    )

    b = Scatter(ring, in_parts)
    b.state, c.got = sync(b.state, c.got)
    b.send()
    c.add()
    c.state, u2_first, u2_low, hid = sync(c.state, u2_first, u2_low, hid)
    c.send()
    u2_second = across(u2_low[1])
    y_keep, y_give = call(functools.partial(last_projection, rows), [pair_full, pair_low], [], 3 * project, scal, hid, down_mine)

    y_give, c.got, b.got, u2_second = sync(y_give, c.got, b.got, u2_second)
    b.add()
    b.send()
    c.add()
    c.send()
    gx2, ga = call(
        functools.partial(middle_back, rows),
        [shape((rows, width), F32), pair_low],
        [],
        0,
        scal,
        u2_keep,
        u2_got,
        u2_first,
        u2_second,
        x2,
        cot_own,
        cot_far,
    )
    ga_near = sibling(ga)
    gqkv, ga_all, u1_keep, u1_give = call(
        functools.partial(attention_back, rows, width),
        [shape((full_rows, 3 * quarter), BF), shape((full_rows, width), BF), pair_full, pair_low],
        [pltpu.VMEM((full_rows, quarter), BF), pltpu.VMEM((3, rows, quarter), F32)],
        7 * project,
        scal,
        ga,
        ga_near,
        out_rows,
        qkv,
        probs,
        qkv_mine,
        cosine,
        sine,
    )

    gqkv, u1_give, b.got = sync(gqkv, u1_give, b.got)
    b.add()
    b.send()
    u1_got = sibling(u1_give)
    first_parts = call(
        functools.partial(grad_first_parts, size, double, width),
        [shape((double, width), BF)] * size,
        [pltpu.VMEM((width, width), F32)],
        4 * project,
        scal,
        h1,
        gqkv,
        o_all,
        ga_all,
    )
    down_low = sum(v.astype(F32) for v in c.run()).astype(BF)

    a = Scatter(ring, first_parts)
    a.state, u1_got, down_low = sync(a.state, u1_got, down_low)
    a.send()
    u1_low = (u1_keep[1] + u1_got[1].astype(F32)).astype(BF)
    u1_far = across(u1_low)

    a.got, b.got, u1_far, y_give = sync(a.got, b.got, u1_far, y_give)
    a.add()
    a.send()
    b.add()
    b.send()
    down_other = across(down_low)
    y_got = sibling(y_give)

    (grad_tokens,) = call(
        functools.partial(finish_tokens, rows), [shape((rows, width), F32)], [], 0, scal, u1_keep, u1_got, u1_far, own, gx2
    )
    while a.step < ring.half - 2:
        a.got, down_other, grad_tokens = sync(a.got, down_other, grad_tokens)
        a.add()
        a.send()
    y_low = (y_keep[1] + y_got[1].astype(F32)).astype(BF)
    y_far = across(y_low)

    def halves(summed):
        columns = summed[0].shape[1]
        return call(functools.partial(split_rows, size), [shape((shard_rows, columns), BF)] * 2, [], 0, scal, *summed)

    in_keep, in_give = halves(b.run())
    in_near = sibling(in_give)
    a.got, in_keep, in_near, y_far = sync(a.got, in_keep, in_near, y_far)
    a.add()
    a.send()
    in_far = across(in_keep)
    in_diagonal = across(in_near)
    first_keep, first_give = halves(a.run())
    first_keep, first_give, in_far = sync(first_keep, first_give, in_far)
    first_far = across(first_keep)
    first_near = sibling(first_give)
    first_diagonal = across(first_near)
    y_far, down_other, in_keep, first_near = sync(y_far, down_other, in_keep, first_near)
    result = (x2[:rows] + (y_keep[0] + y_got[0].astype(F32) + y_far.astype(F32))).astype(BF)
    (grad_down,) = call(functools.partial(unpack_down, size, piece), [shape((2 * piece, width), F32)], [], 0, scal, down_low, down_other)
    (grad_in,) = call(
        functools.partial(unpack_in, size, units, piece, padded),
        [shape((shard_rows, 2 * units), F32)],
        [pltpu.VMEM((4, shard_rows, 2 * member_units), F32)],
        0,
        scal,
        in_keep,
        in_near,
        in_far,
        in_diagonal,
    )
    grad_qkv, grad_out = call(
        functools.partial(unpack_first, size, width),
        [shape((shard_rows, 3 * width), F32), shape((shard_rows, width), F32)],
        [],
        0,
        scal,
        first_keep,
        first_near,
        first_far,
        first_diagonal,
    )
    return (
        result.reshape(micro, 1, length, width),
        grad_tokens.reshape(micro, 1, length, width),
        grad_qkv,
        grad_out,
        grad_in,
        grad_down,
    )


def solution(mesh):
    inner = Mesh(mesh.devices.reshape(mesh.shape["rep"], mesh.shape["shard"] // 2, 2), ("rep", "ring", "core"))
    everyone = ("rep", "ring", "core")
    group = ("ring", "core")
    sequences = P(None, everyone, None, None)
    weights = P(group, None)
    return jax.shard_map(
        local,
        mesh=inner,
        in_specs=(sequences, P(None, everyone), weights, weights, weights, weights, sequences),
        out_specs=(sequences, sequences, weights, weights, weights, weights),
        check_vma=False,
    )
```

```python
import functools

import jax
import jax.numpy as jnp
import numpy as np
from jax import lax
from jax.experimental import pallas as pl
from jax.experimental.pallas import tpu as pltpu
from jax.sharding import Mesh, PartitionSpec as P

H = 16
HD = 64
HALF = HD // 2
LANES = 128
PACK = 16
ROWS = 8
BF = jnp.bfloat16
F32 = jnp.float32
SWAP = ((0, 1), (1, 0))
MIB = 1 << 20
WEIGHT = {'ring_add': 16000000000, 'unpack_in': 4000000000, 'pack_in': 1000000000, 'hidden_back': 32000000000, 'grad_first_parts': 32000000000, 'middle_back': 4000000000, 'hidden_units': 16000000000, 'last_projection': 4000000000}
BLOCKS = ((0, 1, 2, 3), (1, 0, 3, 2), (2, 3, 0, 1), (3, 2, 1, 0))


def dot(left, right):
    return jnp.dot(left, right, preferred_element_type=F32)


def dot_rt(left, right):
    return lax.dot_general(left, right, (((1,), (1,)), ((), ())), preferred_element_type=F32)


def dot_lt(left, right):
    return lax.dot_general(left, right, (((0,), (0,)), ((), ())), preferred_element_type=F32)


def norm_rows(values):
    centre = values - jnp.mean(values, axis=-1, keepdims=True)
    inverse = lax.rsqrt(jnp.mean(centre * centre, axis=-1, keepdims=True) + 1e-05)
    return (centre * inverse, inverse)


def norm_back(normed, inverse, upstream):
    return inverse * (
        upstream
        - jnp.mean(upstream, axis=-1, keepdims=True)
        - normed * jnp.mean(upstream * normed, axis=-1, keepdims=True)
    )


def across(value):
    return lax.ppermute(value, "rep", SWAP)


def sibling(value):
    return lax.ppermute(value, "core", SWAP)


def order_of(size):
    return list(range(0, size, 2)) + list(range(size - 1, 0, -2))


def scalar_table(size):
    order = order_of(size)
    place = np.argsort(order)
    table = np.zeros((2, size, 2, 2 * size + 5), np.int32)
    for rep in range(2):
        for g in range(size):
            for core in range(2):
                at = [order[(place[g] + k) % size] for k in range(size)]
                of = [(place[o] - place[g]) % size for o in range(size)]
                members = [2 * core + rep, 2 * (1 - core) + rep, 2 * core + 1 - rep, 2 * (1 - core) + 1 - rep]
                table[rep, g, core] = at + of + [core] + members
    return table


def upper_half(rows):
    return -(-(rows // 2) // PACK) * PACK


class Ring:
    def __init__(self, size):
        self.size = size
        self.half = size // 2
        order = order_of(size)
        self.right = [(order[i], order[(i + 1) % size]) for i in range(size)]
        self.left = [(b, a) for a, b in self.right]

    def exchange(self, pair):
        return lax.ppermute(pair[0], "ring", self.right), lax.ppermute(pair[1], "ring", self.left)


class Gather:
    def __init__(self, ring, chunk):
        self.ring = ring
        self.step = 0
        self.got = {0: chunk}
        self.cut = upper_half(chunk.shape[0])
        self.state = (chunk, chunk)

    def advance(self):
        if self.step == self.ring.half:
            return
        self.step += 1
        if self.step == self.ring.half:
            self.far = self.ring.exchange((self.state[0][: self.cut], self.state[1][self.cut :]))
            self.state = ()
            return
        self.state = self.ring.exchange(self.state)
        self.got[self.ring.size - self.step], self.got[self.step] = self.state

    def finish(self):
        while self.step < self.ring.half:
            self.advance()
        return [self.got[k] for k in range(self.ring.size) if k != self.ring.half] + list(self.far)


def ring_add(cut, right_term, left_term, right_got, left_got, right_ref, left_ref):
    if cut is None:
        right_ref[...] = (right_term[...].astype(F32) + right_got[...].astype(F32)).astype(BF)
        left_ref[...] = (left_term[...].astype(F32) + left_got[...].astype(F32)).astype(BF)
    else:
        right_ref[:cut] = (right_term[:cut].astype(F32) + right_got[...].astype(F32)).astype(BF)
        right_ref[cut:] = right_term[cut:]
        left_ref[:cut] = left_term[:cut]
        left_ref[cut:] = (left_term[cut:].astype(F32) + left_got[...].astype(F32)).astype(BF)


class Scatter:
    def __init__(self, ring, parts):
        self.ring = ring
        self.step = 0
        self.parts = parts
        self.cut = upper_half(parts[0].shape[0])
        far = parts[ring.half]
        self.state = (far[: self.cut], far[self.cut :])

    def send(self):
        self.got = self.ring.exchange(self.state)

    def add(self):
        ring = self.ring
        self.step += 1
        place = ring.half - self.step
        terms = (self.parts[place], self.parts[ring.size - place])
        body = functools.partial(ring_add, self.cut if self.step == 1 else None)
        self.state = tuple(call(body, [shape(t.shape, BF) for t in terms], [], 16000000000, *terms, *self.got, smem=0))

    def run(self):
        while self.step < self.ring.half - 1:
            self.add()
            self.send()
        return self.parts[0], *self.got


def sync(*values):
    return lax.optimization_barrier(values)


def call(body, outs, scratch, flops, *args, smem=1, still=0):
    nbytes = sum(a.size * a.dtype.itemsize for a in args) + sum(o.size * o.dtype.itemsize for o in outs)
    spaces = [pltpu.SMEM] * smem + [pl.ANY] * still + [pltpu.VMEM] * (len(args) - smem - still)
    return pl.pallas_call(
        body,
        name=body.func.__name__,
        out_shape=outs,
        in_specs=[pl.BlockSpec(memory_space=space) for space in spaces],
        out_specs=[pl.BlockSpec(memory_space=pltpu.VMEM)] * len(outs),
        scratch_shapes=scratch,
        compiler_params=pltpu.CompilerParams(vmem_limit_bytes=12 * MIB),
        cost_estimate=pl.CostEstimate(flops=WEIGHT.get(body.func.__name__, flops), bytes_accessed=nbytes, transcendentals=0),
    )(*args)


def shape(dims, dtype):
    return jax.ShapeDtypeStruct(dims, dtype)


def lanes(start, size):
    return pl.ds(pl.multiple_of(start, LANES), size)


def tiles_of(extent, tile=256):
    return [(at, min(tile, extent - at)) for at in range(0, extent, tile)]


def main_part(units):
    return units // LANES * LANES


def runs(size, stride, piece):
    units = size * stride
    main = main_part(units)
    rest = units - main
    for g in range(size):
        first = g * stride
        for low, high in ((first, min(first + piece, main)), (max(first, main), first + piece)):
            if low < high:
                columns = tuple(p * main + low if low < main else 2 * main + p * rest + low - main for p in range(2))
                yield g, low - first, high - low, columns


def pack_tokens(rows, prefix_ref, tokens_ref, own_ref):
    own_ref[:rows, :] = tokens_ref[...]
    for m in range(prefix_ref.shape[1]):
        own_ref[rows + m : rows + m + 1, :] = jnp.broadcast_to(prefix_ref[:, m : m + 1].astype(F32), (1, own_ref.shape[1])).astype(BF)


def pack_first(size, width, scal, qkv_ref, out_ref, own_ref, sib_ref, sems):
    quarter = width // 4
    copies = []
    for ref, member in ((own_ref, scal[2 * size + 1]), (sib_ref, scal[2 * size + 2])):
        for j in range(4):
            source = qkv_ref.at[:, lanes(j * width + member * quarter, quarter)] if j < 3 else out_ref.at[:, lanes(member * quarter, quarter)]
            copies.append(pltpu.make_async_copy(source, ref.at[:, j * quarter : (j + 1) * quarter], sems.at[len(copies)]))
            copies[-1].start()
    for copy in copies:
        copy.wait()


def pack_in(size, units, piece, padded, scal, in_ref, down_ref, own_ref, sib_ref, rows_ref):
    rep = scal[2 * size + 1] - 2 * scal[2 * size]
    for r in range(2):

        @pl.when(rep == r)
        def _(r=r):
            rows_ref[...] = down_ref[r * piece : (r + 1) * piece, :]

    for ref, member in ((own_ref, scal[2 * size + 1]), (sib_ref, scal[2 * size + 2])):
        if padded > piece:
            ref[...] = jnp.zeros_like(ref)
        for q in range(4):

            @pl.when(member == q)
            def _(ref=ref, q=q):
                for g, offset, length, columns in runs(size, padded, piece):
                    for part in range(2):
                        start = part * units + (g * 4 + q) * piece + offset
                        ref[:, columns[part] : columns[part] + length] = in_ref[:, start : start + length]


def place_chunks(size, scal, chunk_refs, store):
    half = size // 2
    places = [k for k in range(size) if k != half]
    for k, ref in zip(places, chunk_refs, strict=False):
        store(scal[k], 0, ref[...])
    top, bottom = chunk_refs[-2:]
    store(scal[half], 0, top[...])
    store(scal[half], top.shape[0], bottom[...])


def place_rows(size, shard_rows, scal, chunk_refs, put):
    core = scal[2 * size]

    def store(chip, first, value):
        for lower in range(2):
            begin = lower * shard_rows - first
            if begin < 0 or begin >= value.shape[0]:
                continue
            row = chip * (2 * shard_rows) + (core if lower == 0 else 1 - core) * shard_rows
            put(pl.multiple_of(row, PACK), value[begin : begin + shard_rows])

    place_chunks(size, scal, chunk_refs, store)


def turned(values):
    lane = lax.broadcasted_iota(jnp.int32, values.shape, 1) % HD
    wide = values.shape[1]
    return jnp.where(lane < HALF, pltpu.roll(values, wide - HALF, 1), pltpu.roll(values, HALF, 1))


def visible(rows, length, limits):
    query = lax.broadcasted_iota(jnp.int32, (rows, rows), 0)
    key = lax.broadcasted_iota(jnp.int32, (rows, rows), 1)
    inside = (key % length).astype(F32)
    limit = jnp.zeros((rows, rows), F32)
    for s in range(rows // length):
        limit = jnp.where(key // length == s, limits[s : s + 1, :rows].astype(F32), limit)
    return (query // length == key // length) & ((key <= query) | (inside < limit))


def gather_out(size, shard_rows, quarter, scal, *refs):
    out_ref = refs[-1]

    def put(row, value):
        out_ref[pl.ds(row, shard_rows), :] = value[:, 3 * quarter :]

    place_rows(size, shard_rows, scal, refs[:-1], put)


def attention(size, shard_rows, rows, length, width, n_chunks, scal, *refs):
    blocks = refs[:4]
    chunks = refs[4 : 4 + n_chunks]
    cos_ref, sin_ref, o_ref, h1_ref, qkv_ref, p_ref, w_ref = refs[4 + n_chunks :]
    quarter = width // 4

    def put(row, value):
        w_ref[pl.ds(row, shard_rows), :] = value[:, : 3 * quarter]

    place_rows(size, shard_rows, scal, chunks, put)
    for b in range(4):
        normed, _ = norm_rows(blocks[b][:rows, :].astype(F32))
        h1_ref[b * rows : (b + 1) * rows, :] = normed.astype(BF)
    for j in range(3):
        mixed = dot(h1_ref[...], w_ref[:, j * quarter : (j + 1) * quarter])
        for b in range(4):
            piece = mixed[b * rows : (b + 1) * rows, :]
            if j < 2:
                piece = piece * cos_ref[...] + turned(piece) * sin_ref[...]
            qkv_ref[b * rows : (b + 1) * rows, j * quarter : (j + 1) * quarter] = piece.astype(BF)
    for b in range(4):
        allowed = visible(rows, length, blocks[b][rows:, :])
        block = slice(b * rows, (b + 1) * rows)
        for h in range(quarter // HD):
            query = qkv_ref[block, h * HD : (h + 1) * HD]
            keys = qkv_ref[block, quarter + h * HD : quarter + (h + 1) * HD]
            values = qkv_ref[block, 2 * quarter + h * HD : 2 * quarter + (h + 1) * HD]
            scores = jnp.where(allowed, dot_rt(query, keys) * HD ** (-0.5), -1e30)
            expo = jnp.exp(scores - jnp.max(scores, axis=-1, keepdims=True))
            probs = expo / jnp.sum(expo, axis=-1, keepdims=True)
            p_ref[b * (quarter // HD) + h] = probs
            o_ref[b, :, h * HD : (h + 1) * HD] = dot(probs.astype(BF), values).astype(BF)


def middle(size, rows, width, scal, *refs):
    blocks = refs[:4]
    o_own, o_far, w_own, w_far, near_ref = refs[4:9]
    full = 4 * rows
    outputs = (
        lambda b: o_own[b],
        lambda b: near_ref[b * rows : (b + 1) * rows],
        lambda b: o_far[b],
        lambda b: near_ref[full + b * rows : full + (b + 1) * rows],
    )
    weights = (w_own, near_ref.at[2 * full : 2 * full + width], w_far, near_ref.at[2 * full + width :])
    x2_ref, h2_ref, o_ref, rows_ref, w_full = refs[9:]
    quarter = width // 4
    members = [scal[2 * size + 1 + m] for m in range(4)]
    for m in range(4):
        w_full[:, lanes(members[m] * quarter, quarter)] = weights[m][...]
        for b in range(4):
            o_ref[b * rows : (b + 1) * rows, lanes(members[m] * quarter, quarter)] = outputs[m](BLOCKS[m][b])
    rows_ref[...] = w_full[pl.ds(pl.multiple_of(members[0] * quarter, quarter), quarter), :]
    for j in range(4):
        columns = slice(j * quarter, (j + 1) * quarter)
        added = dot(o_ref[...], w_full[:, columns])
        for b in range(4):
            x2_ref[b * rows : (b + 1) * rows, columns] = blocks[b][:rows, columns].astype(F32) + added[b * rows : (b + 1) * rows, :]
    for b in range(4):
        block = slice(b * rows, (b + 1) * rows)
        normed, _ = norm_rows(x2_ref[block, :])
        h2_ref[block, :] = normed.astype(BF)


def hidden_units(size, shard_rows, members_units, n_chunks, scal, h2_ref, *refs):
    chunks = refs[:n_chunks]
    up_ref, gate_ref, hid_ref, w_ref = refs[n_chunks:]

    def put(row, value):
        w_ref[pl.ds(row, shard_rows), :] = value

    place_rows(size, shard_rows, scal, chunks, put)
    main = main_part(members_units)
    rest = members_units - main

    def put_units(columns, up, gate):
        up_ref[:, columns] = up
        gate_ref[:, columns] = gate
        hid_ref[:, columns] = (gate * jax.nn.sigmoid(gate) * up).astype(BF)

    for at, tile in tiles_of(main):
        up = dot(h2_ref[...], w_ref[:, at : at + tile])
        put_units(slice(at, at + tile), up, dot(h2_ref[...], w_ref[:, main + at : main + at + tile]))
    if rest:
        both = dot(h2_ref[...], w_ref[:, 2 * main :])
        put_units(slice(main, members_units), both[:, :rest], both[:, rest:])


def hidden_back(size, rows, padded, piece, n_chunks, scal, *refs):
    gm_ref = refs[0]
    chunks = refs[1 : 1 + n_chunks]
    up_ref, gate_ref, w_in, ggu_ref, keep_ref, give_ref, down_ref = refs[1 + n_chunks :]
    units = up_ref.shape[1]
    width = gm_ref.shape[1]
    if padded > piece:
        down_ref[...] = jnp.zeros_like(down_ref)

    def store(chip, first, value):
        down_ref[pl.ds(pl.multiple_of(chip * padded + first, ROWS), value.shape[0]), :] = value

    place_chunks(size, scal, chunks, store)

    main = main_part(units)
    rest = units - main
    pieces = [(at, size_, at, main + at) for at, size_ in tiles_of(main)]
    if rest:
        pieces.append((main, rest, 2 * main, 2 * main + rest))
    for at, count, up_at, gate_at in pieces:
        grad = dot_rt(gm_ref[...], down_ref[at : at + count, :])
        up = up_ref[:, at : at + count]
        gate = gate_ref[:, at : at + count]
        sig = jax.nn.sigmoid(gate)
        ggu_ref[:, up_at : up_at + count] = (grad * (gate * sig)).astype(BF)
        ggu_ref[:, gate_at : gate_at + count] = (grad * up * (sig * (1.0 + gate * (1.0 - sig)))).astype(BF)

    for at, count in tiles_of(width):
        back = dot_rt(ggu_ref[...], w_in[at : at + count, :])
        share(back, rows, keep_ref, give_ref, slice(at, at + count))


def share(partial, rows, keep_ref, give_ref, columns):
    keep_ref[0, :, columns] = partial[:rows]
    give_ref[0, :, columns] = partial[rows : 2 * rows].astype(BF)
    keep_ref[1, :, columns] = partial[2 * rows : 3 * rows]
    give_ref[1, :, columns] = partial[3 * rows :].astype(BF)


def last_projection(rows, scal, hid_ref, down_ref, keep_ref, give_ref):
    for at, count in tiles_of(down_ref.shape[1]):
        columns = slice(at, at + count)
        share(dot(hid_ref[...], down_ref[:, columns]), rows, keep_ref, give_ref, columns)


def write_parts(size, stride, scal, total, refs):
    for k, ref in enumerate(refs):
        ref[...] = total[pl.ds(pl.multiple_of(scal[k] * stride, ROWS), ref.shape[0]), :].astype(BF)


def grad_down_parts(size, rows, padded, scal, hid_ref, *refs):
    gm_ref, total = refs[-2:]
    for b in range(4):
        gm_ref[b * rows : (b + 1) * rows, :] = refs[b][...]
    for at, count in tiles_of(gm_ref.shape[1]):
        columns = slice(at, at + count)
        total[:, columns] = dot_lt(hid_ref[...], gm_ref[:, columns])

    write_parts(size, padded, scal, total, refs[4:-2])


def grad_in_parts(size, double, scal, h2_ref, ggu_ref, *refs):
    total = refs[-1]
    for at, tile in tiles_of(ggu_ref.shape[1]):
        total[:, at : at + tile] = dot_lt(h2_ref[...], ggu_ref[:, at : at + tile])
    write_parts(size, double, scal, total, refs[:-1])


def middle_back(rows, scal, keep_ref, got_ref, far_first, far_second, x2_ref, cot_own, cot_far, gx2_ref, ga_ref):
    for i, cot in ((0, cot_own), (1, cot_far)):
        upstream = keep_ref[i] + got_ref[i].astype(F32) + (far_second, far_first)[i][...].astype(F32)
        normed, inverse = norm_rows(x2_ref[2 * i * rows : (2 * i + 1) * rows, :])
        total = cot[...].astype(F32) + norm_back(normed, inverse, upstream)
        if i == 0:
            gx2_ref[...] = total
        ga_ref[i] = total.astype(BF)


def attention_back(rows, width, scal, ga_own, ga_near, out_rows, qkv_ref, p_ref, w_ref, cos_ref, sin_ref, gqkv_ref, ga_ref, keep_ref, give_ref, go_ref, grad_ref):
    quarter = width // 4
    for b, value in enumerate((ga_own[0], ga_near[0], ga_own[1], ga_near[1])):
        ga_ref[b * rows : (b + 1) * rows, :] = value
    go_ref[...] = dot_rt(ga_ref[...], out_rows[...]).astype(BF)
    for b in range(4):
        block = slice(b * rows, (b + 1) * rows)
        for h in range(quarter // HD):
            head = slice(h * HD, (h + 1) * HD)
            query = qkv_ref[block, h * HD : (h + 1) * HD]
            keys = qkv_ref[block, quarter + h * HD : quarter + (h + 1) * HD]
            values = qkv_ref[block, 2 * quarter + h * HD : 2 * quarter + (h + 1) * HD]
            probs = p_ref[b * (quarter // HD) + h]
            go = go_ref[block, head]
            dprob = dot_rt(go, values)
            centre = jnp.sum(probs * dprob, axis=-1, keepdims=True)
            dscore = (probs * (dprob - centre)).astype(BF)
            grad_ref[0, :, head] = dot(dscore, keys) * HD ** (-0.5)
            grad_ref[1, :, head] = dot_lt(dscore, query) * HD ** (-0.5)
            grad_ref[2, :, head] = dot_lt(probs.astype(BF), go)
        for j in range(3):
            grad = grad_ref[j]
            if j < 2:
                grad = grad * cos_ref[...] - turned(grad) * sin_ref[...]
            gqkv_ref[block, j * quarter : (j + 1) * quarter] = grad.astype(BF)
    for j in range(4):
        columns = slice(j * quarter, (j + 1) * quarter)
        share(dot_rt(gqkv_ref[...], w_ref[columns, :]), rows, keep_ref, give_ref, columns)


def grad_first_parts(size, double, width, scal, h1_ref, gqkv_ref, o_ref, ga_ref, *refs):
    total = refs[-1]
    quarter = width // 4
    for j in range(3):
        columns = slice(j * quarter, (j + 1) * quarter)
        total[:, columns] = dot_lt(h1_ref[...], gqkv_ref[:, columns])
    total[:, 3 * quarter :] = dot_lt(o_ref[...], ga_ref[:, lanes(scal[2 * size + 1] * quarter, quarter)])
    write_parts(size, double, scal, total, refs[:-1])


def split_rows(size, scal, own_ref, right_ref, left_ref, keep_ref, give_ref):
    core = scal[2 * size]
    rows = keep_ref.shape[0]
    for ref, first in ((keep_ref, core), (give_ref, 1 - core)):
        here = pl.ds(pl.multiple_of(first * rows, PACK), rows)
        ref[...] = (own_ref[here, :].astype(F32) + right_ref[here, :].astype(F32) + left_ref[here, :].astype(F32)).astype(BF)


def finish_tokens(rows, scal, keep_ref, got_ref, far_ref, block_ref, gx2_ref, out_ref):
    upstream = keep_ref[0] + got_ref[0].astype(F32) + far_ref[...].astype(F32)
    normed, inverse = norm_rows(block_ref[:rows, :].astype(F32))
    out_ref[...] = gx2_ref[...] + norm_back(normed, inverse, upstream)


def unpack_down(size, piece, scal, low_ref, other_ref, out_ref):
    rep = scal[2 * size + 1] - 2 * scal[2 * size]
    for r in range(2):

        @pl.when(rep == r)
        def _(r=r):
            out_ref[r * piece : (r + 1) * piece, :] = low_ref[...].astype(F32)
            out_ref[(1 - r) * piece : (2 - r) * piece, :] = other_ref[...].astype(F32)


def unpack_first(size, width, scal, own_ref, near_ref, far_ref, diagonal_ref, qkv_ref, out_ref):
    quarter = width // 4
    for m, ref in enumerate((own_ref, near_ref, far_ref, diagonal_ref)):
        value = ref[...].astype(F32)
        at = scal[2 * size + 1 + m] * quarter
        for j in range(3):
            qkv_ref[:, lanes(j * width + at, quarter)] = value[:, j * quarter : (j + 1) * quarter]
        out_ref[:, lanes(at, quarter)] = value[:, 3 * quarter :]


def unpack_in(size, units, piece, padded, scal, own_ref, near_ref, far_ref, diagonal_ref, in_ref, held):
    for m, ref in enumerate((own_ref, near_ref, far_ref, diagonal_ref)):
        held[scal[2 * size + 1 + m]] = ref[...].astype(F32)
    for q in range(4):
        for g, offset, length, columns in runs(size, padded, piece):
            for part in range(2):
                start = part * units + (g * 4 + q) * piece + offset
                in_ref[:, start : start + length] = held[q, :, columns[part] : columns[part] + length]


def local(tokens, prefix, qkv_weight, out_weight, in_weight, down_weight, cotangent):
    micro, _, length, width = tokens.shape
    rows = micro * length
    size = lax.axis_size("ring")
    ring = Ring(size)
    rep = lax.axis_index("rep")
    core = lax.axis_index("core")
    shard_rows = qkv_weight.shape[0]
    double = 2 * shard_rows
    units = in_weight.shape[1] // 2
    quarter = width // 4
    heads = quarter // HD
    piece = units // (4 * size)
    padded = -(-piece // ROWS) * ROWS
    while 2 * size * padded % LANES:
        padded += ROWS
    member_units = size * padded
    chunks = size + 1
    table = scalar_table(size)
    scal = lax.dynamic_slice(
        jnp.asarray(table.reshape(-1, table.shape[-1])), ((rep * size + lax.axis_index("ring")) * 2 + core, 0), (1, table.shape[-1])
    )[0]

    position = np.arange(length, dtype=np.float32)[:, None]
    frequency = np.float32(10000.0) ** (-np.arange(0, HD, 2, dtype=np.float32) / np.float32(HD))
    angles = (position * frequency[None, :]).astype(np.float32)
    angles = np.concatenate([angles, angles], axis=-1)
    sign = np.where(np.arange(HD) < HALF, -1.0, 1.0).astype(np.float32)
    cosine = jnp.asarray(np.tile(np.cos(angles), (micro, heads)).astype(np.float32))
    sine = jnp.asarray(np.tile(np.sin(angles) * sign, (micro, heads)).astype(np.float32))

    full_rows = 4 * rows
    pair_low = shape((2, rows, width), BF)
    pair_full = shape((2, rows, width), F32)
    project = 2 * full_rows * width * quarter

    tokens = tokens.reshape(rows, width)
    cot_own = cotangent.reshape(rows, width)
    a_own, a_sib = call(
        functools.partial(pack_first, size, width),
        [shape((shard_rows, width), BF)] * 2,
        [pltpu.SemaphoreType.DMA((8,))],
        0,
        scal,
        qkv_weight,
        out_weight,
        still=2,
    )
    a = Gather(ring, jnp.concatenate([a_own, sibling(a_sib)], axis=0))

    a.state, in_weight, tokens = sync(a.state, in_weight, tokens)
    a.advance()
    b_own, b_sib, down_rows = call(
        functools.partial(pack_in, size, units, piece, padded),
        [shape((shard_rows, 2 * member_units), BF)] * 2 + [shape((piece, width), BF)],
        [],
        0,
        scal,
        in_weight,
        down_weight,
    )
    c = Gather(ring, down_rows)
    c.advance()
    b_got = sibling(b_sib)
    (own,) = call(functools.partial(pack_tokens, rows), [shape((rows + micro, width), BF)], [], 0, prefix.reshape(1, micro), tokens, smem=0)
    near = sibling(own)

    a.state, own, b_own, b_got, near = sync(a.state, own, b_own, b_got, near)
    a.advance()
    far = across(own)
    b = Gather(ring, jnp.concatenate([b_own, b_got], axis=0))

    (a.state,) = sync(a.state)
    a.advance()
    far, cot_own, b.state, c.state = sync(far, cot_own, b.state, c.state)
    cot_far = across(cot_own)
    b.advance()

    while a.step < ring.half - 1:
        (a.state,) = sync(a.state)
        a.advance()
    a.state, far, cot_far = sync(a.state, far, cot_far)
    a_chunks = a.finish()
    diagonal = sibling(far)

    a_chunks, b.state, c.state, diagonal = sync(a_chunks, b.state, c.state, diagonal)
    blocks = [own, near, far, diagonal]
    b.advance()
    c.advance()
    (out_mine,) = call(functools.partial(gather_out, size, shard_rows, quarter), [shape((width, quarter), BF)], [], 0, scal, *a_chunks)
    out_far = across(out_mine)
    o_own, h1, qkv, probs, qkv_mine = call(
        functools.partial(attention, size, shard_rows, rows, length, width, chunks),
        [
            shape((4, rows, quarter), BF),
            shape((full_rows, width), BF),
            shape((full_rows, 3 * quarter), BF),
            shape((4 * heads, rows, rows), F32),
            shape((width, 3 * quarter), BF),
        ],
        [],
        3 * project,
        scal,
        *blocks,
        *a_chunks,
        cosine,
        sine,
    )

    o_own, out_mine, b.state, c.state = sync(o_own, out_mine, b.state, c.state)
    o_far = across(o_own)
    b.advance()
    c.advance()

    o_far, out_far, b.state, c.state = sync(o_far, out_far, b.state, c.state)
    kept = [o_own.reshape(full_rows, quarter), o_far.reshape(full_rows, quarter), out_mine, out_far]
    near_all = sibling(jnp.concatenate(kept, axis=0))
    b_chunks = b.finish()
    c_chunks = c.finish()
    x2, h2, o_all, out_rows = call(
        functools.partial(middle, size, rows, width),
        [
            shape((full_rows, width), F32),
            shape((full_rows, width), BF),
            shape((full_rows, width), BF),
            shape((quarter, width), BF),
        ],
        [pltpu.VMEM((width, width), BF)],
        4 * project,
        scal,
        *blocks,
        o_own,
        o_far,
        out_mine,
        out_far,
        near_all,
    )

    h2, b_chunks, c_chunks, cot_own, cot_far = sync(h2, b_chunks, c_chunks, cot_own, cot_far)
    cot_near = sibling(cot_own)
    cot_diagonal = sibling(cot_far)
    up, gate, hid, in_mine = call(
        functools.partial(hidden_units, size, shard_rows, member_units, chunks),
        [
            shape((full_rows, member_units), F32),
            shape((full_rows, member_units), F32),
            shape((full_rows, member_units), BF),
            shape((width, 2 * member_units), BF),
        ],
        [],
        6 * project,
        scal,
        h2,
        *b_chunks,
    )
    hid, cot_near, cot_diagonal = sync(hid, cot_near, cot_diagonal)
    *down_parts, gm = call(
        functools.partial(grad_down_parts, size, rows, padded),
        [shape((piece, width), BF)] * size + [shape((full_rows, width), BF)],
        [pltpu.VMEM((member_units, width), F32)],
        3 * project,
        scal,
        hid,
        cot_own,
        cot_near,
        cot_far,
        cot_diagonal,
    )

    c = Scatter(ring, down_parts)
    c.state, gm, up, c_chunks = sync(c.state, gm, up, c_chunks)
    c.send()
    ggu, u2_keep, u2_give, down_mine = call(
        functools.partial(hidden_back, size, rows, padded, piece, chunks),
        [shape((full_rows, 2 * member_units), BF), pair_full, pair_low, shape((member_units, width), BF)],
        [],
        9 * project,
        scal,
        gm,
        *c_chunks,
        up,
        gate,
        in_mine,
    )

    u2_give, c.got = sync(u2_give, c.got)
    u2_got = sibling(u2_give)
    c.add()
    c.send()
    u2_low = (u2_keep + u2_got.astype(F32)).astype(BF)

    u2_low, ggu = sync(u2_low, ggu)
    u2_first = across(u2_low[0])
    in_parts = call(
        functools.partial(grad_in_parts, size, double),
        [shape((double, 2 * member_units), BF)] * size,
        [pltpu.VMEM((width, 2 * member_units), F32)],
        6 * project,
        scal,
        h2,
        ggu,
    )

    b = Scatter(ring, in_parts)
    b.state, c.got = sync(b.state, c.got)
    b.send()
    c.add()
    c.state, u2_first, u2_low, hid = sync(c.state, u2_first, u2_low, hid)
    c.send()
    u2_second = across(u2_low[1])
    y_keep, y_give = call(functools.partial(last_projection, rows), [pair_full, pair_low], [], 3 * project, scal, hid, down_mine)

    y_give, c.got, b.got, u2_second = sync(y_give, c.got, b.got, u2_second)
    b.add()
    b.send()
    c.add()
    c.send()
    gx2, ga = call(
        functools.partial(middle_back, rows),
        [shape((rows, width), F32), pair_low],
        [],
        0,
        scal,
        u2_keep,
        u2_got,
        u2_first,
        u2_second,
        x2,
        cot_own,
        cot_far,
    )
    ga_near = sibling(ga)
    gqkv, ga_all, u1_keep, u1_give = call(
        functools.partial(attention_back, rows, width),
        [shape((full_rows, 3 * quarter), BF), shape((full_rows, width), BF), pair_full, pair_low],
        [pltpu.VMEM((full_rows, quarter), BF), pltpu.VMEM((3, rows, quarter), F32)],
        7 * project,
        scal,
        ga,
        ga_near,
        out_rows,
        qkv,
        probs,
        qkv_mine,
        cosine,
        sine,
    )

    gqkv, u1_give, b.got = sync(gqkv, u1_give, b.got)
    b.add()
    b.send()
    u1_got = sibling(u1_give)
    first_parts = call(
        functools.partial(grad_first_parts, size, double, width),
        [shape((double, width), BF)] * size,
        [pltpu.VMEM((width, width), F32)],
        4 * project,
        scal,
        h1,
        gqkv,
        o_all,
        ga_all,
    )
    down_low = sum(v.astype(F32) for v in c.run()).astype(BF)

    a = Scatter(ring, first_parts)
    a.state, u1_got, down_low = sync(a.state, u1_got, down_low)
    a.send()
    u1_low = (u1_keep[1] + u1_got[1].astype(F32)).astype(BF)
    u1_far = across(u1_low)

    a.got, b.got, u1_far, y_give = sync(a.got, b.got, u1_far, y_give)
    a.add()
    a.send()
    b.add()
    b.send()
    down_other = across(down_low)
    y_got = sibling(y_give)

    (grad_tokens,) = call(
        functools.partial(finish_tokens, rows), [shape((rows, width), F32)], [], 0, scal, u1_keep, u1_got, u1_far, own, gx2
    )
    while a.step < ring.half - 2:
        a.got, down_other, grad_tokens = sync(a.got, down_other, grad_tokens)
        a.add()
        a.send()
    y_low = (y_keep[1] + y_got[1].astype(F32)).astype(BF)
    y_far = across(y_low)

    def halves(summed):
        columns = summed[0].shape[1]
        return call(functools.partial(split_rows, size), [shape((shard_rows, columns), BF)] * 2, [], 0, scal, *summed)

    in_keep, in_give = halves(b.run())
    in_near = sibling(in_give)
    a.got, in_keep, in_near, y_far = sync(a.got, in_keep, in_near, y_far)
    a.add()
    a.send()
    in_far = across(in_keep)
    in_diagonal = across(in_near)
    first_keep, first_give = halves(a.run())
    first_keep, first_give, in_far = sync(first_keep, first_give, in_far)
    first_far = across(first_keep)
    first_near = sibling(first_give)
    first_diagonal = across(first_near)
    y_far, down_other, in_keep, first_near = sync(y_far, down_other, in_keep, first_near)
    result = (x2[:rows] + (y_keep[0] + y_got[0].astype(F32) + y_far.astype(F32))).astype(BF)
    (grad_down,) = call(functools.partial(unpack_down, size, piece), [shape((2 * piece, width), F32)], [], 0, scal, down_low, down_other)
    (grad_in,) = call(
        functools.partial(unpack_in, size, units, piece, padded),
        [shape((shard_rows, 2 * units), F32)],
        [pltpu.VMEM((4, shard_rows, 2 * member_units), F32)],
        0,
        scal,
        in_keep,
        in_near,
        in_far,
        in_diagonal,
    )
    grad_qkv, grad_out = call(
        functools.partial(unpack_first, size, width),
        [shape((shard_rows, 3 * width), F32), shape((shard_rows, width), F32)],
        [],
        0,
        scal,
        first_keep,
        first_near,
        first_far,
        first_diagonal,
    )
    return (
        result.reshape(micro, 1, length, width),
        grad_tokens.reshape(micro, 1, length, width),
        grad_qkv,
        grad_out,
        grad_in,
        grad_down,
    )


def solution(mesh):
    inner = Mesh(mesh.devices.reshape(mesh.shape["rep"], mesh.shape["shard"] // 2, 2), ("rep", "ring", "core"))
    everyone = ("rep", "ring", "core")
    group = ("ring", "core")
    sequences = P(None, everyone, None, None)
    weights = P(group, None)
    return jax.shard_map(
        local,
        mesh=inner,
        in_specs=(sequences, P(None, everyone), weights, weights, weights, weights, sequences),
        out_specs=(sequences, sequences, weights, weights, weights, weights),
        check_vma=False,
    )
```
